256 devices in a mesh: dp: 32 (over y, z), vocab: 8 (over x, core).
Axes of the slice: x: 4, y: 4, z: 8, core: 2. Of those that a mesh axis runs over, the one named last changes fastest.
Arguments:
- hidden: bfloat16 [24576, 2048], P('dp', 'vocab')
- gain: bfloat16 [2048], replicated, may hold values from 0.5 to 1.5
- head: bfloat16 [2048, 32000], P('dp', 'vocab')
- target_ids: int32 [24576], P('dp'), may hold values from 0 to 31999
- seq_lens: int32 [64], replicated, may hold values from 64 to 704, as said below
- seq_owner: int32 [64], replicated, may hold values from 0 to 31, as said below
Outputs:
- logprob: float32 [24576], P('dp')
- entropy: float32 [24576], P('dp')
The draws below stay inside these ranges and needn't reach their ends.
Inputs may be any that keep to these rules, and one draw needn't show every extreme that they name: `seq_lens`: the lengths of the sequences owned by one dp index sum to at most 768; in every draw the sequences of some dp index sum to exactly 768. `seq_owner`: every dp index owns exactly 2 sequences.
All inputs are finite; a program needn't handle non-finite values.
Results may differ from the reference program's by a relative error of at most 0.0075.
Values may be sent and summed in bfloat16 or wider, within the bound.
A program may use at most 64 MiB of HBM per device.

```python
import math
import jax
import jax.numpy as jnp
import numpy as np
from jax import lax

D = 2048
V = 32000
CAP = 768
SEQ_DEV = 2
SEQS = 64
TOKENS = 24576
N_DP = 32


def shared_direction(key):
    return jax.random.truncated_normal(jax.random.fold_in(key, 9), -4.0, 4.0, (D,), jnp.float32) / math.sqrt(D)


def head_spread():
    spread = 3.0
    return spread


def head_values(key):
    spread = head_spread()
    noise = jax.random.truncated_normal(jax.random.fold_in(key, 3), -5.0, 5.0, (D, V), jnp.float32)
    amplitude = 300.0 / math.sqrt(D)
    return noise * (spread / math.sqrt(D)) + amplitude * shared_direction(key)[:, None]


def draw_head(key, part):
    return head_values(key).astype(jnp.bfloat16)


def draw_hidden(key, part):
    spread = head_spread()
    base = jax.random.truncated_normal(jax.random.fold_in(key, 5), -4.0, 4.0, (TOKENS, D), jnp.float32)
    row_scale = jnp.exp(jax.random.uniform(jax.random.fold_in(key, 6), (TOKENS, 1), jnp.float32) * math.log(10.0))
    col_scale = jnp.exp(jax.random.uniform(jax.random.fold_in(key, 7), (1, D), jnp.float32) * math.log(10.0))
    values = base * row_scale * col_scale
    weights = head_values(key)
    direction = shared_direction(key)
    row_index = jnp.arange(TOKENS, dtype=jnp.int32)
    first = row_index * 7919 % V
    second = (first + V // 2 + 1) % V
    paired = jnp.take(weights, first, axis=1).T + 0.98 * jnp.take(weights, second, axis=1).T
    strength = jnp.where(row_index % 3 == 0, 0.0, jnp.where(row_index % 3 == 1, 0.3, 0.6))
    lift = spread * (1.0 + 0.5 * (row_index // 61 % 3).astype(jnp.float32))
    aligned = (paired + strength[:, None] * base * (spread / math.sqrt(D)) + lift[:, None] * direction[None, :]) * row_scale
    chosen = row_index % 61 == 0
    values = jnp.where(chosen[:, None], aligned, values)
    return values.astype(jnp.bfloat16)


def sequence_plan(key):
    base = jax.random.fold_in(key, 17)
    order = jax.random.permutation(jax.random.fold_in(base, 1), SEQS).astype(jnp.int32)
    shorts = jax.random.randint(jax.random.fold_in(base, 2), (SEQS,), CAP // 6, CAP // 3 + 1, dtype=jnp.int32)
    devices = SEQS // SEQ_DEV
    flags = jax.random.randint(jax.random.fold_in(base, 3), (devices,), 0, 8, dtype=jnp.int32) == 0
    forced = jax.random.randint(jax.random.fold_in(base, 4), (), 0, devices, dtype=jnp.int32)
    device_index = jnp.arange(devices, dtype=jnp.int32)
    first = jnp.where(device_index == forced, CAP // 12, shorts[0::2])
    second = jnp.where(flags, CAP - first, shorts[1::2])
    second = jnp.where(device_index == forced, CAP - CAP // 12, second)
    by_slot = jnp.stack([first, second], axis=1).reshape(SEQS)
    lengths = by_slot[order]
    owners = order // SEQ_DEV
    return (lengths.astype(jnp.int32), owners.astype(jnp.int32))


def draw_seq_lens(key, part):
    return sequence_plan(key)[0]


def draw_seq_owner(key, part):
    return sequence_plan(key)[1]


def with_ends(drawn, own_key, least, largest):
    index_at = [jax.random.randint(jax.random.fold_in(own_key, axis), (), 0, length) for axis, length in enumerate(drawn.shape)]
    main_axis = drawn.shape.index(max(drawn.shape))
    neighbour = index_at[:main_axis] + [(index_at[main_axis] + 1) % drawn.shape[main_axis]] + index_at[main_axis + 1:]
    return drawn.at[tuple(index_at)].set(least).at[tuple(neighbour)].set(largest)


def cumulative_ranks(amount, slope):
    weights = [(1 << 20) // math.isqrt(rank ** slope) + 1 for rank in range(1, amount + 1)]
    width = 1 + sum(weights) // (1 << 30)
    return np.cumsum(np.array([max(1, weight // width) for weight in weights]))


def ranked_ids(own_key, extent, count, lean):
    table = cumulative_ranks(count, lean)
    ticket = jax.random.randint(jax.random.fold_in(own_key, 1), extent, 0, int(table[count - 1]))
    standing = jnp.searchsorted(jnp.asarray(table, jnp.int32), ticket, side="right")
    return jax.random.permutation(jax.random.fold_in(own_key, 2), count)[standing].astype(jnp.int32)


def setup_inputs(seed: int = 0) -> dict:
    key_of = jax.random.split(jax.random.key(seed), 7)
    hidden = draw_hidden(jax.random.fold_in(key_of[6], 71), 0)
    gain = jnp.clip(1.0 + 0.1 * jax.random.normal(key_of[1], (D,), jnp.float32), 0.5, 1.5).astype(jnp.bfloat16)
    head = draw_head(jax.random.fold_in(key_of[6], 71), 0)
    target_ids = with_ends(ranked_ids(key_of[3], (TOKENS,), V, 2), jax.random.fold_in(key_of[3], 3), 0, V - 1).astype(jnp.int32)
    seq_lens = draw_seq_lens(jax.random.fold_in(key_of[6], 71), 0)
    seq_owner = draw_seq_owner(jax.random.fold_in(key_of[6], 71), 0)
    return dict(hidden=hidden, gain=gain, head=head, target_ids=target_ids, seq_lens=seq_lens, seq_owner=seq_owner)


EPS = 1e-05

def reference(hidden, gain, head, target_ids, seq_lens, seq_owner):
    owners = jnp.arange(N_DP, dtype=jnp.int32)
    loads = lax.optimization_barrier(jnp.sum(jnp.where(seq_owner[:, None] == owners[None, :], seq_lens[:, None], 0), axis=0)).astype(jnp.int32)
    slot_index = jnp.arange(TOKENS, dtype=jnp.int32)
    live = slot_index % CAP < loads[(slot_index // CAP).astype(jnp.int32)]
    wide = hidden.astype(jnp.float32)
    normed = (wide * lax.rsqrt(lax.optimization_barrier(jnp.mean(wide * wide, axis=1, keepdims=True)) + EPS) * gain.astype(jnp.float32)).astype(jnp.bfloat16)
    weight_full = head.astype(jnp.float32)
    block_rows = min(128, CAP)

    def scored(block_norm, block_ids):
        logits = jnp.dot(block_norm.astype(jnp.float32), weight_full, precision=lax.Precision.HIGHEST)
        top = lax.optimization_barrier(jnp.max(logits, axis=1))
        expo = jnp.exp(logits - top[:, None])
        total = lax.optimization_barrier(jnp.sum(expo, axis=1))
        weighted = lax.optimization_barrier(jnp.sum(expo * logits, axis=1))
        lse = top + jnp.log(total)
        picked = jnp.take_along_axis(logits, block_ids[:, None], axis=1)[:, 0]
        return (picked - lse, lse - weighted / total)

    def skipped(block_norm, block_ids):
        zeros = jnp.zeros((block_rows,), jnp.float32)
        return (zeros, zeros)

    def per_block(item):
        block_norm, block_ids, block_live = item
        return lax.cond(jnp.any(block_live), scored, skipped, block_norm, block_ids)
    blocks = TOKENS // block_rows
    log_part, ent_part = lax.map(per_block, (normed.reshape(blocks, block_rows, D), target_ids.reshape(blocks, block_rows), live.reshape(blocks, block_rows)))
    logprob = jnp.where(live, log_part.reshape(TOKENS), 0.0)
    entropy = jnp.where(live, ent_part.reshape(TOKENS), 0.0)
    return (logprob, entropy)
```

```python
import jax
import jax.numpy as jnp
from jax import lax
from jax.sharding import PartitionSpec as P

EPS = 1e-05


def chunk_bounds(breadth, parts):
    step = -(-breadth // parts)
    step = -(-step // 128) * 128
    bounds = []
    start = 0
    while start < breadth:
        stop = min(start + step, breadth)
        bounds.append((start, stop))
        start = stop
    return bounds


def chunk_stats(normed, columns, local_id, start):
    logits = jnp.dot(normed, columns, preferred_element_type=jnp.float32)
    top = jnp.max(logits, axis=1)
    expo = jnp.exp(logits - top[:, None])
    total = jnp.sum(expo, axis=1)
    weighted = jnp.sum(expo * logits, axis=1)
    ids = start + lax.broadcasted_iota(jnp.int32, logits.shape, 1)
    picked = jnp.sum(jnp.where(ids == local_id[:, None], logits, 0.0), axis=1)
    return top, total, weighted, picked


def local(hidden, gain, head, target_ids, seq_lens, seq_owner):
    groups = lax.axis_size("dp")
    position = lax.axis_index("dp")
    slice_index = lax.axis_index("vocab")
    slots = hidden.shape[0]
    breadth = head.shape[1]
    owners = jnp.arange(groups, dtype=jnp.int32)
    loads = jnp.sum(jnp.where(seq_owner[:, None] == owners[None, :], seq_lens[:, None], 0), axis=0)
    own_live = jnp.arange(slots, dtype=jnp.int32) < loads[position]
    features = lax.all_gather(hidden, "vocab", axis=1, tiled=True)
    wide = features.astype(jnp.float32)
    normed = (
        wide
        * lax.rsqrt(jnp.mean(wide * wide, axis=1, keepdims=True) + EPS)
        * gain.astype(jnp.float32)
    ).astype(jnp.bfloat16)
    local_id = target_ids - slice_index * breadth
    parts = []
    for start, stop in chunk_bounds(breadth, 4):
        columns = lax.all_gather(head[:, start:stop], "dp", axis=0, tiled=True)
        parts.append(chunk_stats(normed, columns, local_id, start))
    tops = jnp.stack([p[0] for p in parts])
    top_local = jnp.max(tops, axis=0)
    scale = jnp.exp(tops - top_local[None, :])
    total_local = jnp.sum(jnp.stack([p[1] for p in parts]) * scale, axis=0)
    weighted_local = jnp.sum(jnp.stack([p[2] for p in parts]) * scale, axis=0)
    picked_local = jnp.sum(jnp.stack([p[3] for p in parts]), axis=0)
    top = lax.pmax(top_local, "vocab")
    factor = jnp.exp(top_local - top)
    total, weighted, picked = lax.psum(
        (total_local * factor, weighted_local * factor, picked_local), "vocab"
    )
    lse = top + jnp.log(total)
    logprob = picked - lse
    entropy = lse - weighted / total
    return (jnp.where(own_live, logprob, 0.0), jnp.where(own_live, entropy, 0.0))


def solution(mesh):
    return jax.shard_map(
        local,
        mesh=mesh,
        in_specs=(P("dp", "vocab"), P(), P("dp", "vocab"), P("dp"), P(), P()),
        out_specs=(P("dp"), P("dp")),
        check_vma=False,
    )
```

```python
import functools

import jax
import jax.numpy as jnp
from jax import lax
from jax.experimental import pallas as pl
from jax.experimental.pallas import tpu as pltpu
from jax.sharding import PartitionSpec as P

EPS = 1e-05
MESH = pl.DeviceIdType.MESH


def dp_grid(mesh):
    size = mesh.shape["dp"]
    try:
        zs = {tuple(mesh.devices[i, 0].coords)[2] for i in range(size)}
        nz = len(zs)
    except Exception:
        nz = size // 4
    return size // nz, nz


def head_gather_kernel(ny, nz, head_ref, out_ref, send_sem, recv_sem, local_sem):
    dp = lax.axis_index("dp")
    v = lax.axis_index("vocab")
    y = dp // nz
    z = dp % nz
    yr = (y + 1) % ny
    yl = (y + ny - 1) % ny

    def zs(k):
        return (z + k + 8 * nz) % nz

    def ys(k):
        return (y + k + 8 * ny) % ny

    def dev(yy, zz):
        return (yy * nz + zz, v)

    rows = head_ref.shape[1]
    hr = rows // 2

    barrier = pltpu.get_barrier_semaphore()
    peers = [dev(yr, z), dev(yl, z), dev(y, zs(1)), dev(y, zs(-1))]
    for peer in peers:
        pl.semaphore_signal(barrier, inc=1, device_id=peer, device_id_type=MESH)
    pl.semaphore_wait(barrier, len(peers))

    copies = {}

    def send(key, src, dst, peer):
        c = pltpu.make_async_remote_copy(
            src_ref=src,
            dst_ref=dst,
            send_sem=send_sem.at[len(copies)],
            recv_sem=recv_sem.at[len(copies)],
            device_id=peer,
            device_id_type=MESH,
        )
        copies[key] = c
        c.start()

    def arrived(key):
        copies[key].wait_recv()

    local = pltpu.make_async_copy(head_ref, out_ref.at[y, z], local_sem)
    local.start()

    send("ay_r1", head_ref.at[0], out_ref.at[y, z, 0], dev(yr, z))
    send("ay_l1", head_ref.at[0], out_ref.at[y, z, 0], dev(yl, z))
    send("bz_r1", head_ref.at[1], out_ref.at[y, z, 1], dev(y, zs(1)))
    send("bz_l1", head_ref.at[1], out_ref.at[y, z, 1], dev(y, zs(-1)))

    zhalf = nz // 2
    yhalf = ny // 2

    def fwd_single_z(step):
        src_r = zs(-(step - 1))
        src_l = zs(step - 1)
        if step < zhalf or nz % 2 == 1:
            send(f"bz_r{step}", out_ref.at[y, src_r, 1], out_ref.at[y, src_r, 1], dev(y, zs(1)))
            send(f"bz_l{step}", out_ref.at[y, src_l, 1], out_ref.at[y, src_l, 1], dev(y, zs(-1)))
        else:
            send(f"bz_r{step}", out_ref.at[y, src_r, 1, pl.ds(0, hr)],
                 out_ref.at[y, src_r, 1, pl.ds(0, hr)], dev(y, zs(1)))
            send(f"bz_l{step}", out_ref.at[y, src_l, 1, pl.ds(hr, hr)],
                 out_ref.at[y, src_l, 1, pl.ds(hr, hr)], dev(y, zs(-1)))

    def fwd_single_y(step):
        src_r = ys(-(step - 1))
        src_l = ys(step - 1)
        if step < yhalf or ny % 2 == 1:
            send(f"ay_r{step}", out_ref.at[src_r, z, 0], out_ref.at[src_r, z, 0], dev(yr, z))
            send(f"ay_l{step}", out_ref.at[src_l, z, 0], out_ref.at[src_l, z, 0], dev(yl, z))
        else:
            send(f"ay_r{step}", out_ref.at[src_r, z, 0, pl.ds(0, hr)],
                 out_ref.at[src_r, z, 0, pl.ds(0, hr)], dev(yr, z))
            send(f"ay_l{step}", out_ref.at[src_l, z, 0, pl.ds(hr, hr)],
                 out_ref.at[src_l, z, 0, pl.ds(hr, hr)], dev(yl, z))

    def fwd_group_z(step):
        src_r = zs(-(step - 1))
        src_l = zs(step - 1)
        if step < zhalf or nz % 2 == 1:
            send(f"az_r{step}", out_ref.at[:, src_r, 0], out_ref.at[:, src_r, 0], dev(y, zs(1)))
            send(f"az_l{step}", out_ref.at[:, src_l, 0], out_ref.at[:, src_l, 0], dev(y, zs(-1)))
        else:
            send(f"az_r{step}", out_ref.at[pl.ds(0, yhalf), src_r, 0],
                 out_ref.at[pl.ds(0, yhalf), src_r, 0], dev(y, zs(1)))
            send(f"az_l{step}", out_ref.at[pl.ds(yhalf, ny - yhalf), src_l, 0],
                 out_ref.at[pl.ds(yhalf, ny - yhalf), src_l, 0], dev(y, zs(-1)))

    def fwd_group_y(step):
        src_r = ys(-(step - 1))
        src_l = ys(step - 1)
        if step < yhalf or ny % 2 == 1:
            send(f"by_r{step}", out_ref.at[src_r, :, 1], out_ref.at[src_r, :, 1], dev(yr, z))
            send(f"by_l{step}", out_ref.at[src_l, :, 1], out_ref.at[src_l, :, 1], dev(yl, z))
        else:
            send(f"by_r{step}", out_ref.at[src_r, pl.ds(0, zhalf), 1],
                 out_ref.at[src_r, pl.ds(0, zhalf), 1], dev(yr, z))
            send(f"by_l{step}", out_ref.at[src_l, pl.ds(zhalf, nz - zhalf), 1],
                 out_ref.at[src_l, pl.ds(zhalf, nz - zhalf), 1], dev(yl, z))

    ysteps = ny // 2 if ny % 2 == 0 else (ny - 1) // 2
    zsteps = nz // 2 if nz % 2 == 0 else (nz - 1) // 2

    for step in range(2, max(ysteps, zsteps) + 1):
        if step <= ysteps:
            arrived(f"ay_r{step - 1}")
            arrived(f"ay_l{step - 1}")
            fwd_single_y(step)
        if step <= zsteps:
            arrived(f"bz_r{step - 1}")
            arrived(f"bz_l{step - 1}")
            fwd_single_z(step)
    local.wait()
    if ysteps >= 1:
        arrived(f"ay_r{ysteps}")
        arrived(f"ay_l{ysteps}")
    send("az_r1", out_ref.at[:, z, 0], out_ref.at[:, z, 0], dev(y, zs(1)))
    send("az_l1", out_ref.at[:, z, 0], out_ref.at[:, z, 0], dev(y, zs(-1)))
    if zsteps >= 1:
        arrived(f"bz_r{zsteps}")
        arrived(f"bz_l{zsteps}")
    send("by_r1", out_ref.at[y, :, 1], out_ref.at[y, :, 1], dev(yr, z))
    send("by_l1", out_ref.at[y, :, 1], out_ref.at[y, :, 1], dev(yl, z))
    for step in range(2, max(ysteps, zsteps) + 1):
        if step <= zsteps:
            arrived(f"az_r{step - 1}")
            arrived(f"az_l{step - 1}")
            fwd_group_z(step)
        if step <= ysteps:
            arrived(f"by_r{step - 1}")
            arrived(f"by_l{step - 1}")
            fwd_group_y(step)
    arrived(f"az_r{zsteps}")
    arrived(f"az_l{zsteps}")
    arrived(f"by_r{ysteps}")
    arrived(f"by_l{ysteps}")
    for c in copies.values():
        c.wait_send()


def gather_head(head, ny, nz):
    rows, width = head.shape
    blocks = head.reshape(2, rows // 2, width)
    streams = 4 * (ny // 2 + nz // 2)
    out = pl.pallas_call(
        functools.partial(head_gather_kernel, ny, nz),
        out_shape=jax.ShapeDtypeStruct((ny, nz, 2, rows // 2, width), head.dtype),
        in_specs=[pl.BlockSpec(memory_space=pl.ANY)],
        out_specs=pl.BlockSpec(memory_space=pl.ANY),
        scratch_shapes=[
            pltpu.SemaphoreType.DMA((streams,)),
            pltpu.SemaphoreType.DMA((streams,)),
            pltpu.SemaphoreType.DMA(()),
        ],
        compiler_params=pltpu.CompilerParams(collective_id=0, has_side_effects=True),
        cost_estimate=pl.CostEstimate(
            flops=0, transcendentals=0, bytes_accessed=2 * ny * nz * rows * width * 2
        ),
    )(blocks)
    return out.reshape(ny * nz * rows, width)


def stats_kernel(n, stats_ref, out_ref, send_sem, recv_sem):
    dp = lax.axis_index("dp")
    v = lax.axis_index("vocab")
    barrier = pltpu.get_barrier_semaphore()
    for k in range(1, n):
        pl.semaphore_signal(barrier, inc=1, device_id=(dp, (v + k) % n), device_id_type=MESH)
    pl.semaphore_wait(barrier, n - 1)
    copies = []
    for k in range(1, n):
        c = pltpu.make_async_remote_copy(
            src_ref=stats_ref,
            dst_ref=out_ref.at[v],
            send_sem=send_sem.at[k - 1],
            recv_sem=recv_sem.at[k - 1],
            device_id=(dp, (v + k) % n),
            device_id_type=MESH,
        )
        c.start()
        copies.append(c)
    out_ref[v] = stats_ref[...]
    for c in copies:
        c.wait_recv()
    for c in copies:
        c.wait_send()


def exchange_stats(stats, n):
    return pl.pallas_call(
        functools.partial(stats_kernel, n),
        out_shape=jax.ShapeDtypeStruct((n,) + stats.shape, stats.dtype),
        in_specs=[pl.BlockSpec(memory_space=pltpu.VMEM)],
        out_specs=pl.BlockSpec(memory_space=pltpu.VMEM),
        scratch_shapes=[
            pltpu.SemaphoreType.DMA((n - 1,)),
            pltpu.SemaphoreType.DMA((n - 1,)),
        ],
        compiler_params=pltpu.CompilerParams(collective_id=1, has_side_effects=True),
    )(stats)


def local(ny, nz, hidden, gain, head, target_ids, seq_lens, seq_owner):
    groups = lax.axis_size("dp")
    slices = lax.axis_size("vocab")
    position = lax.axis_index("dp")
    slice_index = lax.axis_index("vocab")
    slots = hidden.shape[0]
    breadth = head.shape[1]
    owners = jnp.arange(groups, dtype=jnp.int32)
    loads = jnp.sum(jnp.where(seq_owner[:, None] == owners[None, :], seq_lens[:, None], 0), axis=0)
    own_live = jnp.arange(slots, dtype=jnp.int32) < loads[position]
    columns = gather_head(head, ny, nz)
    features = lax.all_gather(hidden, "vocab", axis=1, tiled=True)
    wide = features.astype(jnp.float32)
    normed = (
        wide
        * lax.rsqrt(jnp.mean(wide * wide, axis=1, keepdims=True) + EPS)
        * gain.astype(jnp.float32)
    ).astype(jnp.bfloat16)
    logits = jnp.dot(normed, columns, preferred_element_type=jnp.float32)
    top_local = jnp.max(logits, axis=1)
    expo = jnp.exp(logits - top_local[:, None])
    total_local = jnp.sum(expo, axis=1)
    weighted_local = jnp.sum(expo * logits, axis=1)
    local_id = target_ids - slice_index * breadth
    ids = lax.broadcasted_iota(jnp.int32, logits.shape, 1)
    picked_local = jnp.sum(jnp.where(ids == local_id[:, None], logits, 0.0), axis=1)
    stats = jnp.stack([top_local, total_local, weighted_local, picked_local])
    every = exchange_stats(stats, slices)
    tops = every[:, 0]
    top = jnp.max(tops, axis=0)
    factor = jnp.exp(tops - top[None, :])
    total = jnp.sum(every[:, 1] * factor, axis=0)
    weighted = jnp.sum(every[:, 2] * factor, axis=0)
    picked = jnp.sum(every[:, 3], axis=0)
    lse = top + jnp.log(total)
    logprob = picked - lse
    entropy = lse - weighted / total
    return (jnp.where(own_live, logprob, 0.0), jnp.where(own_live, entropy, 0.0))


def solution(mesh):
    ny, nz = dp_grid(mesh)
    return jax.shard_map(
        functools.partial(local, ny, nz),
        mesh=mesh,
        in_specs=(P("dp", "vocab"), P(), P("dp", "vocab"), P("dp"), P(), P()),
        out_specs=(P("dp"), P("dp")),
        check_vma=False,
    )
```

```python
import functools

import jax
import jax.numpy as jnp
from jax import lax
from jax.experimental import pallas as pl
from jax.experimental.pallas import tpu as pltpu
from jax.sharding import PartitionSpec as P

EPS = 1e-05
MESH = pl.DeviceIdType.MESH


def dp_grid(mesh):
    size = mesh.shape["dp"]
    try:
        zs = {tuple(mesh.devices[i, 0].coords)[2] for i in range(size)}
        nz = len(zs)
    except Exception:
        nz = size // 4
    return size // nz, nz


def head_gather_kernel(ny, nz, split, head_ref, out_ref, send_sem, recv_sem, local_sem):
    dp = lax.axis_index("dp")
    v = lax.axis_index("vocab")
    y = dp // nz
    z = dp % nz
    rows, width = head_ref.shape
    hr = rows // 2
    cols = (pl.ds(0, split), pl.ds(split, width - split))

    def zs(k):
        return (z + k + 8 * nz) % nz

    def ys(k):
        return (y + k + 8 * ny) % ny

    def dev(yy, zz):
        return (yy * nz + zz, v)

    right_y, left_y = dev(ys(1), z), dev(ys(-1), z)
    right_z, left_z = dev(y, zs(1)), dev(y, zs(-1))

    barrier = pltpu.get_barrier_semaphore()
    peers = [right_y, left_y, right_z, left_z]
    for peer in peers:
        pl.semaphore_signal(barrier, inc=1, device_id=peer, device_id_type=MESH)
    pl.semaphore_wait(barrier, len(peers))

    copies = {}

    def send(key, view, peer, src=None):
        c = pltpu.make_async_remote_copy(
            src_ref=view if src is None else src,
            dst_ref=view,
            send_sem=send_sem.at[len(copies)],
            recv_sem=recv_sem.at[len(copies)],
            device_id=peer,
            device_id_type=MESH,
        )
        copies[key] = c
        c.start()

    def arrived(key):
        copies[key].wait_recv()

    local = pltpu.make_async_copy(head_ref, out_ref.at[y, z], local_sem)
    local.start()

    ysteps = ny // 2
    zsteps = nz // 2

    def single_y(step):
        if step == 1:
            send("ay_r1", out_ref.at[y, z, :, cols[0]], right_y, head_ref.at[:, cols[0]])
            send("ay_l1", out_ref.at[y, z, :, cols[0]], left_y, head_ref.at[:, cols[0]])
            return
        src_r, src_l = ys(-(step - 1)), ys(step - 1)
        if step < ny - step or ny % 2 == 1:
            send(f"ay_r{step}", out_ref.at[src_r, z, :, cols[0]], right_y)
            send(f"ay_l{step}", out_ref.at[src_l, z, :, cols[0]], left_y)
        else:
            send(f"ay_r{step}", out_ref.at[src_r, z, pl.ds(0, hr), cols[0]], right_y)
            send(f"ay_l{step}", out_ref.at[src_l, z, pl.ds(hr, rows - hr), cols[0]], left_y)

    def single_z(step):
        if step == 1:
            send("bz_r1", out_ref.at[y, z, :, cols[1]], right_z, head_ref.at[:, cols[1]])
            send("bz_l1", out_ref.at[y, z, :, cols[1]], left_z, head_ref.at[:, cols[1]])
            return
        src_r, src_l = zs(-(step - 1)), zs(step - 1)
        if step < nz - step or nz % 2 == 1:
            send(f"bz_r{step}", out_ref.at[y, src_r, :, cols[1]], right_z)
            send(f"bz_l{step}", out_ref.at[y, src_l, :, cols[1]], left_z)
        else:
            send(f"bz_r{step}", out_ref.at[y, src_r, pl.ds(0, hr), cols[1]], right_z)
            send(f"bz_l{step}", out_ref.at[y, src_l, pl.ds(hr, rows - hr), cols[1]], left_z)

    def group_z(step):
        src_r, src_l = zs(-(step - 1)), zs(step - 1)
        if step < nz - step or nz % 2 == 1:
            send(f"az_r{step}", out_ref.at[:, src_r, :, cols[0]], right_z)
            send(f"az_l{step}", out_ref.at[:, src_l, :, cols[0]], left_z)
        else:
            half = ny // 2
            send(f"az_r{step}", out_ref.at[pl.ds(0, half), src_r, :, cols[0]], right_z)
            send(f"az_l{step}", out_ref.at[pl.ds(half, ny - half), src_l, :, cols[0]], left_z)

    def group_y(step):
        src_r, src_l = ys(-(step - 1)), ys(step - 1)
        if step < ny - step or ny % 2 == 1:
            send(f"by_r{step}", out_ref.at[src_r, :, :, cols[1]], right_y)
            send(f"by_l{step}", out_ref.at[src_l, :, :, cols[1]], left_y)
        else:
            half = nz // 2
            send(f"by_r{step}", out_ref.at[src_r, pl.ds(0, half), :, cols[1]], right_y)
            send(f"by_l{step}", out_ref.at[src_l, pl.ds(half, nz - half), :, cols[1]], left_y)

    single_y(1)
    single_z(1)
    for step in range(2, max(ysteps, zsteps) + 1):
        if step <= ysteps:
            arrived(f"ay_r{step - 1}")
            arrived(f"ay_l{step - 1}")
            single_y(step)
        if step <= zsteps:
            arrived(f"bz_r{step - 1}")
            arrived(f"bz_l{step - 1}")
            single_z(step)
    local.wait()
    arrived(f"ay_r{ysteps}")
    arrived(f"ay_l{ysteps}")
    send("az_r1", out_ref.at[:, z, :, cols[0]], right_z)
    send("az_l1", out_ref.at[:, z, :, cols[0]], left_z)
    arrived(f"bz_r{zsteps}")
    arrived(f"bz_l{zsteps}")
    send("by_r1", out_ref.at[y, :, :, cols[1]], right_y)
    send("by_l1", out_ref.at[y, :, :, cols[1]], left_y)
    for step in range(2, max(ysteps, zsteps) + 1):
        if step <= zsteps:
            arrived(f"az_r{step - 1}")
            arrived(f"az_l{step - 1}")
            group_z(step)
        if step <= ysteps:
            arrived(f"by_r{step - 1}")
            arrived(f"by_l{step - 1}")
            group_y(step)
    arrived(f"az_r{zsteps}")
    arrived(f"az_l{zsteps}")
    arrived(f"by_r{ysteps}")
    arrived(f"by_l{ysteps}")
    for c in copies.values():
        c.wait_send()


def gather_head(head, ny, nz):
    rows, width = head.shape
    share = 0.405
    split = max(128, min(width - 128, int(round(width * share / 128)) * 128))
    streams = 4 * (ny // 2 + nz // 2)
    out = pl.pallas_call(
        functools.partial(head_gather_kernel, ny, nz, split),
        out_shape=jax.ShapeDtypeStruct((ny, nz, rows, width), head.dtype),
        in_specs=[pl.BlockSpec(memory_space=pl.ANY)],
        out_specs=pl.BlockSpec(memory_space=pl.ANY),
        scratch_shapes=[
            pltpu.SemaphoreType.DMA((streams,)),
            pltpu.SemaphoreType.DMA((streams,)),
            pltpu.SemaphoreType.DMA(()),
        ],
        compiler_params=pltpu.CompilerParams(collective_id=0, has_side_effects=True),
        cost_estimate=pl.CostEstimate(
            flops=0, transcendentals=0, bytes_accessed=2 * ny * nz * rows * width * 2
        ),
    )(head)
    return out.reshape(ny * nz * rows, width)


def stats_kernel(n, stats_ref, out_ref, send_sem, recv_sem):
    dp = lax.axis_index("dp")
    v = lax.axis_index("vocab")
    barrier = pltpu.get_barrier_semaphore()
    for k in range(1, n):
        pl.semaphore_signal(barrier, inc=1, device_id=(dp, (v + k) % n), device_id_type=MESH)
    pl.semaphore_wait(barrier, n - 1)
    copies = []
    for k in range(1, n):
        c = pltpu.make_async_remote_copy(
            src_ref=stats_ref,
            dst_ref=out_ref.at[v],
            send_sem=send_sem.at[k - 1],
            recv_sem=recv_sem.at[k - 1],
            device_id=(dp, (v + k) % n),
            device_id_type=MESH,
        )
        c.start()
        copies.append(c)
    out_ref[v] = stats_ref[...]
    for c in copies:
        c.wait_recv()
    for c in copies:
        c.wait_send()


def exchange_stats(stats, n):
    return pl.pallas_call(
        functools.partial(stats_kernel, n),
        out_shape=jax.ShapeDtypeStruct((n,) + stats.shape, stats.dtype),
        in_specs=[pl.BlockSpec(memory_space=pltpu.VMEM)],
        out_specs=pl.BlockSpec(memory_space=pltpu.VMEM),
        scratch_shapes=[
            pltpu.SemaphoreType.DMA((n - 1,)),
            pltpu.SemaphoreType.DMA((n - 1,)),
        ],
        compiler_params=pltpu.CompilerParams(collective_id=1, has_side_effects=True),
    )(stats)


def local(ny, nz, hidden, gain, head, target_ids, seq_lens, seq_owner):
    groups = lax.axis_size("dp")
    slices = lax.axis_size("vocab")
    position = lax.axis_index("dp")
    slice_index = lax.axis_index("vocab")
    slots = hidden.shape[0]
    breadth = head.shape[1]
    owners = jnp.arange(groups, dtype=jnp.int32)
    loads = jnp.sum(jnp.where(seq_owner[:, None] == owners[None, :], seq_lens[:, None], 0), axis=0)
    own_live = jnp.arange(slots, dtype=jnp.int32) < loads[position]
    columns = gather_head(head, ny, nz)
    features = lax.all_gather(hidden, "vocab", axis=1, tiled=True)
    wide = features.astype(jnp.float32)
    normed = (
        wide
        * lax.rsqrt(jnp.mean(wide * wide, axis=1, keepdims=True) + EPS)
        * gain.astype(jnp.float32)
    ).astype(jnp.bfloat16)
    logits = jnp.dot(normed, columns, preferred_element_type=jnp.float32)
    top_local = jnp.max(logits, axis=1)
    expo = jnp.exp(logits - top_local[:, None])
    total_local = jnp.sum(expo, axis=1)
    weighted_local = jnp.sum(expo * logits, axis=1)
    local_id = target_ids - slice_index * breadth
    ids = lax.broadcasted_iota(jnp.int32, logits.shape, 1)
    picked_local = jnp.sum(jnp.where(ids == local_id[:, None], logits, 0.0), axis=1)
    stats = jnp.stack([top_local, total_local, weighted_local, picked_local])
    every = exchange_stats(stats, slices)
    tops = every[:, 0]
    top = jnp.max(tops, axis=0)
    factor = jnp.exp(tops - top[None, :])
    total = jnp.sum(every[:, 1] * factor, axis=0)
    weighted = jnp.sum(every[:, 2] * factor, axis=0)
    picked = jnp.sum(every[:, 3], axis=0)
    lse = top + jnp.log(total)
    logprob = picked - lse
    entropy = lse - weighted / total
    return (jnp.where(own_live, logprob, 0.0), jnp.where(own_live, entropy, 0.0))


def solution(mesh):
    ny, nz = dp_grid(mesh)
    return jax.shard_map(
        functools.partial(local, ny, nz),
        mesh=mesh,
        in_specs=(P("dp", "vocab"), P(), P("dp", "vocab"), P("dp"), P(), P()),
        out_specs=(P("dp"), P("dp")),
        check_vma=False,
    )
```

```python
import functools

import jax
import jax.numpy as jnp
from jax import lax
from jax.experimental import pallas as pl
from jax.experimental.pallas import tpu as pltpu
from jax.sharding import PartitionSpec as P

EPS = 1e-05
MESH = pl.DeviceIdType.MESH


def dp_grid(mesh):
    size = mesh.shape["dp"]
    try:
        zs = {tuple(mesh.devices[i, 0].coords)[2] for i in range(size)}
        nz = len(zs)
    except Exception:
        nz = size // 4
    return size // nz, nz


def head_gather_kernel(ny, nz, nv, head_ref, hidden_ref, out_ref, feat_ref, send_sem, recv_sem,
                       local_sem, hsend_sem, hrecv_sem, hlocal_sem):
    dp = lax.axis_index("dp")
    v = lax.axis_index("vocab")
    y = dp // nz
    z = dp % nz
    yr = (y + 1) % ny
    yl = (y + ny - 1) % ny

    def zs(k):
        return (z + k + 8 * nz) % nz

    def ys(k):
        return (y + k + 8 * ny) % ny

    def dev(yy, zz):
        return (yy * nz + zz, v)

    rows = head_ref.shape[1]
    hr = rows // 2

    barrier = pltpu.get_barrier_semaphore()
    peers = [dev(yr, z), dev(yl, z), dev(y, zs(1)), dev(y, zs(-1))]
    peers += [(dp, (v + k) % nv) for k in range(1, nv)]
    for peer in peers:
        pl.semaphore_signal(barrier, inc=1, device_id=peer, device_id_type=MESH)
    pl.semaphore_wait(barrier, len(peers))

    copies = {}

    def send(key, src, dst, peer):
        c = pltpu.make_async_remote_copy(
            src_ref=src,
            dst_ref=dst,
            send_sem=send_sem.at[len(copies)],
            recv_sem=recv_sem.at[len(copies)],
            device_id=peer,
            device_id_type=MESH,
        )
        copies[key] = c
        c.start()

    def arrived(key):
        copies[key].wait_recv()

    local = pltpu.make_async_copy(head_ref, out_ref.at[y, z], local_sem)
    local.start()

    breadth = hidden_ref.shape[1]
    own_cols = feat_ref.at[:, pl.ds(pl.multiple_of(v * breadth, breadth), breadth)]
    hidden_copies = []
    for k in range(1, nv):
        c = pltpu.make_async_remote_copy(
            src_ref=hidden_ref,
            dst_ref=own_cols,
            send_sem=hsend_sem.at[k - 1],
            recv_sem=hrecv_sem.at[k - 1],
            device_id=(dp, (v + k) % nv),
            device_id_type=MESH,
        )
        c.start()
        hidden_copies.append(c)
    hidden_local = pltpu.make_async_copy(hidden_ref, own_cols, hlocal_sem)
    hidden_local.start()

    send("ay_r1", head_ref.at[0], out_ref.at[y, z, 0], dev(yr, z))
    send("ay_l1", head_ref.at[0], out_ref.at[y, z, 0], dev(yl, z))
    send("bz_r1", head_ref.at[1], out_ref.at[y, z, 1], dev(y, zs(1)))
    send("bz_l1", head_ref.at[1], out_ref.at[y, z, 1], dev(y, zs(-1)))

    zhalf = nz // 2
    yhalf = ny // 2

    def fwd_single_z(step):
        src_r = zs(-(step - 1))
        src_l = zs(step - 1)
        if step < zhalf or nz % 2 == 1:
            send(f"bz_r{step}", out_ref.at[y, src_r, 1], out_ref.at[y, src_r, 1], dev(y, zs(1)))
            send(f"bz_l{step}", out_ref.at[y, src_l, 1], out_ref.at[y, src_l, 1], dev(y, zs(-1)))
        else:
            send(f"bz_r{step}", out_ref.at[y, src_r, 1, pl.ds(0, hr)],
                 out_ref.at[y, src_r, 1, pl.ds(0, hr)], dev(y, zs(1)))
            send(f"bz_l{step}", out_ref.at[y, src_l, 1, pl.ds(hr, hr)],
                 out_ref.at[y, src_l, 1, pl.ds(hr, hr)], dev(y, zs(-1)))

    def fwd_single_y(step):
        src_r = ys(-(step - 1))
        src_l = ys(step - 1)
        if step < yhalf or ny % 2 == 1:
            send(f"ay_r{step}", out_ref.at[src_r, z, 0], out_ref.at[src_r, z, 0], dev(yr, z))
            send(f"ay_l{step}", out_ref.at[src_l, z, 0], out_ref.at[src_l, z, 0], dev(yl, z))
        else:
            send(f"ay_r{step}", out_ref.at[src_r, z, 0, pl.ds(0, hr)],
                 out_ref.at[src_r, z, 0, pl.ds(0, hr)], dev(yr, z))
            send(f"ay_l{step}", out_ref.at[src_l, z, 0, pl.ds(hr, hr)],
                 out_ref.at[src_l, z, 0, pl.ds(hr, hr)], dev(yl, z))

    def fwd_group_z(step):
        src_r = zs(-(step - 1))
        src_l = zs(step - 1)
        if step < zhalf or nz % 2 == 1:
            send(f"az_r{step}", out_ref.at[:, src_r, 0], out_ref.at[:, src_r, 0], dev(y, zs(1)))
            send(f"az_l{step}", out_ref.at[:, src_l, 0], out_ref.at[:, src_l, 0], dev(y, zs(-1)))
        else:
            send(f"az_r{step}", out_ref.at[pl.ds(0, yhalf), src_r, 0],
                 out_ref.at[pl.ds(0, yhalf), src_r, 0], dev(y, zs(1)))
            send(f"az_l{step}", out_ref.at[pl.ds(yhalf, ny - yhalf), src_l, 0],
                 out_ref.at[pl.ds(yhalf, ny - yhalf), src_l, 0], dev(y, zs(-1)))

    def fwd_group_y(step):
        src_r = ys(-(step - 1))
        src_l = ys(step - 1)
        if step < yhalf or ny % 2 == 1:
            send(f"by_r{step}", out_ref.at[src_r, :, 1], out_ref.at[src_r, :, 1], dev(yr, z))
            send(f"by_l{step}", out_ref.at[src_l, :, 1], out_ref.at[src_l, :, 1], dev(yl, z))
        else:
            send(f"by_r{step}", out_ref.at[src_r, pl.ds(0, zhalf), 1],
                 out_ref.at[src_r, pl.ds(0, zhalf), 1], dev(yr, z))
            send(f"by_l{step}", out_ref.at[src_l, pl.ds(zhalf, nz - zhalf), 1],
                 out_ref.at[src_l, pl.ds(zhalf, nz - zhalf), 1], dev(yl, z))

    ysteps = ny // 2 if ny % 2 == 0 else (ny - 1) // 2
    zsteps = nz // 2 if nz % 2 == 0 else (nz - 1) // 2

    for step in range(2, max(ysteps, zsteps) + 1):
        if step <= ysteps:
            arrived(f"ay_r{step - 1}")
            arrived(f"ay_l{step - 1}")
            fwd_single_y(step)
        if step <= zsteps:
            arrived(f"bz_r{step - 1}")
            arrived(f"bz_l{step - 1}")
            fwd_single_z(step)
    local.wait()
    if ysteps >= 1:
        arrived(f"ay_r{ysteps}")
        arrived(f"ay_l{ysteps}")
    send("az_r1", out_ref.at[:, z, 0], out_ref.at[:, z, 0], dev(y, zs(1)))
    send("az_l1", out_ref.at[:, z, 0], out_ref.at[:, z, 0], dev(y, zs(-1)))
    if zsteps >= 1:
        arrived(f"bz_r{zsteps}")
        arrived(f"bz_l{zsteps}")
    send("by_r1", out_ref.at[y, :, 1], out_ref.at[y, :, 1], dev(yr, z))
    send("by_l1", out_ref.at[y, :, 1], out_ref.at[y, :, 1], dev(yl, z))
    for step in range(2, max(ysteps, zsteps) + 1):
        if step <= zsteps:
            arrived(f"az_r{step - 1}")
            arrived(f"az_l{step - 1}")
            fwd_group_z(step)
        if step <= ysteps:
            arrived(f"by_r{step - 1}")
            arrived(f"by_l{step - 1}")
            fwd_group_y(step)
    arrived(f"az_r{zsteps}")
    arrived(f"az_l{zsteps}")
    arrived(f"by_r{ysteps}")
    arrived(f"by_l{ysteps}")
    hidden_local.wait()
    for c in hidden_copies:
        c.wait_recv()
    for c in list(copies.values()) + hidden_copies:
        c.wait_send()


def gather_all(head, hidden, ny, nz, nv):
    rows, width = head.shape
    slots, breadth = hidden.shape
    blocks = head.reshape(2, rows // 2, width)
    streams = 4 * (ny // 2 + nz // 2)
    out, feat = pl.pallas_call(
        functools.partial(head_gather_kernel, ny, nz, nv),
        out_shape=(
            jax.ShapeDtypeStruct((ny, nz, 2, rows // 2, width), head.dtype),
            jax.ShapeDtypeStruct((slots, nv * breadth), hidden.dtype),
        ),
        in_specs=[pl.BlockSpec(memory_space=pl.ANY)] * 2,
        out_specs=(pl.BlockSpec(memory_space=pl.ANY),) * 2,
        scratch_shapes=[
            pltpu.SemaphoreType.DMA((streams,)),
            pltpu.SemaphoreType.DMA((streams,)),
            pltpu.SemaphoreType.DMA(()),
            pltpu.SemaphoreType.DMA((nv - 1,)),
            pltpu.SemaphoreType.DMA((nv - 1,)),
            pltpu.SemaphoreType.DMA(()),
        ],
        compiler_params=pltpu.CompilerParams(collective_id=0, has_side_effects=True),
        cost_estimate=pl.CostEstimate(
            flops=0, transcendentals=0, bytes_accessed=2 * ny * nz * rows * width * 2
        ),
    )(blocks, hidden)
    return out.reshape(ny * nz * rows, width), feat


def stats_kernel(n, stats_ref, out_ref, send_sem, recv_sem):
    dp = lax.axis_index("dp")
    v = lax.axis_index("vocab")
    barrier = pltpu.get_barrier_semaphore()
    for k in range(1, n):
        pl.semaphore_signal(barrier, inc=1, device_id=(dp, (v + k) % n), device_id_type=MESH)
    pl.semaphore_wait(barrier, n - 1)
    copies = []
    for k in range(1, n):
        c = pltpu.make_async_remote_copy(
            src_ref=stats_ref,
            dst_ref=out_ref.at[v],
            send_sem=send_sem.at[k - 1],
            recv_sem=recv_sem.at[k - 1],
            device_id=(dp, (v + k) % n),
            device_id_type=MESH,
        )
        c.start()
        copies.append(c)
    out_ref[v] = stats_ref[...]
    for c in copies:
        c.wait_recv()
    for c in copies:
        c.wait_send()


def exchange_stats(stats, n):
    return pl.pallas_call(
        functools.partial(stats_kernel, n),
        out_shape=jax.ShapeDtypeStruct((n,) + stats.shape, stats.dtype),
        in_specs=[pl.BlockSpec(memory_space=pltpu.VMEM)],
        out_specs=pl.BlockSpec(memory_space=pltpu.VMEM),
        scratch_shapes=[
            pltpu.SemaphoreType.DMA((n - 1,)),
            pltpu.SemaphoreType.DMA((n - 1,)),
        ],
        compiler_params=pltpu.CompilerParams(collective_id=1, has_side_effects=True),
    )(stats)


def local(ny, nz, hidden, gain, head, target_ids, seq_lens, seq_owner):
    groups = lax.axis_size("dp")
    slices = lax.axis_size("vocab")
    position = lax.axis_index("dp")
    slice_index = lax.axis_index("vocab")
    slots = hidden.shape[0]
    breadth = head.shape[1]
    owners = jnp.arange(groups, dtype=jnp.int32)
    loads = jnp.sum(jnp.where(seq_owner[:, None] == owners[None, :], seq_lens[:, None], 0), axis=0)
    own_live = jnp.arange(slots, dtype=jnp.int32) < loads[position]
    columns, features = gather_all(head, hidden, ny, nz, slices)
    wide = features.astype(jnp.float32)
    normed = (
        wide
        * lax.rsqrt(jnp.mean(wide * wide, axis=1, keepdims=True) + EPS)
        * gain.astype(jnp.float32)
    ).astype(jnp.bfloat16)
    logits = jnp.dot(normed, columns, preferred_element_type=jnp.float32)
    top_local = jnp.max(logits, axis=1)
    expo = jnp.exp(logits - top_local[:, None])
    total_local = jnp.sum(expo, axis=1)
    weighted_local = jnp.sum(expo * logits, axis=1)
    local_id = target_ids - slice_index * breadth
    ids = lax.broadcasted_iota(jnp.int32, logits.shape, 1)
    picked_local = jnp.sum(jnp.where(ids == local_id[:, None], logits, 0.0), axis=1)
    stats = jnp.stack([top_local, total_local, weighted_local, picked_local])
    every = exchange_stats(stats, slices)
    tops = every[:, 0]
    top = jnp.max(tops, axis=0)
    factor = jnp.exp(tops - top[None, :])
    total = jnp.sum(every[:, 1] * factor, axis=0)
    weighted = jnp.sum(every[:, 2] * factor, axis=0)
    picked = jnp.sum(every[:, 3], axis=0)
    lse = top + jnp.log(total)
    logprob = picked - lse
    entropy = lse - weighted / total
    return (jnp.where(own_live, logprob, 0.0), jnp.where(own_live, entropy, 0.0))


def solution(mesh):
    ny, nz = dp_grid(mesh)
    return jax.shard_map(
        functools.partial(local, ny, nz),
        mesh=mesh,
        in_specs=(P("dp", "vocab"), P(), P("dp", "vocab"), P("dp"), P(), P()),
        out_specs=(P("dp"), P("dp")),
        check_vma=False,
    )
```

```python
import functools

import jax
import jax.numpy as jnp
from jax import lax
from jax.experimental import pallas as pl
from jax.experimental.pallas import tpu as pltpu
from jax.sharding import PartitionSpec as P

EPS = 1e-05
MESH = pl.DeviceIdType.MESH


def dp_grid(mesh):
    size = mesh.shape["dp"]
    try:
        zs = {tuple(mesh.devices[i, 0].coords)[2] for i in range(size)}
        nz = len(zs)
    except Exception:
        nz = size // 4
    return size // nz, nz


def head_gather_kernel(ny, nz, nv, head_ref, hidden_ref, out_ref, feat_ref, send_sem, recv_sem,
                       local_sem, hsend_sem, hrecv_sem, hlocal_sem):
    dp = lax.axis_index("dp")
    v = lax.axis_index("vocab")
    y = dp // nz
    z = dp % nz
    yr = (y + 1) % ny
    yl = (y + ny - 1) % ny

    def zs(k):
        return (z + k + 8 * nz) % nz

    def ys(k):
        return (y + k + 8 * ny) % ny

    def dev(yy, zz):
        return (yy * nz + zz, v)

    rows = head_ref.shape[1]
    hr = rows // 2

    barrier = pltpu.get_barrier_semaphore()
    peers = [dev(yr, z), dev(yl, z), dev(y, zs(1)), dev(y, zs(-1))]
    peers += [(dp, (v + k) % nv) for k in range(1, nv)]
    for peer in peers:
        pl.semaphore_signal(barrier, inc=1, device_id=peer, device_id_type=MESH)
    pl.semaphore_wait(barrier, len(peers))

    copies = {}

    def send(key, src, dst, peer):
        c = pltpu.make_async_remote_copy(
            src_ref=src,
            dst_ref=dst,
            send_sem=send_sem.at[len(copies)],
            recv_sem=recv_sem.at[len(copies)],
            device_id=peer,
            device_id_type=MESH,
        )
        copies[key] = c
        c.start()

    def arrived(key):
        copies[key].wait_recv()

    local = pltpu.make_async_copy(head_ref, out_ref.at[y, z], local_sem)
    local.start()

    breadth = hidden_ref.shape[1]
    own_cols = feat_ref.at[:, pl.ds(pl.multiple_of(v * breadth, breadth), breadth)]
    hidden_copies = []
    for k in range(1, nv):
        c = pltpu.make_async_remote_copy(
            src_ref=hidden_ref,
            dst_ref=own_cols,
            send_sem=hsend_sem.at[k - 1],
            recv_sem=hrecv_sem.at[k - 1],
            device_id=(dp, (v + k) % nv),
            device_id_type=MESH,
        )
        c.start()
        hidden_copies.append(c)
    hidden_local = pltpu.make_async_copy(hidden_ref, own_cols, hlocal_sem)
    hidden_local.start()

    send("ay_r1", head_ref.at[0], out_ref.at[y, z, 0], dev(yr, z))
    send("ay_l1", head_ref.at[0], out_ref.at[y, z, 0], dev(yl, z))
    send("bz_r1", head_ref.at[1], out_ref.at[y, z, 1], dev(y, zs(1)))
    send("bz_l1", head_ref.at[1], out_ref.at[y, z, 1], dev(y, zs(-1)))

    zhalf = nz // 2
    yhalf = ny // 2

    def fwd_single_z(step):
        src_r = zs(-(step - 1))
        src_l = zs(step - 1)
        if step < zhalf or nz % 2 == 1:
            send(f"bz_r{step}", out_ref.at[y, src_r, 1], out_ref.at[y, src_r, 1], dev(y, zs(1)))
            send(f"bz_l{step}", out_ref.at[y, src_l, 1], out_ref.at[y, src_l, 1], dev(y, zs(-1)))
        else:
            send(f"bz_r{step}", out_ref.at[y, src_r, 1, pl.ds(0, hr)],
                 out_ref.at[y, src_r, 1, pl.ds(0, hr)], dev(y, zs(1)))
            send(f"bz_l{step}", out_ref.at[y, src_l, 1, pl.ds(hr, hr)],
                 out_ref.at[y, src_l, 1, pl.ds(hr, hr)], dev(y, zs(-1)))

    def fwd_single_y(step):
        src_r = ys(-(step - 1))
        src_l = ys(step - 1)
        if step < yhalf or ny % 2 == 1:
            send(f"ay_r{step}", out_ref.at[src_r, z, 0], out_ref.at[src_r, z, 0], dev(yr, z))
            send(f"ay_l{step}", out_ref.at[src_l, z, 0], out_ref.at[src_l, z, 0], dev(yl, z))
        else:
            send(f"ay_r{step}", out_ref.at[src_r, z, 0, pl.ds(0, hr)],
                 out_ref.at[src_r, z, 0, pl.ds(0, hr)], dev(yr, z))
            send(f"ay_l{step}", out_ref.at[src_l, z, 0, pl.ds(hr, hr)],
                 out_ref.at[src_l, z, 0, pl.ds(hr, hr)], dev(yl, z))

    def fwd_group_z(step):
        src_r = zs(-(step - 1))
        src_l = zs(step - 1)
        if step < zhalf or nz % 2 == 1:
            send(f"az_r{step}", out_ref.at[:, src_r, 0], out_ref.at[:, src_r, 0], dev(y, zs(1)))
            send(f"az_l{step}", out_ref.at[:, src_l, 0], out_ref.at[:, src_l, 0], dev(y, zs(-1)))
        else:
            send(f"az_r{step}", out_ref.at[pl.ds(0, yhalf), src_r, 0],
                 out_ref.at[pl.ds(0, yhalf), src_r, 0], dev(y, zs(1)))
            send(f"az_l{step}", out_ref.at[pl.ds(yhalf, ny - yhalf), src_l, 0],
                 out_ref.at[pl.ds(yhalf, ny - yhalf), src_l, 0], dev(y, zs(-1)))

    def fwd_group_y(step):
        src_r = ys(-(step - 1))
        src_l = ys(step - 1)
        if step < yhalf or ny % 2 == 1:
            send(f"by_r{step}", out_ref.at[src_r, :, 1], out_ref.at[src_r, :, 1], dev(yr, z))
            send(f"by_l{step}", out_ref.at[src_l, :, 1], out_ref.at[src_l, :, 1], dev(yl, z))
        else:
            send(f"by_r{step}", out_ref.at[src_r, pl.ds(0, zhalf), 1],
                 out_ref.at[src_r, pl.ds(0, zhalf), 1], dev(yr, z))
            send(f"by_l{step}", out_ref.at[src_l, pl.ds(zhalf, nz - zhalf), 1],
                 out_ref.at[src_l, pl.ds(zhalf, nz - zhalf), 1], dev(yl, z))

    ysteps = ny // 2 if ny % 2 == 0 else (ny - 1) // 2
    zsteps = nz // 2 if nz % 2 == 0 else (nz - 1) // 2

    for step in range(2, max(ysteps, zsteps) + 1):
        if step <= ysteps:
            arrived(f"ay_r{step - 1}")
            arrived(f"ay_l{step - 1}")
            fwd_single_y(step)
        if step <= zsteps:
            arrived(f"bz_r{step - 1}")
            arrived(f"bz_l{step - 1}")
            fwd_single_z(step)
    local.wait()
    if ysteps >= 1:
        arrived(f"ay_r{ysteps}")
        arrived(f"ay_l{ysteps}")
    send("az_r1", out_ref.at[:, z, 0], out_ref.at[:, z, 0], dev(y, zs(1)))
    send("az_l1", out_ref.at[:, z, 0], out_ref.at[:, z, 0], dev(y, zs(-1)))
    if zsteps >= 1:
        arrived(f"bz_r{zsteps}")
        arrived(f"bz_l{zsteps}")
    send("by_r1", out_ref.at[y, :, 1], out_ref.at[y, :, 1], dev(yr, z))
    send("by_l1", out_ref.at[y, :, 1], out_ref.at[y, :, 1], dev(yl, z))
    for step in range(2, max(ysteps, zsteps) + 1):
        if step <= zsteps:
            arrived(f"az_r{step - 1}")
            arrived(f"az_l{step - 1}")
            fwd_group_z(step)
        if step <= ysteps:
            arrived(f"by_r{step - 1}")
            arrived(f"by_l{step - 1}")
            fwd_group_y(step)
    arrived(f"az_r{zsteps}")
    arrived(f"az_l{zsteps}")
    arrived(f"by_r{ysteps}")
    arrived(f"by_l{ysteps}")
    hidden_local.wait()
    for c in hidden_copies:
        c.wait_recv()
    for c in list(copies.values()) + hidden_copies:
        c.wait_send()


def gather_all(head, hidden, ny, nz, nv):
    rows, width = head.shape
    slots, breadth = hidden.shape
    blocks = head.reshape(2, rows // 2, width)
    streams = 4 * (ny // 2 + nz // 2)
    out, feat = pl.pallas_call(
        functools.partial(head_gather_kernel, ny, nz, nv),
        out_shape=(
            jax.ShapeDtypeStruct((ny, nz, 2, rows // 2, width), head.dtype),
            jax.ShapeDtypeStruct((slots, nv * breadth), hidden.dtype),
        ),
        in_specs=[pl.BlockSpec(memory_space=pltpu.VMEM)] * 2,
        out_specs=(pl.BlockSpec(memory_space=pl.ANY),) * 2,
        scratch_shapes=[
            pltpu.SemaphoreType.DMA((streams,)),
            pltpu.SemaphoreType.DMA((streams,)),
            pltpu.SemaphoreType.DMA(()),
            pltpu.SemaphoreType.DMA((nv - 1,)),
            pltpu.SemaphoreType.DMA((nv - 1,)),
            pltpu.SemaphoreType.DMA(()),
        ],
        compiler_params=pltpu.CompilerParams(collective_id=0, has_side_effects=True),
        cost_estimate=pl.CostEstimate(
            flops=0, transcendentals=0, bytes_accessed=2 * ny * nz * rows * width * 2
        ),
    )(blocks, hidden)
    return out.reshape(ny * nz * rows, width), feat


def stats_kernel(n, stats_ref, out_ref, send_sem, recv_sem):
    dp = lax.axis_index("dp")
    v = lax.axis_index("vocab")
    barrier = pltpu.get_barrier_semaphore()
    for k in range(1, n):
        pl.semaphore_signal(barrier, inc=1, device_id=(dp, (v + k) % n), device_id_type=MESH)
    pl.semaphore_wait(barrier, n - 1)
    copies = []
    for k in range(1, n):
        c = pltpu.make_async_remote_copy(
            src_ref=stats_ref,
            dst_ref=out_ref.at[v],
            send_sem=send_sem.at[k - 1],
            recv_sem=recv_sem.at[k - 1],
            device_id=(dp, (v + k) % n),
            device_id_type=MESH,
        )
        c.start()
        copies.append(c)
    out_ref[v] = stats_ref[...]
    for c in copies:
        c.wait_recv()
    for c in copies:
        c.wait_send()


def exchange_stats(stats, n):
    return pl.pallas_call(
        functools.partial(stats_kernel, n),
        out_shape=jax.ShapeDtypeStruct((n,) + stats.shape, stats.dtype),
        in_specs=[pl.BlockSpec(memory_space=pltpu.VMEM)],
        out_specs=pl.BlockSpec(memory_space=pltpu.VMEM),
        scratch_shapes=[
            pltpu.SemaphoreType.DMA((n - 1,)),
            pltpu.SemaphoreType.DMA((n - 1,)),
        ],
        compiler_params=pltpu.CompilerParams(collective_id=1, has_side_effects=True),
    )(stats)


def local(ny, nz, hidden, gain, head, target_ids, seq_lens, seq_owner):
    groups = lax.axis_size("dp")
    slices = lax.axis_size("vocab")
    position = lax.axis_index("dp")
    slice_index = lax.axis_index("vocab")
    slots = hidden.shape[0]
    breadth = head.shape[1]
    owners = jnp.arange(groups, dtype=jnp.int32)
    loads = jnp.sum(jnp.where(seq_owner[:, None] == owners[None, :], seq_lens[:, None], 0), axis=0)
    own_live = jnp.arange(slots, dtype=jnp.int32) < loads[position]
    columns, features = gather_all(head, hidden, ny, nz, slices)
    wide = features.astype(jnp.float32)
    normed = (
        wide
        * lax.rsqrt(jnp.mean(wide * wide, axis=1, keepdims=True) + EPS)
        * gain.astype(jnp.float32)
    ).astype(jnp.bfloat16)
    logits = jnp.dot(normed, columns, preferred_element_type=jnp.float32)
    top_local = jnp.max(logits, axis=1)
    expo = jnp.exp(logits - top_local[:, None])
    total_local = jnp.sum(expo, axis=1)
    weighted_local = jnp.sum(expo * logits, axis=1)
    local_id = target_ids - slice_index * breadth
    ids = lax.broadcasted_iota(jnp.int32, logits.shape, 1)
    picked_local = jnp.sum(jnp.where(ids == local_id[:, None], logits, 0.0), axis=1)
    stats = jnp.stack([top_local, total_local, weighted_local, picked_local])
    every = exchange_stats(stats, slices)
    tops = every[:, 0]
    top = jnp.max(tops, axis=0)
    factor = jnp.exp(tops - top[None, :])
    total = jnp.sum(every[:, 1] * factor, axis=0)
    weighted = jnp.sum(every[:, 2] * factor, axis=0)
    picked = jnp.sum(every[:, 3], axis=0)
    lse = top + jnp.log(total)
    logprob = picked - lse
    entropy = lse - weighted / total
    return (jnp.where(own_live, logprob, 0.0), jnp.where(own_live, entropy, 0.0))


def solution(mesh):
    ny, nz = dp_grid(mesh)
    return jax.shard_map(
        functools.partial(local, ny, nz),
        mesh=mesh,
        in_specs=(P("dp", "vocab"), P(), P("dp", "vocab"), P("dp"), P(), P()),
        out_specs=(P("dp"), P("dp")),
        check_vma=False,
    )
```

```python
import functools

import jax
import jax.numpy as jnp
from jax import lax
from jax.experimental import pallas as pl
from jax.experimental.pallas import tpu as pltpu
from jax.sharding import PartitionSpec as P

EPS = 1e-05
MESH = pl.DeviceIdType.MESH


def dp_grid(mesh):
    size = mesh.shape["dp"]
    try:
        zs = {tuple(mesh.devices[i, 0].coords)[2] for i in range(size)}
        nz = len(zs)
    except Exception:
        nz = size // 4
    return size // nz, nz


class Ring:
    def __init__(self, ny, nz, send_sem, recv_sem):
        self.ny, self.nz = ny, nz
        self.dp = lax.axis_index("dp")
        self.v = lax.axis_index("vocab")
        self.y = self.dp // nz
        self.z = self.dp % nz
        self.send_sem, self.recv_sem = send_sem, recv_sem
        self.copies = {}
        self.right_y, self.left_y = self.dev(self.ys(1), self.z), self.dev(self.ys(-1), self.z)
        self.right_z, self.left_z = self.dev(self.y, self.zs(1)), self.dev(self.y, self.zs(-1))

    def zs(self, k):
        return (self.z + k + 8 * self.nz) % self.nz

    def ys(self, k):
        return (self.y + k + 8 * self.ny) % self.ny

    def dev(self, yy, zz):
        return (yy * self.nz + zz, self.v)

    def send(self, key, view, peer, src=None):
        c = pltpu.make_async_remote_copy(
            src_ref=view if src is None else src,
            dst_ref=view,
            send_sem=self.send_sem.at[len(self.copies)],
            recv_sem=self.recv_sem.at[len(self.copies)],
            device_id=peer,
            device_id_type=MESH,
        )
        self.copies[key] = c
        c.start()

    def arrived(self, key):
        self.copies[key].wait_recv()

    def drain(self):
        for c in self.copies.values():
            c.wait_send()


def phase_one_kernel(ny, nz, nv, head_ref, hidden_ref, out_ref, feat_ref, send_sem, recv_sem,
                     local_sem, hsend_sem, hrecv_sem, hlocal_sem):
    ring = Ring(ny, nz, send_sem, recv_sem)
    y, z, v, dp = ring.y, ring.z, ring.v, ring.dp
    rows = head_ref.shape[1]
    hr = rows // 2

    barrier = pltpu.get_barrier_semaphore()
    peers = [ring.right_y, ring.left_y, ring.right_z, ring.left_z]
    peers += [(dp, (v + k) % nv) for k in range(1, nv)]
    for peer in peers:
        pl.semaphore_signal(barrier, inc=1, device_id=peer, device_id_type=MESH)
    pl.semaphore_wait(barrier, len(peers))

    local = pltpu.make_async_copy(head_ref, out_ref.at[y, z], local_sem)
    local.start()
    breadth = hidden_ref.shape[1]
    own_cols = feat_ref.at[:, pl.ds(pl.multiple_of(v * breadth, breadth), breadth)]
    hidden_copies = []
    for k in range(1, nv):
        c = pltpu.make_async_remote_copy(
            src_ref=hidden_ref,
            dst_ref=own_cols,
            send_sem=hsend_sem.at[k - 1],
            recv_sem=hrecv_sem.at[k - 1],
            device_id=(dp, (v + k) % nv),
            device_id_type=MESH,
        )
        c.start()
        hidden_copies.append(c)
    hidden_local = pltpu.make_async_copy(hidden_ref, own_cols, hlocal_sem)
    hidden_local.start()

    def single_y(step):
        if step == 1:
            ring.send("ay1", out_ref.at[y, z, 0], ring.right_y, head_ref.at[0])
            ring.send("ay1l", out_ref.at[y, z, 0], ring.left_y, head_ref.at[0])
            return
        src_r, src_l = ring.ys(-(step - 1)), ring.ys(step - 1)
        if step < ny - step:
            ring.send(f"ay{step}", out_ref.at[src_r, z, 0], ring.right_y)
            ring.send(f"ay{step}l", out_ref.at[src_l, z, 0], ring.left_y)
        else:
            ring.send(f"ay{step}", out_ref.at[src_r, z, 0, pl.ds(0, hr)], ring.right_y)
            ring.send(f"ay{step}l", out_ref.at[src_l, z, 0, pl.ds(hr, rows - hr)], ring.left_y)

    def single_z(step):
        if step == 1:
            ring.send("bz1", out_ref.at[y, z, 1], ring.right_z, head_ref.at[1])
            ring.send("bz1l", out_ref.at[y, z, 1], ring.left_z, head_ref.at[1])
            return
        src_r, src_l = ring.zs(-(step - 1)), ring.zs(step - 1)
        if step < nz - step:
            ring.send(f"bz{step}", out_ref.at[y, src_r, 1], ring.right_z)
            ring.send(f"bz{step}l", out_ref.at[y, src_l, 1], ring.left_z)
        else:
            ring.send(f"bz{step}", out_ref.at[y, src_r, 1, pl.ds(0, hr)], ring.right_z)
            ring.send(f"bz{step}l", out_ref.at[y, src_l, 1, pl.ds(hr, rows - hr)], ring.left_z)

    ysteps, zsteps = ny // 2, nz // 2
    single_y(1)
    single_z(1)
    for step in range(2, max(ysteps, zsteps) + 1):
        if step <= ysteps:
            ring.arrived(f"ay{step - 1}")
            ring.arrived(f"ay{step - 1}l")
            single_y(step)
        if step <= zsteps:
            ring.arrived(f"bz{step - 1}")
            ring.arrived(f"bz{step - 1}l")
            single_z(step)
    ring.arrived(f"ay{ysteps}")
    ring.arrived(f"ay{ysteps}l")
    ring.arrived(f"bz{zsteps}")
    ring.arrived(f"bz{zsteps}l")
    local.wait()
    hidden_local.wait()
    for c in hidden_copies:
        c.wait_recv()
    ring.drain()
    for c in hidden_copies:
        c.wait_send()


def phase_two_kernel(ny, nz, h_in, np0_ref, np1_ref, ids_ref, out_ref,
                     top_ref, total_ref, weighted_ref, picked_ref,
                     send_sem, recv_sem, stage_a, stage_b, stage_sem, acc):
    del h_in
    ring = Ring(ny, nz, send_sem, recv_sem)
    y, z = ring.y, ring.z
    rows, width = out_ref.shape[3], out_ref.shape[4]
    ka, kb = ny * rows, nz * rows

    barrier = pltpu.get_barrier_semaphore()
    peers = [ring.right_y, ring.left_y, ring.right_z, ring.left_z]
    for peer in peers:
        pl.semaphore_signal(barrier, inc=1, device_id=peer, device_id_type=MESH)
    pl.semaphore_wait(barrier, len(peers))

    state = {"first": True}

    def accumulate(lhs, rhs):
        part = jnp.dot(lhs, rhs, preferred_element_type=jnp.float32)
        if state["first"]:
            acc[...] = part
            state["first"] = False
        else:
            acc[...] += part

    def use_a(zz):
        c = pltpu.make_async_copy(out_ref.at[:, zz, 0], stage_a, stage_sem.at[0])
        c.start()
        c.wait()
        lhs = np0_ref[:, pl.ds(pl.multiple_of(zz * ka, ka), ka)]
        accumulate(lhs, stage_a[...].reshape(ka, width))

    def use_b(yy):
        c = pltpu.make_async_copy(out_ref.at[yy, :, 1], stage_b, stage_sem.at[1])
        c.start()
        c.wait()
        lhs = np1_ref[:, pl.ds(pl.multiple_of(yy * kb, kb), kb)]
        accumulate(lhs, stage_b[...].reshape(kb, width))

    def group_z(step):
        src_r, src_l = ring.zs(-(step - 1)), ring.zs(step - 1)
        if step < nz - step:
            ring.send(f"az{step}", out_ref.at[:, src_r, 0], ring.right_z)
            ring.send(f"az{step}l", out_ref.at[:, src_l, 0], ring.left_z)
        else:
            half = ny // 2
            ring.send(f"az{step}", out_ref.at[pl.ds(0, half), src_r, 0], ring.right_z)
            ring.send(f"az{step}l", out_ref.at[pl.ds(half, ny - half), src_l, 0], ring.left_z)

    def group_y(step):
        src_r, src_l = ring.ys(-(step - 1)), ring.ys(step - 1)
        if step < ny - step:
            ring.send(f"by{step}", out_ref.at[src_r, :, 1], ring.right_y)
            ring.send(f"by{step}l", out_ref.at[src_l, :, 1], ring.left_y)
        else:
            half = nz // 2
            ring.send(f"by{step}", out_ref.at[src_r, pl.ds(0, half), 1], ring.right_y)
            ring.send(f"by{step}l", out_ref.at[src_l, pl.ds(half, nz - half), 1], ring.left_y)

    ysteps, zsteps = ny // 2, nz // 2
    group_z(1)
    group_y(1)
    use_a(z)
    use_b(y)
    for step in range(2, max(ysteps, zsteps) + 1):
        if step <= zsteps:
            ring.arrived(f"az{step - 1}")
            ring.arrived(f"az{step - 1}l")
            group_z(step)
        if step <= ysteps:
            ring.arrived(f"by{step - 1}")
            ring.arrived(f"by{step - 1}l")
            group_y(step)
        if step <= zsteps:
            use_a(ring.zs(-(step - 1)))
            use_a(ring.zs(step - 1))
        if step <= ysteps:
            use_b(ring.ys(-(step - 1)))
            use_b(ring.ys(step - 1))
    ring.arrived(f"az{zsteps}")
    ring.arrived(f"az{zsteps}l")
    use_a(ring.zs(zsteps))
    ring.arrived(f"by{ysteps}")
    ring.arrived(f"by{ysteps}l")
    use_b(ring.ys(ysteps))

    tile = 32
    slots = acc.shape[0]

    def stats(i, carry):
        r = pl.ds(pl.multiple_of(i * tile, tile), tile)
        logits = acc[r, :]
        top = jnp.max(logits, axis=1, keepdims=True)
        expo = jnp.exp(logits - top)
        total = jnp.sum(expo, axis=1, keepdims=True)
        weighted = jnp.sum(expo * logits, axis=1, keepdims=True)
        ids = lax.broadcasted_iota(jnp.int32, logits.shape, 1)
        picked = jnp.sum(jnp.where(ids == ids_ref[r, :], logits, 0.0), axis=1, keepdims=True)
        top_ref[r, :] = top
        total_ref[r, :] = total
        weighted_ref[r, :] = weighted
        picked_ref[r, :] = picked
        return carry

    lax.fori_loop(0, slots // tile, stats, 0)
    ring.drain()


def gather_phase_one(head, hidden, ny, nz, nv):
    rows, width = head.shape
    slots, breadth = hidden.shape
    blocks = head.reshape(2, rows // 2, width)
    streams = 2 * (ny // 2 + nz // 2)
    return pl.pallas_call(
        functools.partial(phase_one_kernel, ny, nz, nv),
        out_shape=(
            jax.ShapeDtypeStruct((ny, nz, 2, rows // 2, width), head.dtype),
            jax.ShapeDtypeStruct((slots, nv * breadth), hidden.dtype),
        ),
        in_specs=[pl.BlockSpec(memory_space=pltpu.VMEM)] * 2,
        out_specs=(pl.BlockSpec(memory_space=pl.ANY),) * 2,
        scratch_shapes=[
            pltpu.SemaphoreType.DMA((streams,)),
            pltpu.SemaphoreType.DMA((streams,)),
            pltpu.SemaphoreType.DMA(()),
            pltpu.SemaphoreType.DMA((nv - 1,)),
            pltpu.SemaphoreType.DMA((nv - 1,)),
            pltpu.SemaphoreType.DMA(()),
        ],
        compiler_params=pltpu.CompilerParams(collective_id=0, has_side_effects=True),
        cost_estimate=pl.CostEstimate(
            flops=0, transcendentals=0, bytes_accessed=4 * (ny + nz) * rows * width
        ),
    )(blocks, hidden)


def gather_phase_two(h, np0, np1, ids, ny, nz):
    _, _, _, rows, width = h.shape
    slots = np0.shape[0]
    streams = 2 * (ny // 2 + nz // 2)
    col = jax.ShapeDtypeStruct((slots, 1), jnp.float32)
    vmem = pl.BlockSpec(memory_space=pltpu.VMEM)
    outs = pl.pallas_call(
        functools.partial(phase_two_kernel, ny, nz),
        out_shape=(jax.ShapeDtypeStruct(h.shape, h.dtype), col, col, col, col),
        in_specs=[pl.BlockSpec(memory_space=pl.ANY), vmem, vmem, vmem],
        out_specs=(pl.BlockSpec(memory_space=pl.ANY), vmem, vmem, vmem, vmem),
        scratch_shapes=[
            pltpu.SemaphoreType.DMA((streams,)),
            pltpu.SemaphoreType.DMA((streams,)),
            pltpu.VMEM((ny, rows, width), h.dtype),
            pltpu.VMEM((nz, rows, width), h.dtype),
            pltpu.SemaphoreType.DMA((2,)),
            pltpu.VMEM((slots, width), jnp.float32),
        ],
        input_output_aliases={0: 0},
        compiler_params=pltpu.CompilerParams(
            collective_id=2, has_side_effects=True, vmem_limit_bytes=60 * 1024 * 1024
        ),
        cost_estimate=pl.CostEstimate(
            flops=2 * slots * ny * nz * 2 * rows * width,
            transcendentals=slots * width,
            bytes_accessed=4 * ny * nz * rows * width,
        ),
    )(h, np0, np1, ids)
    return outs[1:]


def stats_kernel(n, stats_ref, out_ref, send_sem, recv_sem):
    dp = lax.axis_index("dp")
    v = lax.axis_index("vocab")
    barrier = pltpu.get_barrier_semaphore()
    for k in range(1, n):
        pl.semaphore_signal(barrier, inc=1, device_id=(dp, (v + k) % n), device_id_type=MESH)
    pl.semaphore_wait(barrier, n - 1)
    copies = []
    for k in range(1, n):
        c = pltpu.make_async_remote_copy(
            src_ref=stats_ref,
            dst_ref=out_ref.at[v],
            send_sem=send_sem.at[k - 1],
            recv_sem=recv_sem.at[k - 1],
            device_id=(dp, (v + k) % n),
            device_id_type=MESH,
        )
        c.start()
        copies.append(c)
    out_ref[v] = stats_ref[...]
    for c in copies:
        c.wait_recv()
    for c in copies:
        c.wait_send()


def exchange_stats(stats, n):
    return pl.pallas_call(
        functools.partial(stats_kernel, n),
        out_shape=jax.ShapeDtypeStruct((n,) + stats.shape, stats.dtype),
        in_specs=[pl.BlockSpec(memory_space=pltpu.VMEM)],
        out_specs=pl.BlockSpec(memory_space=pltpu.VMEM),
        scratch_shapes=[
            pltpu.SemaphoreType.DMA((n - 1,)),
            pltpu.SemaphoreType.DMA((n - 1,)),
        ],
        compiler_params=pltpu.CompilerParams(collective_id=1, has_side_effects=True),
    )(stats)


def local(ny, nz, hidden, gain, head, target_ids, seq_lens, seq_owner):
    groups = lax.axis_size("dp")
    slices = lax.axis_size("vocab")
    position = lax.axis_index("dp")
    slice_index = lax.axis_index("vocab")
    slots = hidden.shape[0]
    rows, breadth = head.shape
    owners = jnp.arange(groups, dtype=jnp.int32)
    loads = jnp.sum(jnp.where(seq_owner[:, None] == owners[None, :], seq_lens[:, None], 0), axis=0)
    own_live = jnp.arange(slots, dtype=jnp.int32) < loads[position]
    h, features = gather_phase_one(head, hidden, ny, nz, slices)
    wide = features.astype(jnp.float32)
    normed = (
        wide
        * lax.rsqrt(jnp.mean(wide * wide, axis=1, keepdims=True) + EPS)
        * gain.astype(jnp.float32)
    ).astype(jnp.bfloat16)
    split = normed.reshape(slots, ny, nz, 2, rows // 2)
    np0 = split[:, :, :, 0, :].transpose(0, 2, 1, 3).reshape(slots, nz * ny * (rows // 2))
    np1 = split[:, :, :, 1, :].reshape(slots, ny * nz * (rows // 2))
    local_id = (target_ids - slice_index * breadth).reshape(slots, 1)
    top_c, total_c, weighted_c, picked_c = gather_phase_two(h, np0, np1, local_id, ny, nz)
    stats = jnp.stack([top_c[:, 0], total_c[:, 0], weighted_c[:, 0], picked_c[:, 0]])
    every = exchange_stats(stats, slices)
    tops = every[:, 0]
    top = jnp.max(tops, axis=0)
    factor = jnp.exp(tops - top[None, :])
    total = jnp.sum(every[:, 1] * factor, axis=0)
    weighted = jnp.sum(every[:, 2] * factor, axis=0)
    picked = jnp.sum(every[:, 3], axis=0)
    lse = top + jnp.log(total)
    logprob = picked - lse
    entropy = lse - weighted / total
    return (jnp.where(own_live, logprob, 0.0), jnp.where(own_live, entropy, 0.0))


def solution(mesh):
    ny, nz = dp_grid(mesh)
    return jax.shard_map(
        functools.partial(local, ny, nz),
        mesh=mesh,
        in_specs=(P("dp", "vocab"), P(), P("dp", "vocab"), P("dp"), P(), P()),
        out_specs=(P("dp"), P("dp")),
        check_vma=False,
    )
```

```python
import functools

import jax
import jax.numpy as jnp
from jax import lax
from jax.experimental import pallas as pl
from jax.experimental.pallas import tpu as pltpu
from jax.sharding import PartitionSpec as P

EPS = 1e-05
MESH = pl.DeviceIdType.MESH


def dp_grid(mesh):
    size = mesh.shape["dp"]
    try:
        zs = {tuple(mesh.devices[i, 0].coords)[2] for i in range(size)}
        nz = len(zs)
    except Exception:
        nz = size // 4
    return size // nz, nz


def head_gather_kernel(ny, nz, nv, head_ref, hidden_ref, out_ref, feat_ref, send_sem, recv_sem,
                       local_sem, hsend_sem, hrecv_sem, hlocal_sem):
    dp = lax.axis_index("dp")
    v = lax.axis_index("vocab")
    y = dp // nz
    z = dp % nz
    yr = (y + 1) % ny
    yl = (y + ny - 1) % ny

    def zs(k):
        return (z + k + 8 * nz) % nz

    def ys(k):
        return (y + k + 8 * ny) % ny

    def dev(yy, zz):
        return (yy * nz + zz, v)

    rows = head_ref.shape[1]
    hr = rows // 2

    barrier = pltpu.get_barrier_semaphore()
    peers = [dev(yr, z), dev(yl, z), dev(y, zs(1)), dev(y, zs(-1))]
    peers += [(dp, (v + k) % nv) for k in range(1, nv)]
    for peer in peers:
        pl.semaphore_signal(barrier, inc=1, device_id=peer, device_id_type=MESH)
    pl.semaphore_wait(barrier, len(peers))

    copies = {}

    def send(key, src, dst, peer):
        c = pltpu.make_async_remote_copy(
            src_ref=src,
            dst_ref=dst,
            send_sem=send_sem.at[len(copies)],
            recv_sem=recv_sem.at[len(copies)],
            device_id=peer,
            device_id_type=MESH,
        )
        copies[key] = c
        c.start()

    def arrived(key):
        copies[key].wait_recv()

    local = pltpu.make_async_copy(head_ref, out_ref.at[y, z], local_sem)
    local.start()

    breadth = hidden_ref.shape[1]
    own_cols = feat_ref.at[:, pl.ds(pl.multiple_of(v * breadth, breadth), breadth)]
    hidden_copies = []
    for k in range(1, nv):
        c = pltpu.make_async_remote_copy(
            src_ref=hidden_ref,
            dst_ref=own_cols,
            send_sem=hsend_sem.at[k - 1],
            recv_sem=hrecv_sem.at[k - 1],
            device_id=(dp, (v + k) % nv),
            device_id_type=MESH,
        )
        c.start()
        hidden_copies.append(c)
    hidden_local = pltpu.make_async_copy(hidden_ref, own_cols, hlocal_sem)
    hidden_local.start()

    plan = []

    def ring_plan(name, n, block, right, left, first_src, needs0):
        steps = n // 2
        for step in range(1, steps + 1):
            for side, peer, sign in (("r", right, -1), ("l", left, 1)):
                key = f"{name}{side}{step}"
                view = block(sign * (step - 1))
                if 2 * step == n:
                    view = view.at[pl.ds(0, hr)] if side == "r" else view.at[pl.ds(hr, rows - hr)]
                    src = view
                elif step == 1 and first_src is not None:
                    src = first_src
                else:
                    src = view
                if step == 1 and 2 * step == n and first_src is not None:
                    src = first_src.at[pl.ds(0, hr)] if side == "r" else first_src.at[pl.ds(hr, rows - hr)]
                needs = list(needs0) if step == 1 else [f"{name}{side}{step - 1}"]
                plan.append((key, src, view, peer, needs))

    right_y, left_y = dev(yr, z), dev(yl, z)
    right_z, left_z = dev(y, zs(1)), dev(y, zs(-1))

    def arrival_keys(name, n, offset):
        steps = n // 2
        if offset == 0:
            return []
        k = abs(offset) if abs(offset) <= steps else n - abs(offset)
        if 2 * k == n:
            return [f"{name}r{k}", f"{name}l{k}"]
        return [f"{name}r{k}"] if offset < 0 else [f"{name}l{k}"]

    ring_plan("ay", ny, lambda k: out_ref.at[ys(k), z, 0], right_y, left_y, head_ref.at[0], [])
    ring_plan("bz", nz, lambda k: out_ref.at[y, zs(k), 1], right_z, left_z, head_ref.at[1], [])
    y_offsets = [0] + [s * k for k in range(1, ny // 2 + 1) for s in (-1, 1) if not (s == 1 and 2 * k == ny)]
    z_offsets = [0] + [s * k for k in range(1, nz // 2 + 1) for s in (-1, 1) if not (s == 1 and 2 * k == nz)]
    for dy in y_offsets:
        ring_plan(f"az{dy + ny}_", nz, lambda k, dy=dy: out_ref.at[ys(dy), zs(k), 0], right_z, left_z,
                  head_ref.at[0] if dy == 0 else None, arrival_keys("ay", ny, dy))
    for dz in z_offsets:
        ring_plan(f"by{dz + nz}_", ny, lambda k, dz=dz: out_ref.at[ys(k), zs(dz), 1], right_y, left_y,
                  head_ref.at[1] if dz == 0 else None, arrival_keys("bz", nz, dz))

    level = {}
    for key, _, _, _, needs in plan:
        level[key] = 1 + max([level[n] for n in needs], default=-1)
    order = sorted(range(len(plan)), key=lambda i: (level[plan[i][0]], i))
    index = {plan[i][0]: i for i in range(len(plan))}
    waited = set()
    copies = {}
    for i in order:
        key, src, dst, peer, needs = plan[i]
        for n in needs:
            if n not in waited:
                copies[n].wait_recv()
                waited.add(n)
        c = pltpu.make_async_remote_copy(
            src_ref=src,
            dst_ref=dst,
            send_sem=send_sem.at[index[key]],
            recv_sem=recv_sem.at[index[key]],
            device_id=peer,
            device_id_type=MESH,
        )
        c.start()
        copies[key] = c
    for i in order:
        key = plan[i][0]
        if key not in waited:
            copies[key].wait_recv()
            waited.add(key)
    local.wait()
    hidden_local.wait()
    for c in hidden_copies:
        c.wait_recv()
    for c in list(copies.values()) + hidden_copies:
        c.wait_send()


def gather_all(head, hidden, ny, nz, nv):
    rows, width = head.shape
    slots, breadth = hidden.shape
    blocks = head.reshape(2, rows // 2, width)
    streams = 2 * (ny // 2 + nz // 2 + ny * (nz // 2) + nz * (ny // 2))
    out, feat = pl.pallas_call(
        functools.partial(head_gather_kernel, ny, nz, nv),
        out_shape=(
            jax.ShapeDtypeStruct((ny, nz, 2, rows // 2, width), head.dtype),
            jax.ShapeDtypeStruct((slots, nv * breadth), hidden.dtype),
        ),
        in_specs=[pl.BlockSpec(memory_space=pl.ANY)] * 2,
        out_specs=(pl.BlockSpec(memory_space=pl.ANY),) * 2,
        scratch_shapes=[
            pltpu.SemaphoreType.DMA((streams,)),
            pltpu.SemaphoreType.DMA((streams,)),
            pltpu.SemaphoreType.DMA(()),
            pltpu.SemaphoreType.DMA((nv - 1,)),
            pltpu.SemaphoreType.DMA((nv - 1,)),
            pltpu.SemaphoreType.DMA(()),
        ],
        compiler_params=pltpu.CompilerParams(collective_id=0, has_side_effects=True),
        cost_estimate=pl.CostEstimate(
            flops=0, transcendentals=0, bytes_accessed=2 * ny * nz * rows * width * 2
        ),
    )(blocks, hidden)
    return out.reshape(ny * nz * rows, width), feat


def stats_kernel(n, stats_ref, out_ref, send_sem, recv_sem):
    dp = lax.axis_index("dp")
    v = lax.axis_index("vocab")
    barrier = pltpu.get_barrier_semaphore()
    for k in range(1, n):
        pl.semaphore_signal(barrier, inc=1, device_id=(dp, (v + k) % n), device_id_type=MESH)
    pl.semaphore_wait(barrier, n - 1)
    copies = []
    for k in range(1, n):
        c = pltpu.make_async_remote_copy(
            src_ref=stats_ref,
            dst_ref=out_ref.at[v],
            send_sem=send_sem.at[k - 1],
            recv_sem=recv_sem.at[k - 1],
            device_id=(dp, (v + k) % n),
            device_id_type=MESH,
        )
        c.start()
        copies.append(c)
    out_ref[v] = stats_ref[...]
    for c in copies:
        c.wait_recv()
    for c in copies:
        c.wait_send()


def exchange_stats(stats, n):
    return pl.pallas_call(
        functools.partial(stats_kernel, n),
        out_shape=jax.ShapeDtypeStruct((n,) + stats.shape, stats.dtype),
        in_specs=[pl.BlockSpec(memory_space=pltpu.VMEM)],
        out_specs=pl.BlockSpec(memory_space=pltpu.VMEM),
        scratch_shapes=[
            pltpu.SemaphoreType.DMA((n - 1,)),
            pltpu.SemaphoreType.DMA((n - 1,)),
        ],
        compiler_params=pltpu.CompilerParams(collective_id=1, has_side_effects=True),
    )(stats)


def local(ny, nz, hidden, gain, head, target_ids, seq_lens, seq_owner):
    groups = lax.axis_size("dp")
    slices = lax.axis_size("vocab")
    position = lax.axis_index("dp")
    slice_index = lax.axis_index("vocab")
    slots = hidden.shape[0]
    breadth = head.shape[1]
    owners = jnp.arange(groups, dtype=jnp.int32)
    loads = jnp.sum(jnp.where(seq_owner[:, None] == owners[None, :], seq_lens[:, None], 0), axis=0)
    own_live = jnp.arange(slots, dtype=jnp.int32) < loads[position]
    columns, features = gather_all(head, hidden, ny, nz, slices)
    wide = features.astype(jnp.float32)
    normed = (
        wide
        * lax.rsqrt(jnp.mean(wide * wide, axis=1, keepdims=True) + EPS)
        * gain.astype(jnp.float32)
    ).astype(jnp.bfloat16)
    logits = jnp.dot(normed, columns, preferred_element_type=jnp.float32)
    top_local = jnp.max(logits, axis=1)
    expo = jnp.exp(logits - top_local[:, None])
    total_local = jnp.sum(expo, axis=1)
    weighted_local = jnp.sum(expo * logits, axis=1)
    local_id = target_ids - slice_index * breadth
    ids = lax.broadcasted_iota(jnp.int32, logits.shape, 1)
    picked_local = jnp.sum(jnp.where(ids == local_id[:, None], logits, 0.0), axis=1)
    stats = jnp.stack([top_local, total_local, weighted_local, picked_local])
    every = exchange_stats(stats, slices)
    tops = every[:, 0]
    top = jnp.max(tops, axis=0)
    factor = jnp.exp(tops - top[None, :])
    total = jnp.sum(every[:, 1] * factor, axis=0)
    weighted = jnp.sum(every[:, 2] * factor, axis=0)
    picked = jnp.sum(every[:, 3], axis=0)
    lse = top + jnp.log(total)
    logprob = picked - lse
    entropy = lse - weighted / total
    return (jnp.where(own_live, logprob, 0.0), jnp.where(own_live, entropy, 0.0))


def solution(mesh):
    ny, nz = dp_grid(mesh)
    return jax.shard_map(
        functools.partial(local, ny, nz),
        mesh=mesh,
        in_specs=(P("dp", "vocab"), P(), P("dp", "vocab"), P("dp"), P(), P()),
        out_specs=(P("dp"), P("dp")),
        check_vma=False,
    )
```

```python
import functools

import jax
import jax.numpy as jnp
from jax import lax
from jax.experimental import pallas as pl
from jax.experimental.pallas import tpu as pltpu
from jax.sharding import PartitionSpec as P

EPS = 1e-05
MESH = pl.DeviceIdType.MESH


def dp_grid(mesh):
    size = mesh.shape["dp"]
    try:
        zs = {tuple(mesh.devices[i, 0].coords)[2] for i in range(size)}
        nz = len(zs)
    except Exception:
        nz = size // 4
    return size // nz, nz


def head_gather_kernel(ny, nz, nv, split, head_ref, hidden_ref, out_ref, feat_ref, send_sem, recv_sem,
                       local_sem, hsend_sem, hrecv_sem, hlocal_sem):
    dp = lax.axis_index("dp")
    v = lax.axis_index("vocab")
    y = dp // nz
    z = dp % nz
    yr = (y + 1) % ny
    yl = (y + ny - 1) % ny

    def zs(k):
        return (z + k + 8 * nz) % nz

    def ys(k):
        return (y + k + 8 * ny) % ny

    def dev(yy, zz):
        return (yy * nz + zz, v)

    rows, width = head_ref.shape
    hr = rows // 2
    cols = (pl.ds(0, split), pl.ds(split, width - split))

    barrier = pltpu.get_barrier_semaphore()
    peers = [dev(yr, z), dev(yl, z), dev(y, zs(1)), dev(y, zs(-1))]
    peers += [(dp, (v + k) % nv) for k in range(1, nv)]
    for peer in peers:
        pl.semaphore_signal(barrier, inc=1, device_id=peer, device_id_type=MESH)
    pl.semaphore_wait(barrier, len(peers))

    copies = {}

    def send(key, src, dst, peer):
        c = pltpu.make_async_remote_copy(
            src_ref=src,
            dst_ref=dst,
            send_sem=send_sem.at[len(copies)],
            recv_sem=recv_sem.at[len(copies)],
            device_id=peer,
            device_id_type=MESH,
        )
        copies[key] = c
        c.start()

    def arrived(key):
        copies[key].wait_recv()

    local = pltpu.make_async_copy(head_ref, out_ref.at[y, z], local_sem)
    local.start()

    breadth = hidden_ref.shape[1]
    own_cols = feat_ref.at[:, pl.ds(pl.multiple_of(v * breadth, breadth), breadth)]
    hidden_copies = []
    for k in range(1, nv):
        c = pltpu.make_async_remote_copy(
            src_ref=hidden_ref,
            dst_ref=own_cols,
            send_sem=hsend_sem.at[k - 1],
            recv_sem=hrecv_sem.at[k - 1],
            device_id=(dp, (v + k) % nv),
            device_id_type=MESH,
        )
        c.start()
        hidden_copies.append(c)
    hidden_local = pltpu.make_async_copy(hidden_ref, own_cols, hlocal_sem)
    hidden_local.start()

    plan = []

    def ring_plan(name, n, block, right, left, first_src, needs0):
        steps = n // 2
        for step in range(1, steps + 1):
            for side, peer, sign in (("r", right, -1), ("l", left, 1)):
                key = f"{name}{side}{step}"
                view = block(sign * (step - 1))
                if 2 * step == n:
                    view = view.at[pl.ds(0, hr)] if side == "r" else view.at[pl.ds(hr, rows - hr)]
                    src = view
                elif step == 1 and first_src is not None:
                    src = first_src
                else:
                    src = view
                if step == 1 and 2 * step == n and first_src is not None:
                    src = first_src.at[pl.ds(0, hr)] if side == "r" else first_src.at[pl.ds(hr, rows - hr)]
                needs = list(needs0) if step == 1 else [f"{name}{side}{step - 1}"]
                plan.append((key, src, view, peer, needs))

    right_y, left_y = dev(yr, z), dev(yl, z)
    right_z, left_z = dev(y, zs(1)), dev(y, zs(-1))

    def arrival_keys(name, n, offset):
        steps = n // 2
        if offset == 0:
            return []
        k = abs(offset) if abs(offset) <= steps else n - abs(offset)
        if 2 * k == n:
            return [f"{name}r{k}", f"{name}l{k}"]
        return [f"{name}r{k}"] if offset < 0 else [f"{name}l{k}"]

    ring_plan("ay", ny, lambda k: out_ref.at[ys(k), z, :, cols[0]], right_y, left_y,
              head_ref.at[:, cols[0]], [])
    ring_plan("bz", nz, lambda k: out_ref.at[y, zs(k), :, cols[1]], right_z, left_z,
              head_ref.at[:, cols[1]], [])
    y_offsets = [0] + [s * k for k in range(1, ny // 2 + 1) for s in (-1, 1) if not (s == 1 and 2 * k == ny)]
    z_offsets = [0] + [s * k for k in range(1, nz // 2 + 1) for s in (-1, 1) if not (s == 1 and 2 * k == nz)]
    for dy in y_offsets:
        ring_plan(f"az{dy + ny}_", nz, lambda k, dy=dy: out_ref.at[ys(dy), zs(k), :, cols[0]],
                  right_z, left_z, head_ref.at[:, cols[0]] if dy == 0 else None,
                  arrival_keys("ay", ny, dy))
    for dz in z_offsets:
        ring_plan(f"by{dz + nz}_", ny, lambda k, dz=dz: out_ref.at[ys(k), zs(dz), :, cols[1]],
                  right_y, left_y, head_ref.at[:, cols[1]] if dz == 0 else None,
                  arrival_keys("bz", nz, dz))

    level = {}
    for key, _, _, _, needs in plan:
        level[key] = 1 + max([level[n] for n in needs], default=-1)
    order = sorted(range(len(plan)), key=lambda i: (level[plan[i][0]], i))
    index = {plan[i][0]: i for i in range(len(plan))}
    waited = set()
    copies = {}
    for i in order:
        key, src, dst, peer, needs = plan[i]
        for n in needs:
            if n not in waited:
                copies[n].wait_recv()
                waited.add(n)
        c = pltpu.make_async_remote_copy(
            src_ref=src,
            dst_ref=dst,
            send_sem=send_sem.at[index[key]],
            recv_sem=recv_sem.at[index[key]],
            device_id=peer,
            device_id_type=MESH,
        )
        c.start()
        copies[key] = c
    for i in order:
        key = plan[i][0]
        if key not in waited:
            copies[key].wait_recv()
            waited.add(key)
    local.wait()
    hidden_local.wait()
    for c in hidden_copies:
        c.wait_recv()
    for c in list(copies.values()) + hidden_copies:
        c.wait_send()


def gather_all(head, hidden, ny, nz, nv):
    rows, width = head.shape
    slots, breadth = hidden.shape
    split = max(128, min(width - 128, int(round(width * 0.405 / 128)) * 128))
    streams = 2 * (ny // 2 + nz // 2 + ny * (nz // 2) + nz * (ny // 2))
    out, feat = pl.pallas_call(
        functools.partial(head_gather_kernel, ny, nz, nv, split),
        out_shape=(
            jax.ShapeDtypeStruct((ny, nz, rows, width), head.dtype),
            jax.ShapeDtypeStruct((slots, nv * breadth), hidden.dtype),
        ),
        in_specs=[pl.BlockSpec(memory_space=pl.ANY)] * 2,
        out_specs=(pl.BlockSpec(memory_space=pl.ANY),) * 2,
        scratch_shapes=[
            pltpu.SemaphoreType.DMA((streams,)),
            pltpu.SemaphoreType.DMA((streams,)),
            pltpu.SemaphoreType.DMA(()),
            pltpu.SemaphoreType.DMA((nv - 1,)),
            pltpu.SemaphoreType.DMA((nv - 1,)),
            pltpu.SemaphoreType.DMA(()),
        ],
        compiler_params=pltpu.CompilerParams(collective_id=0, has_side_effects=True),
        cost_estimate=pl.CostEstimate(
            flops=0, transcendentals=0, bytes_accessed=2 * ny * nz * rows * width * 2
        ),
    )(head, hidden)
    return out.reshape(ny * nz * rows, width), feat


def stats_kernel(n, stats_ref, out_ref, send_sem, recv_sem):
    dp = lax.axis_index("dp")
    v = lax.axis_index("vocab")
    barrier = pltpu.get_barrier_semaphore()
    for k in range(1, n):
        pl.semaphore_signal(barrier, inc=1, device_id=(dp, (v + k) % n), device_id_type=MESH)
    pl.semaphore_wait(barrier, n - 1)
    copies = []
    for k in range(1, n):
        c = pltpu.make_async_remote_copy(
            src_ref=stats_ref,
            dst_ref=out_ref.at[v],
            send_sem=send_sem.at[k - 1],
            recv_sem=recv_sem.at[k - 1],
            device_id=(dp, (v + k) % n),
            device_id_type=MESH,
        )
        c.start()
        copies.append(c)
    out_ref[v] = stats_ref[...]
    for c in copies:
        c.wait_recv()
    for c in copies:
        c.wait_send()


def exchange_stats(stats, n):
    return pl.pallas_call(
        functools.partial(stats_kernel, n),
        out_shape=jax.ShapeDtypeStruct((n,) + stats.shape, stats.dtype),
        in_specs=[pl.BlockSpec(memory_space=pltpu.VMEM)],
        out_specs=pl.BlockSpec(memory_space=pltpu.VMEM),
        scratch_shapes=[
            pltpu.SemaphoreType.DMA((n - 1,)),
            pltpu.SemaphoreType.DMA((n - 1,)),
        ],
        compiler_params=pltpu.CompilerParams(collective_id=1, has_side_effects=True),
    )(stats)


def local(ny, nz, hidden, gain, head, target_ids, seq_lens, seq_owner):
    groups = lax.axis_size("dp")
    slices = lax.axis_size("vocab")
    position = lax.axis_index("dp")
    slice_index = lax.axis_index("vocab")
    slots = hidden.shape[0]
    breadth = head.shape[1]
    owners = jnp.arange(groups, dtype=jnp.int32)
    loads = jnp.sum(jnp.where(seq_owner[:, None] == owners[None, :], seq_lens[:, None], 0), axis=0)
    own_live = jnp.arange(slots, dtype=jnp.int32) < loads[position]
    columns, features = gather_all(head, hidden, ny, nz, slices)
    wide = features.astype(jnp.float32)
    normed = (
        wide
        * lax.rsqrt(jnp.mean(wide * wide, axis=1, keepdims=True) + EPS)
        * gain.astype(jnp.float32)
    ).astype(jnp.bfloat16)
    logits = jnp.dot(normed, columns, preferred_element_type=jnp.float32)
    top_local = jnp.max(logits, axis=1)
    expo = jnp.exp(logits - top_local[:, None])
    total_local = jnp.sum(expo, axis=1)
    weighted_local = jnp.sum(expo * logits, axis=1)
    local_id = target_ids - slice_index * breadth
    ids = lax.broadcasted_iota(jnp.int32, logits.shape, 1)
    picked_local = jnp.sum(jnp.where(ids == local_id[:, None], logits, 0.0), axis=1)
    stats = jnp.stack([top_local, total_local, weighted_local, picked_local])
    every = exchange_stats(stats, slices)
    tops = every[:, 0]
    top = jnp.max(tops, axis=0)
    factor = jnp.exp(tops - top[None, :])
    total = jnp.sum(every[:, 1] * factor, axis=0)
    weighted = jnp.sum(every[:, 2] * factor, axis=0)
    picked = jnp.sum(every[:, 3], axis=0)
    lse = top + jnp.log(total)
    logprob = picked - lse
    entropy = lse - weighted / total
    return (jnp.where(own_live, logprob, 0.0), jnp.where(own_live, entropy, 0.0))


def solution(mesh):
    ny, nz = dp_grid(mesh)
    return jax.shard_map(
        functools.partial(local, ny, nz),
        mesh=mesh,
        in_specs=(P("dp", "vocab"), P(), P("dp", "vocab"), P("dp"), P(), P()),
        out_specs=(P("dp"), P("dp")),
        check_vma=False,
    )
```

```python
import functools

import jax
import jax.numpy as jnp
from jax import lax
from jax.experimental import pallas as pl
from jax.experimental.pallas import tpu as pltpu
from jax.sharding import PartitionSpec as P

EPS = 1e-05
MESH = pl.DeviceIdType.MESH


def dp_grid(mesh):
    size = mesh.shape["dp"]
    try:
        zs = {tuple(mesh.devices[i, 0].coords)[2] for i in range(size)}
        nz = len(zs)
    except Exception:
        nz = size // 4
    return size // nz, nz


def head_gather_kernel(ny, nz, nv, split, head_ref, hidden_ref, out_ref, feat_ref, send_sem, recv_sem,
                       local_sem, hsend_sem, hrecv_sem, hlocal_sem):
    dp = lax.axis_index("dp")
    v = lax.axis_index("vocab")
    y = dp // nz
    z = dp % nz
    yr = (y + 1) % ny
    yl = (y + ny - 1) % ny

    def zs(k):
        return (z + k + 8 * nz) % nz

    def ys(k):
        return (y + k + 8 * ny) % ny

    def dev(yy, zz):
        return (yy * nz + zz, v)

    width = head_ref.shape[1]
    parts = 2
    prow = head_ref.shape[0] // parts
    rows, hr = prow, prow // 2
    cols = (pl.ds(0, split), pl.ds(split, width - split))

    barrier = pltpu.get_barrier_semaphore()
    peers = [dev(yr, z), dev(yl, z), dev(y, zs(1)), dev(y, zs(-1))]
    peers += [(dp, (v + k) % nv) for k in range(1, nv)]
    for peer in peers:
        pl.semaphore_signal(barrier, inc=1, device_id=peer, device_id_type=MESH)
    pl.semaphore_wait(barrier, len(peers))

    copies = {}

    def send(key, src, dst, peer):
        c = pltpu.make_async_remote_copy(
            src_ref=src,
            dst_ref=dst,
            send_sem=send_sem.at[len(copies)],
            recv_sem=recv_sem.at[len(copies)],
            device_id=peer,
            device_id_type=MESH,
        )
        copies[key] = c
        c.start()

    def arrived(key):
        copies[key].wait_recv()

    local = pltpu.make_async_copy(head_ref, out_ref.at[y, z], local_sem)
    local.start()

    breadth = hidden_ref.shape[1]
    own_cols = feat_ref.at[:, pl.ds(pl.multiple_of(v * breadth, breadth), breadth)]
    hidden_copies = []
    for k in range(1, nv):
        c = pltpu.make_async_remote_copy(
            src_ref=hidden_ref,
            dst_ref=own_cols,
            send_sem=hsend_sem.at[k - 1],
            recv_sem=hrecv_sem.at[k - 1],
            device_id=(dp, (v + k) % nv),
            device_id_type=MESH,
        )
        c.start()
        hidden_copies.append(c)
    hidden_local = pltpu.make_async_copy(hidden_ref, own_cols, hlocal_sem)
    hidden_local.start()

    plan = []

    def ring_plan(name, n, block, right, left, first_src, needs0):
        steps = n // 2
        for step in range(1, steps + 1):
            for side, peer, sign in (("r", right, -1), ("l", left, 1)):
                key = f"{name}{side}{step}"
                view = block(sign * (step - 1))
                if 2 * step == n:
                    view = view.at[pl.ds(0, hr)] if side == "r" else view.at[pl.ds(hr, rows - hr)]
                    src = view
                elif step == 1 and first_src is not None:
                    src = first_src
                else:
                    src = view
                if step == 1 and 2 * step == n and first_src is not None:
                    src = first_src.at[pl.ds(0, hr)] if side == "r" else first_src.at[pl.ds(hr, rows - hr)]
                needs = list(needs0) if step == 1 else [f"{name}{side}{step - 1}"]
                plan.append((key, src, view, peer, needs))

    right_y, left_y = dev(yr, z), dev(yl, z)
    right_z, left_z = dev(y, zs(1)), dev(y, zs(-1))

    def arrival_keys(name, n, offset):
        steps = n // 2
        if offset == 0:
            return []
        k = abs(offset) if abs(offset) <= steps else n - abs(offset)
        if 2 * k == n:
            return [f"{name}r{k}", f"{name}l{k}"]
        return [f"{name}r{k}"] if offset < 0 else [f"{name}l{k}"]

    y_offsets = [0] + [s * k for k in range(1, ny // 2 + 1) for s in (-1, 1) if not (s == 1 and 2 * k == ny)]
    z_offsets = [0] + [s * k for k in range(1, nz // 2 + 1) for s in (-1, 1) if not (s == 1 and 2 * k == nz)]
    for q in range(parts):
        rq = pl.ds(q * prow, prow)
        ring_plan(f"ay{q}", ny, lambda k: out_ref.at[ys(k), z, rq, cols[0]], right_y, left_y,
                  head_ref.at[rq, cols[0]], [])
        ring_plan(f"bz{q}", nz, lambda k: out_ref.at[y, zs(k), rq, cols[1]], right_z, left_z,
                  head_ref.at[rq, cols[1]], [])
        for dy in y_offsets:
            ring_plan(f"az{q}.{dy + ny}_", nz,
                      lambda k, dy=dy: out_ref.at[ys(dy), zs(k), rq, cols[0]],
                      right_z, left_z, head_ref.at[rq, cols[0]] if dy == 0 else None,
                      arrival_keys(f"ay{q}", ny, dy))
        for dz in z_offsets:
            ring_plan(f"by{q}.{dz + nz}_", ny,
                      lambda k, dz=dz: out_ref.at[ys(k), zs(dz), rq, cols[1]],
                      right_y, left_y, head_ref.at[rq, cols[1]] if dz == 0 else None,
                      arrival_keys(f"bz{q}", nz, dz))

    level = {}
    for key, _, _, _, needs in plan:
        level[key] = 1 + max([level[n] for n in needs], default=-1)
    order = sorted(range(len(plan)), key=lambda i: (level[plan[i][0]], i))
    index = {plan[i][0]: i for i in range(len(plan))}
    waited = set()
    copies = {}
    for i in order:
        key, src, dst, peer, needs = plan[i]
        for n in needs:
            if n not in waited:
                copies[n].wait_recv()
                waited.add(n)
        c = pltpu.make_async_remote_copy(
            src_ref=src,
            dst_ref=dst,
            send_sem=send_sem.at[index[key]],
            recv_sem=recv_sem.at[index[key]],
            device_id=peer,
            device_id_type=MESH,
        )
        c.start()
        copies[key] = c
    for i in order:
        key = plan[i][0]
        if key not in waited:
            copies[key].wait_recv()
            waited.add(key)
    local.wait()
    hidden_local.wait()
    for c in hidden_copies:
        c.wait_recv()
    for c in list(copies.values()) + hidden_copies:
        c.wait_send()


def gather_all(head, hidden, ny, nz, nv):
    rows, width = head.shape
    slots, breadth = hidden.shape
    split = max(128, min(width - 128, int(round(width * 0.405 / 128)) * 128))
    streams = 4 * (ny // 2 + nz // 2 + ny * (nz // 2) + nz * (ny // 2))
    out, feat = pl.pallas_call(
        functools.partial(head_gather_kernel, ny, nz, nv, split),
        out_shape=(
            jax.ShapeDtypeStruct((ny, nz, rows, width), head.dtype),
            jax.ShapeDtypeStruct((slots, nv * breadth), hidden.dtype),
        ),
        in_specs=[pl.BlockSpec(memory_space=pl.ANY)] * 2,
        out_specs=(pl.BlockSpec(memory_space=pl.ANY),) * 2,
        scratch_shapes=[
            pltpu.SemaphoreType.DMA((streams,)),
            pltpu.SemaphoreType.DMA((streams,)),
            pltpu.SemaphoreType.DMA(()),
            pltpu.SemaphoreType.DMA((nv - 1,)),
            pltpu.SemaphoreType.DMA((nv - 1,)),
            pltpu.SemaphoreType.DMA(()),
        ],
        compiler_params=pltpu.CompilerParams(collective_id=0, has_side_effects=True),
        cost_estimate=pl.CostEstimate(
            flops=0, transcendentals=0, bytes_accessed=2 * ny * nz * rows * width * 2
        ),
    )(head, hidden)
    return out.reshape(ny * nz * rows, width), feat


def stats_kernel(n, stats_ref, out_ref, send_sem, recv_sem):
    dp = lax.axis_index("dp")
    v = lax.axis_index("vocab")
    barrier = pltpu.get_barrier_semaphore()
    for k in range(1, n):
        pl.semaphore_signal(barrier, inc=1, device_id=(dp, (v + k) % n), device_id_type=MESH)
    pl.semaphore_wait(barrier, n - 1)
    copies = []
    for k in range(1, n):
        c = pltpu.make_async_remote_copy(
            src_ref=stats_ref,
            dst_ref=out_ref.at[v],
            send_sem=send_sem.at[k - 1],
            recv_sem=recv_sem.at[k - 1],
            device_id=(dp, (v + k) % n),
            device_id_type=MESH,
        )
        c.start()
        copies.append(c)
    out_ref[v] = stats_ref[...]
    for c in copies:
        c.wait_recv()
    for c in copies:
        c.wait_send()


def exchange_stats(stats, n):
    return pl.pallas_call(
        functools.partial(stats_kernel, n),
        out_shape=jax.ShapeDtypeStruct((n,) + stats.shape, stats.dtype),
        in_specs=[pl.BlockSpec(memory_space=pltpu.VMEM)],
        out_specs=pl.BlockSpec(memory_space=pltpu.VMEM),
        scratch_shapes=[
            pltpu.SemaphoreType.DMA((n - 1,)),
            pltpu.SemaphoreType.DMA((n - 1,)),
        ],
        compiler_params=pltpu.CompilerParams(collective_id=1, has_side_effects=True),
    )(stats)


def local(ny, nz, hidden, gain, head, target_ids, seq_lens, seq_owner):
    groups = lax.axis_size("dp")
    slices = lax.axis_size("vocab")
    position = lax.axis_index("dp")
    slice_index = lax.axis_index("vocab")
    slots = hidden.shape[0]
    breadth = head.shape[1]
    owners = jnp.arange(groups, dtype=jnp.int32)
    loads = jnp.sum(jnp.where(seq_owner[:, None] == owners[None, :], seq_lens[:, None], 0), axis=0)
    own_live = jnp.arange(slots, dtype=jnp.int32) < loads[position]
    columns, features = gather_all(head, hidden, ny, nz, slices)
    wide = features.astype(jnp.float32)
    normed = (
        wide
        * lax.rsqrt(jnp.mean(wide * wide, axis=1, keepdims=True) + EPS)
        * gain.astype(jnp.float32)
    ).astype(jnp.bfloat16)
    logits = jnp.dot(normed, columns, preferred_element_type=jnp.float32)
    top_local = jnp.max(logits, axis=1)
    expo = jnp.exp(logits - top_local[:, None])
    total_local = jnp.sum(expo, axis=1)
    weighted_local = jnp.sum(expo * logits, axis=1)
    local_id = target_ids - slice_index * breadth
    ids = lax.broadcasted_iota(jnp.int32, logits.shape, 1)
    picked_local = jnp.sum(jnp.where(ids == local_id[:, None], logits, 0.0), axis=1)
    stats = jnp.stack([top_local, total_local, weighted_local, picked_local])
    every = exchange_stats(stats, slices)
    tops = every[:, 0]
    top = jnp.max(tops, axis=0)
    factor = jnp.exp(tops - top[None, :])
    total = jnp.sum(every[:, 1] * factor, axis=0)
    weighted = jnp.sum(every[:, 2] * factor, axis=0)
    picked = jnp.sum(every[:, 3], axis=0)
    lse = top + jnp.log(total)
    logprob = picked - lse
    entropy = lse - weighted / total
    return (jnp.where(own_live, logprob, 0.0), jnp.where(own_live, entropy, 0.0))


def solution(mesh):
    ny, nz = dp_grid(mesh)
    return jax.shard_map(
        functools.partial(local, ny, nz),
        mesh=mesh,
        in_specs=(P("dp", "vocab"), P(), P("dp", "vocab"), P("dp"), P(), P()),
        out_specs=(P("dp"), P("dp")),
        check_vma=False,
    )
```

```python
import functools

import jax
import jax.numpy as jnp
from jax import lax
from jax.experimental import pallas as pl
from jax.experimental.pallas import tpu as pltpu
from jax.sharding import PartitionSpec as P

EPS = 1e-05
MESH = pl.DeviceIdType.MESH


def dp_grid(mesh):
    size = mesh.shape["dp"]
    try:
        zs = {tuple(mesh.devices[i, 0].coords)[2] for i in range(size)}
        nz = len(zs)
    except Exception:
        nz = size // 4
    return size // nz, nz


def head_gather_kernel(ny, nz, nv, split, head_ref, hidden_ref, out_ref, feat_ref, send_sem, recv_sem,
                       local_sem, hsend_sem, hrecv_sem, hlocal_sem):
    dp = lax.axis_index("dp")
    v = lax.axis_index("vocab")
    y = dp // nz
    z = dp % nz
    yr = (y + 1) % ny
    yl = (y + ny - 1) % ny

    def zs(k):
        return (z + k + 8 * nz) % nz

    def ys(k):
        return (y + k + 8 * ny) % ny

    def dev(yy, zz):
        return (yy * nz + zz, v)

    width = head_ref.shape[1]
    parts = 4
    prow = head_ref.shape[0] // parts
    rows, hr = prow, prow // 2
    cols = (pl.ds(0, split), pl.ds(split, width - split))

    barrier = pltpu.get_barrier_semaphore()
    peers = [dev(yr, z), dev(yl, z), dev(y, zs(1)), dev(y, zs(-1))]
    peers += [(dp, (v + k) % nv) for k in range(1, nv)]
    for peer in peers:
        pl.semaphore_signal(barrier, inc=1, device_id=peer, device_id_type=MESH)
    pl.semaphore_wait(barrier, len(peers))

    copies = {}

    def send(key, src, dst, peer):
        c = pltpu.make_async_remote_copy(
            src_ref=src,
            dst_ref=dst,
            send_sem=send_sem.at[len(copies)],
            recv_sem=recv_sem.at[len(copies)],
            device_id=peer,
            device_id_type=MESH,
        )
        copies[key] = c
        c.start()

    def arrived(key):
        copies[key].wait_recv()

    local = pltpu.make_async_copy(head_ref, out_ref.at[y, z], local_sem)
    local.start()

    breadth = hidden_ref.shape[1]
    own_cols = feat_ref.at[:, pl.ds(pl.multiple_of(v * breadth, breadth), breadth)]
    hidden_copies = []
    for k in range(1, nv):
        c = pltpu.make_async_remote_copy(
            src_ref=hidden_ref,
            dst_ref=own_cols,
            send_sem=hsend_sem.at[k - 1],
            recv_sem=hrecv_sem.at[k - 1],
            device_id=(dp, (v + k) % nv),
            device_id_type=MESH,
        )
        c.start()
        hidden_copies.append(c)
    hidden_local = pltpu.make_async_copy(hidden_ref, own_cols, hlocal_sem)
    hidden_local.start()

    plan = []

    def ring_plan(name, n, block, right, left, first_src, needs0):
        steps = n // 2
        for step in range(1, steps + 1):
            for side, peer, sign in (("r", right, -1), ("l", left, 1)):
                key = f"{name}{side}{step}"
                view = block(sign * (step - 1))
                if 2 * step == n and opp != "split":
                    if side != opp:
                        continue
                    src = first_src if (step == 1 and first_src is not None) else view
                elif 2 * step == n:
                    view = view.at[pl.ds(0, hr)] if side == "r" else view.at[pl.ds(hr, rows - hr)]
                    src = view
                elif step == 1 and first_src is not None:
                    src = first_src
                else:
                    src = view
                if step == 1 and 2 * step == n and first_src is not None:
                    src = first_src.at[pl.ds(0, hr)] if side == "r" else first_src.at[pl.ds(hr, rows - hr)]
                needs = list(needs0) if step == 1 else [f"{name}{side}{step - 1}"]
                plan.append((key, src, view, peer, needs))

    right_y, left_y = dev(yr, z), dev(yl, z)
    right_z, left_z = dev(y, zs(1)), dev(y, zs(-1))

    def arrival_keys(name, n, offset):
        steps = n // 2
        if offset == 0:
            return []
        k = abs(offset) if abs(offset) <= steps else n - abs(offset)
        if 2 * k == n:
            return [f"{name}r{k}", f"{name}l{k}"] if opp == "split" else [f"{name}{opp}{k}"]
        return [f"{name}r{k}"] if offset < 0 else [f"{name}l{k}"]

    y_offsets = [0] + [s * k for k in range(1, ny // 2 + 1) for s in (-1, 1) if not (s == 1 and 2 * k == ny)]
    z_offsets = [0] + [s * k for k in range(1, nz // 2 + 1) for s in (-1, 1) if not (s == 1 and 2 * k == nz)]
    for q in range(parts):
        rq = pl.ds(q * prow, prow)
        opp = "r" if q % 2 == 0 else "l"
        ring_plan(f"ay{q}", ny, lambda k: out_ref.at[ys(k), z, rq, cols[0]], right_y, left_y,
                  head_ref.at[rq, cols[0]], [])
        ring_plan(f"bz{q}", nz, lambda k: out_ref.at[y, zs(k), rq, cols[1]], right_z, left_z,
                  head_ref.at[rq, cols[1]], [])
        for dy in y_offsets:
            ring_plan(f"az{q}.{dy + ny}_", nz,
                      lambda k, dy=dy: out_ref.at[ys(dy), zs(k), rq, cols[0]],
                      right_z, left_z, head_ref.at[rq, cols[0]] if dy == 0 else None,
                      arrival_keys(f"ay{q}", ny, dy))
        for dz in z_offsets:
            ring_plan(f"by{q}.{dz + nz}_", ny,
                      lambda k, dz=dz: out_ref.at[ys(k), zs(dz), rq, cols[1]],
                      right_y, left_y, head_ref.at[rq, cols[1]] if dz == 0 else None,
                      arrival_keys(f"bz{q}", nz, dz))

    level = {}
    for key, _, _, _, needs in plan:
        level[key] = 1 + max([level[n] for n in needs], default=-1)
    order = sorted(range(len(plan)), key=lambda i: (level[plan[i][0]], i))
    index = {plan[i][0]: i for i in range(len(plan))}
    waited = set()
    copies = {}
    for i in order:
        key, src, dst, peer, needs = plan[i]
        for n in needs:
            if n not in waited:
                copies[n].wait_recv()
                waited.add(n)
        c = pltpu.make_async_remote_copy(
            src_ref=src,
            dst_ref=dst,
            send_sem=send_sem.at[index[key]],
            recv_sem=recv_sem.at[index[key]],
            device_id=peer,
            device_id_type=MESH,
        )
        c.start()
        copies[key] = c
    for i in order:
        key = plan[i][0]
        if key not in waited:
            copies[key].wait_recv()
            waited.add(key)
    local.wait()
    hidden_local.wait()
    for c in hidden_copies:
        c.wait_recv()
    for c in list(copies.values()) + hidden_copies:
        c.wait_send()


def gather_all(head, hidden, ny, nz, nv):
    rows, width = head.shape
    slots, breadth = hidden.shape
    split = max(128, min(width - 128, int(round(width * 0.405 / 128)) * 128))
    streams = 8 * (ny // 2 + nz // 2 + ny * (nz // 2) + nz * (ny // 2))
    out, feat = pl.pallas_call(
        functools.partial(head_gather_kernel, ny, nz, nv, split),
        out_shape=(
            jax.ShapeDtypeStruct((ny, nz, rows, width), head.dtype),
            jax.ShapeDtypeStruct((slots, nv * breadth), hidden.dtype),
        ),
        in_specs=[pl.BlockSpec(memory_space=pl.ANY)] * 2,
        out_specs=(pl.BlockSpec(memory_space=pl.ANY),) * 2,
        scratch_shapes=[
            pltpu.SemaphoreType.DMA((streams,)),
            pltpu.SemaphoreType.DMA((streams,)),
            pltpu.SemaphoreType.DMA(()),
            pltpu.SemaphoreType.DMA((nv - 1,)),
            pltpu.SemaphoreType.DMA((nv - 1,)),
            pltpu.SemaphoreType.DMA(()),
        ],
        compiler_params=pltpu.CompilerParams(collective_id=0, has_side_effects=True),
        cost_estimate=pl.CostEstimate(
            flops=0, transcendentals=0, bytes_accessed=2 * ny * nz * rows * width * 2
        ),
    )(head, hidden)
    return out.reshape(ny * nz * rows, width), feat


def stats_kernel(n, stats_ref, out_ref, send_sem, recv_sem):
    dp = lax.axis_index("dp")
    v = lax.axis_index("vocab")
    barrier = pltpu.get_barrier_semaphore()
    for k in range(1, n):
        pl.semaphore_signal(barrier, inc=1, device_id=(dp, (v + k) % n), device_id_type=MESH)
    pl.semaphore_wait(barrier, n - 1)
    copies = []
    for k in range(1, n):
        c = pltpu.make_async_remote_copy(
            src_ref=stats_ref,
            dst_ref=out_ref.at[v],
            send_sem=send_sem.at[k - 1],
            recv_sem=recv_sem.at[k - 1],
            device_id=(dp, (v + k) % n),
            device_id_type=MESH,
        )
        c.start()
        copies.append(c)
    out_ref[v] = stats_ref[...]
    for c in copies:
        c.wait_recv()
    for c in copies:
        c.wait_send()


def exchange_stats(stats, n):
    return pl.pallas_call(
        functools.partial(stats_kernel, n),
        out_shape=jax.ShapeDtypeStruct((n,) + stats.shape, stats.dtype),
        in_specs=[pl.BlockSpec(memory_space=pltpu.VMEM)],
        out_specs=pl.BlockSpec(memory_space=pltpu.VMEM),
        scratch_shapes=[
            pltpu.SemaphoreType.DMA((n - 1,)),
            pltpu.SemaphoreType.DMA((n - 1,)),
        ],
        compiler_params=pltpu.CompilerParams(collective_id=1, has_side_effects=True),
    )(stats)


def local(ny, nz, hidden, gain, head, target_ids, seq_lens, seq_owner):
    groups = lax.axis_size("dp")
    slices = lax.axis_size("vocab")
    position = lax.axis_index("dp")
    slice_index = lax.axis_index("vocab")
    slots = hidden.shape[0]
    breadth = head.shape[1]
    owners = jnp.arange(groups, dtype=jnp.int32)
    loads = jnp.sum(jnp.where(seq_owner[:, None] == owners[None, :], seq_lens[:, None], 0), axis=0)
    own_live = jnp.arange(slots, dtype=jnp.int32) < loads[position]
    columns, features = gather_all(head, hidden, ny, nz, slices)
    wide = features.astype(jnp.float32)
    normed = (
        wide
        * lax.rsqrt(jnp.mean(wide * wide, axis=1, keepdims=True) + EPS)
        * gain.astype(jnp.float32)
    ).astype(jnp.bfloat16)
    logits = jnp.dot(normed, columns, preferred_element_type=jnp.float32)
    top_local = jnp.max(logits, axis=1)
    expo = jnp.exp(logits - top_local[:, None])
    total_local = jnp.sum(expo, axis=1)
    weighted_local = jnp.sum(expo * logits, axis=1)
    local_id = target_ids - slice_index * breadth
    ids = lax.broadcasted_iota(jnp.int32, logits.shape, 1)
    picked_local = jnp.sum(jnp.where(ids == local_id[:, None], logits, 0.0), axis=1)
    stats = jnp.stack([top_local, total_local, weighted_local, picked_local])
    every = exchange_stats(stats, slices)
    tops = every[:, 0]
    top = jnp.max(tops, axis=0)
    factor = jnp.exp(tops - top[None, :])
    total = jnp.sum(every[:, 1] * factor, axis=0)
    weighted = jnp.sum(every[:, 2] * factor, axis=0)
    picked = jnp.sum(every[:, 3], axis=0)
    lse = top + jnp.log(total)
    logprob = picked - lse
    entropy = lse - weighted / total
    return (jnp.where(own_live, logprob, 0.0), jnp.where(own_live, entropy, 0.0))


def solution(mesh):
    ny, nz = dp_grid(mesh)
    return jax.shard_map(
        functools.partial(local, ny, nz),
        mesh=mesh,
        in_specs=(P("dp", "vocab"), P(), P("dp", "vocab"), P("dp"), P(), P()),
        out_specs=(P("dp"), P("dp")),
        check_vma=False,
    )
```

```python
import functools

import jax
import jax.numpy as jnp
from jax import lax
from jax.experimental import pallas as pl
from jax.experimental.pallas import tpu as pltpu
from jax.sharding import PartitionSpec as P

EPS = 1e-05
MESH = pl.DeviceIdType.MESH


def dp_grid(mesh):
    size = mesh.shape["dp"]
    try:
        zs = {tuple(mesh.devices[i, 0].coords)[2] for i in range(size)}
        nz = len(zs)
    except Exception:
        nz = size // 4
    return size // nz, nz


def head_gather_kernel(ny, nz, nv, split, head_ref, hidden_ref, gain_ref, out_ref, normed_ref,
                       send_sem, recv_sem, local_sem, hsend_sem, hrecv_sem, hlocal_sem, feat_ref):
    dp = lax.axis_index("dp")
    v = lax.axis_index("vocab")
    y = dp // nz
    z = dp % nz
    yr = (y + 1) % ny
    yl = (y + ny - 1) % ny

    def zs(k):
        return (z + k + 8 * nz) % nz

    def ys(k):
        return (y + k + 8 * ny) % ny

    def dev(yy, zz):
        return (yy * nz + zz, v)

    width = head_ref.shape[1]
    parts = 2
    prow = head_ref.shape[0] // parts
    rows, hr = prow, prow // 2
    cols = (pl.ds(0, split), pl.ds(split, width - split))

    barrier = pltpu.get_barrier_semaphore()
    peers = [dev(yr, z), dev(yl, z), dev(y, zs(1)), dev(y, zs(-1))]
    peers += [(dp, (v + k) % nv) for k in range(1, nv)]
    for peer in peers:
        pl.semaphore_signal(barrier, inc=1, device_id=peer, device_id_type=MESH)
    pl.semaphore_wait(barrier, len(peers))

    copies = {}

    def send(key, src, dst, peer):
        c = pltpu.make_async_remote_copy(
            src_ref=src,
            dst_ref=dst,
            send_sem=send_sem.at[len(copies)],
            recv_sem=recv_sem.at[len(copies)],
            device_id=peer,
            device_id_type=MESH,
        )
        copies[key] = c
        c.start()

    def arrived(key):
        copies[key].wait_recv()

    local = pltpu.make_async_copy(head_ref, out_ref.at[y, z], local_sem)
    local.start()

    breadth = hidden_ref.shape[1]
    own_cols = feat_ref.at[:, pl.ds(pl.multiple_of(v * breadth, breadth), breadth)]
    hidden_copies = []
    for k in range(1, nv):
        c = pltpu.make_async_remote_copy(
            src_ref=hidden_ref,
            dst_ref=own_cols,
            send_sem=hsend_sem.at[k - 1],
            recv_sem=hrecv_sem.at[k - 1],
            device_id=(dp, (v + k) % nv),
            device_id_type=MESH,
        )
        c.start()
        hidden_copies.append(c)
    hidden_local = pltpu.make_async_copy(hidden_ref, own_cols, hlocal_sem)
    hidden_local.start()

    plan = []

    def ring_plan(name, n, block, right, left, first_src, needs0):
        steps = n // 2
        for step in range(1, steps + 1):
            for side, peer, sign in (("r", right, -1), ("l", left, 1)):
                key = f"{name}{side}{step}"
                view = block(sign * (step - 1))
                if 2 * step == n:
                    view = view.at[pl.ds(0, hr)] if side == "r" else view.at[pl.ds(hr, rows - hr)]
                    src = view
                elif step == 1 and first_src is not None:
                    src = first_src
                else:
                    src = view
                if step == 1 and 2 * step == n and first_src is not None:
                    src = first_src.at[pl.ds(0, hr)] if side == "r" else first_src.at[pl.ds(hr, rows - hr)]
                needs = list(needs0) if step == 1 else [f"{name}{side}{step - 1}"]
                plan.append((key, src, view, peer, needs))

    right_y, left_y = dev(yr, z), dev(yl, z)
    right_z, left_z = dev(y, zs(1)), dev(y, zs(-1))

    def arrival_keys(name, n, offset):
        steps = n // 2
        if offset == 0:
            return []
        k = abs(offset) if abs(offset) <= steps else n - abs(offset)
        if 2 * k == n:
            return [f"{name}r{k}", f"{name}l{k}"]
        return [f"{name}r{k}"] if offset < 0 else [f"{name}l{k}"]

    y_offsets = [0] + [s * k for k in range(1, ny // 2 + 1) for s in (-1, 1) if not (s == 1 and 2 * k == ny)]
    z_offsets = [0] + [s * k for k in range(1, nz // 2 + 1) for s in (-1, 1) if not (s == 1 and 2 * k == nz)]
    for q in range(parts):
        rq = pl.ds(q * prow, prow)
        ring_plan(f"ay{q}", ny, lambda k: out_ref.at[ys(k), z, rq, cols[0]], right_y, left_y,
                  head_ref.at[rq, cols[0]], [])
        ring_plan(f"bz{q}", nz, lambda k: out_ref.at[y, zs(k), rq, cols[1]], right_z, left_z,
                  head_ref.at[rq, cols[1]], [])
        for dy in y_offsets:
            ring_plan(f"az{q}.{dy + ny}_", nz,
                      lambda k, dy=dy: out_ref.at[ys(dy), zs(k), rq, cols[0]],
                      right_z, left_z, head_ref.at[rq, cols[0]] if dy == 0 else None,
                      arrival_keys(f"ay{q}", ny, dy))
        for dz in z_offsets:
            ring_plan(f"by{q}.{dz + nz}_", ny,
                      lambda k, dz=dz: out_ref.at[ys(k), zs(dz), rq, cols[1]],
                      right_y, left_y, head_ref.at[rq, cols[1]] if dz == 0 else None,
                      arrival_keys(f"bz{q}", nz, dz))

    level = {}
    for key, _, _, _, needs in plan:
        level[key] = 1 + max([level[n] for n in needs], default=-1)
    order = sorted(range(len(plan)), key=lambda i: (level[plan[i][0]], i))
    index = {plan[i][0]: i for i in range(len(plan))}
    waited = set()
    copies = {}
    for i in order:
        key, src, dst, peer, needs = plan[i]
        for n in needs:
            if n not in waited:
                copies[n].wait_recv()
                waited.add(n)
        c = pltpu.make_async_remote_copy(
            src_ref=src,
            dst_ref=dst,
            send_sem=send_sem.at[index[key]],
            recv_sem=recv_sem.at[index[key]],
            device_id=peer,
            device_id_type=MESH,
        )
        c.start()
        copies[key] = c
    hidden_local.wait()
    for c in hidden_copies:
        c.wait_recv()
    tile = 64

    def norm_rows(i, carry):
        r = pl.ds(pl.multiple_of(i * tile, tile), tile)
        wide = feat_ref[r, :].astype(jnp.float32)
        scale = lax.rsqrt(jnp.mean(wide * wide, axis=1, keepdims=True) + EPS)
        normed_ref[r, :] = (wide * scale * gain_ref[...]).astype(normed_ref.dtype)
        return carry

    lax.fori_loop(0, feat_ref.shape[0] // tile, norm_rows, 0)
    for i in order:
        key = plan[i][0]
        if key not in waited:
            copies[key].wait_recv()
            waited.add(key)
    local.wait()
    for c in list(copies.values()) + hidden_copies:
        c.wait_send()


def gather_all(head, hidden, gain, ny, nz, nv):
    rows, width = head.shape
    slots, breadth = hidden.shape
    split = max(128, min(width - 128, int(round(width * 0.405 / 128)) * 128))
    streams = 4 * (ny // 2 + nz // 2 + ny * (nz // 2) + nz * (ny // 2))
    out, normed = pl.pallas_call(
        functools.partial(head_gather_kernel, ny, nz, nv, split),
        out_shape=(
            jax.ShapeDtypeStruct((ny, nz, rows, width), head.dtype),
            jax.ShapeDtypeStruct((slots, nv * breadth), hidden.dtype),
        ),
        in_specs=[pl.BlockSpec(memory_space=pl.ANY)] * 2 + [pl.BlockSpec(memory_space=pltpu.VMEM)],
        out_specs=(pl.BlockSpec(memory_space=pl.ANY), pl.BlockSpec(memory_space=pltpu.VMEM)),
        scratch_shapes=[
            pltpu.SemaphoreType.DMA((streams,)),
            pltpu.SemaphoreType.DMA((streams,)),
            pltpu.SemaphoreType.DMA(()),
            pltpu.SemaphoreType.DMA((nv - 1,)),
            pltpu.SemaphoreType.DMA((nv - 1,)),
            pltpu.SemaphoreType.DMA(()),
            pltpu.VMEM((slots, nv * breadth), hidden.dtype),
        ],
        compiler_params=pltpu.CompilerParams(collective_id=0, has_side_effects=True),
        cost_estimate=pl.CostEstimate(
            flops=0, transcendentals=0, bytes_accessed=2 * ny * nz * rows * width * 2
        ),
    )(head, hidden, gain.astype(jnp.float32).reshape(1, nv * breadth))
    return out.reshape(ny * nz * rows, width), normed


def stats_kernel(n, stats_ref, out_ref, send_sem, recv_sem):
    dp = lax.axis_index("dp")
    v = lax.axis_index("vocab")
    barrier = pltpu.get_barrier_semaphore()
    for k in range(1, n):
        pl.semaphore_signal(barrier, inc=1, device_id=(dp, (v + k) % n), device_id_type=MESH)
    pl.semaphore_wait(barrier, n - 1)
    copies = []
    for k in range(1, n):
        c = pltpu.make_async_remote_copy(
            src_ref=stats_ref,
            dst_ref=out_ref.at[v],
            send_sem=send_sem.at[k - 1],
            recv_sem=recv_sem.at[k - 1],
            device_id=(dp, (v + k) % n),
            device_id_type=MESH,
        )
        c.start()
        copies.append(c)
    out_ref[v] = stats_ref[...]
    for c in copies:
        c.wait_recv()
    for c in copies:
        c.wait_send()


def exchange_stats(stats, n):
    return pl.pallas_call(
        functools.partial(stats_kernel, n),
        out_shape=jax.ShapeDtypeStruct((n,) + stats.shape, stats.dtype),
        in_specs=[pl.BlockSpec(memory_space=pltpu.VMEM)],
        out_specs=pl.BlockSpec(memory_space=pltpu.VMEM),
        scratch_shapes=[
            pltpu.SemaphoreType.DMA((n - 1,)),
            pltpu.SemaphoreType.DMA((n - 1,)),
        ],
        compiler_params=pltpu.CompilerParams(collective_id=1, has_side_effects=True),
    )(stats)


def local(ny, nz, hidden, gain, head, target_ids, seq_lens, seq_owner):
    groups = lax.axis_size("dp")
    slices = lax.axis_size("vocab")
    position = lax.axis_index("dp")
    slice_index = lax.axis_index("vocab")
    slots = hidden.shape[0]
    breadth = head.shape[1]
    owners = jnp.arange(groups, dtype=jnp.int32)
    loads = jnp.sum(jnp.where(seq_owner[:, None] == owners[None, :], seq_lens[:, None], 0), axis=0)
    own_live = jnp.arange(slots, dtype=jnp.int32) < loads[position]
    columns, normed = gather_all(head, hidden, gain, ny, nz, slices)
    logits = jnp.dot(normed, columns, preferred_element_type=jnp.float32)
    top_local = jnp.max(logits, axis=1)
    expo = jnp.exp(logits - top_local[:, None])
    total_local = jnp.sum(expo, axis=1)
    weighted_local = jnp.sum(expo * logits, axis=1)
    local_id = target_ids - slice_index * breadth
    ids = lax.broadcasted_iota(jnp.int32, logits.shape, 1)
    picked_local = jnp.sum(jnp.where(ids == local_id[:, None], logits, 0.0), axis=1)
    stats = jnp.stack([top_local, total_local, weighted_local, picked_local])
    every = exchange_stats(stats, slices)
    tops = every[:, 0]
    top = jnp.max(tops, axis=0)
    factor = jnp.exp(tops - top[None, :])
    total = jnp.sum(every[:, 1] * factor, axis=0)
    weighted = jnp.sum(every[:, 2] * factor, axis=0)
    picked = jnp.sum(every[:, 3], axis=0)
    lse = top + jnp.log(total)
    logprob = picked - lse
    entropy = lse - weighted / total
    return (jnp.where(own_live, logprob, 0.0), jnp.where(own_live, entropy, 0.0))


def solution(mesh):
    ny, nz = dp_grid(mesh)
    return jax.shard_map(
        functools.partial(local, ny, nz),
        mesh=mesh,
        in_specs=(P("dp", "vocab"), P(), P("dp", "vocab"), P("dp"), P(), P()),
        out_specs=(P("dp"), P("dp")),
        check_vma=False,
    )
```

```python
import functools

import jax
import jax.numpy as jnp
from jax import lax
from jax.experimental import pallas as pl
from jax.experimental.pallas import tpu as pltpu
from jax.sharding import PartitionSpec as P

EPS = 1e-05
MESH = pl.DeviceIdType.MESH


def dp_grid(mesh):
    size = mesh.shape["dp"]
    try:
        zs = {tuple(mesh.devices[i, 0].coords)[2] for i in range(size)}
        nz = len(zs)
    except Exception:
        nz = size // 4
    return size // nz, nz


def head_gather_kernel(ny, nz, nv, split, head_ref, hidden_ref, gain_ref, out_ref, normed_ref,
                       send_sem, recv_sem, local_sem, hsend_sem, hrecv_sem, hlocal_sem, feat_ref):
    dp = lax.axis_index("dp")
    v = lax.axis_index("vocab")
    y = dp // nz
    z = dp % nz
    yr = (y + 1) % ny
    yl = (y + ny - 1) % ny

    def zs(k):
        return (z + k + 8 * nz) % nz

    def ys(k):
        return (y + k + 8 * ny) % ny

    def dev(yy, zz):
        return (yy * nz + zz, v)

    width = head_ref.shape[1]
    parts = 2
    prow = head_ref.shape[0] // parts
    rows, hr = prow, prow // 2
    cols = (pl.ds(0, split), pl.ds(split, width - split))

    barrier = pltpu.get_barrier_semaphore()
    peers = [dev(yr, z), dev(yl, z), dev(y, zs(1)), dev(y, zs(-1))]
    peers += [(dp, (v + k) % nv) for k in range(1, nv)]
    for peer in peers:
        pl.semaphore_signal(barrier, inc=1, device_id=peer, device_id_type=MESH)
    pl.semaphore_wait(barrier, len(peers))

    copies = {}

    def send(key, src, dst, peer):
        c = pltpu.make_async_remote_copy(
            src_ref=src,
            dst_ref=dst,
            send_sem=send_sem.at[len(copies)],
            recv_sem=recv_sem.at[len(copies)],
            device_id=peer,
            device_id_type=MESH,
        )
        copies[key] = c
        c.start()

    def arrived(key):
        copies[key].wait_recv()

    local = pltpu.make_async_copy(head_ref, out_ref.at[y, z], local_sem)
    local.start()

    breadth = hidden_ref.shape[1]
    own_cols = feat_ref.at[:, pl.ds(pl.multiple_of(v * breadth, breadth), breadth)]
    hidden_copies = []
    for k in range(1, nv):
        c = pltpu.make_async_remote_copy(
            src_ref=hidden_ref,
            dst_ref=own_cols,
            send_sem=hsend_sem.at[k - 1],
            recv_sem=hrecv_sem.at[k - 1],
            device_id=(dp, (v + k) % nv),
            device_id_type=MESH,
        )
        c.start()
        hidden_copies.append(c)
    hidden_local = pltpu.make_async_copy(hidden_ref, own_cols, hlocal_sem)
    hidden_local.start()

    plan = []

    def ring_plan(name, n, block, right, left, first_src, needs0):
        steps = n // 2
        for step in range(1, steps + 1):
            for side, peer, sign in (("r", right, -1), ("l", left, 1)):
                key = f"{name}{side}{step}"
                view = block(sign * (step - 1))
                if 2 * step == n:
                    view = view.at[pl.ds(0, hr)] if side == "r" else view.at[pl.ds(hr, rows - hr)]
                    src = view
                elif step == 1 and first_src is not None:
                    src = first_src
                else:
                    src = view
                if step == 1 and 2 * step == n and first_src is not None:
                    src = first_src.at[pl.ds(0, hr)] if side == "r" else first_src.at[pl.ds(hr, rows - hr)]
                needs = list(needs0) if step == 1 else [f"{name}{side}{step - 1}"]
                plan.append((key, src, view, peer, needs))

    right_y, left_y = dev(yr, z), dev(yl, z)
    right_z, left_z = dev(y, zs(1)), dev(y, zs(-1))

    def arrival_keys(name, n, offset):
        steps = n // 2
        if offset == 0:
            return []
        k = abs(offset) if abs(offset) <= steps else n - abs(offset)
        if 2 * k == n:
            return [f"{name}r{k}", f"{name}l{k}"]
        return [f"{name}r{k}"] if offset < 0 else [f"{name}l{k}"]

    y_offsets = [0] + [s * k for k in range(1, ny // 2 + 1) for s in (-1, 1) if not (s == 1 and 2 * k == ny)]
    z_offsets = [0] + [s * k for k in range(1, nz // 2 + 1) for s in (-1, 1) if not (s == 1 and 2 * k == nz)]
    for q in range(parts):
        rq = pl.ds(q * prow, prow)
        ring_plan(f"ay{q}", ny, lambda k: out_ref.at[ys(k), z, rq, cols[0]], right_y, left_y,
                  head_ref.at[rq, cols[0]], [])
        ring_plan(f"bz{q}", nz, lambda k: out_ref.at[y, zs(k), rq, cols[1]], right_z, left_z,
                  head_ref.at[rq, cols[1]], [])
        for dy in y_offsets:
            ring_plan(f"az{q}.{dy + ny}_", nz,
                      lambda k, dy=dy: out_ref.at[ys(dy), zs(k), rq, cols[0]],
                      right_z, left_z, head_ref.at[rq, cols[0]] if dy == 0 else None,
                      arrival_keys(f"ay{q}", ny, dy))
        for dz in z_offsets:
            ring_plan(f"by{q}.{dz + nz}_", ny,
                      lambda k, dz=dz: out_ref.at[ys(k), zs(dz), rq, cols[1]],
                      right_y, left_y, head_ref.at[rq, cols[1]] if dz == 0 else None,
                      arrival_keys(f"bz{q}", nz, dz))

    level = {}
    for key, _, _, _, needs in plan:
        level[key] = 1 + max([level[n] for n in needs], default=-1)
    order = sorted(range(len(plan)), key=lambda i: (level[plan[i][0]], i))
    index = {plan[i][0]: i for i in range(len(plan))}
    waited = set()
    copies = {}
    for i in order:
        key, src, dst, peer, needs = plan[i]
        for n in needs:
            if n not in waited:
                copies[n].wait_recv()
                waited.add(n)
        c = pltpu.make_async_remote_copy(
            src_ref=src,
            dst_ref=dst,
            send_sem=send_sem.at[index[key]],
            recv_sem=recv_sem.at[index[key]],
            device_id=peer,
            device_id_type=MESH,
        )
        c.start()
        copies[key] = c
    hidden_local.wait()
    for c in hidden_copies:
        c.wait_recv()
    tile = 64

    def norm_rows(i, carry):
        r = pl.ds(pl.multiple_of(i * tile, tile), tile)
        wide = feat_ref[r, :].astype(jnp.float32)
        scale = lax.rsqrt(jnp.mean(wide * wide, axis=1, keepdims=True) + EPS)
        normed_ref[r, :] = (wide * scale * gain_ref[...]).astype(normed_ref.dtype)
        return carry

    lax.fori_loop(0, feat_ref.shape[0] // tile, norm_rows, 0)
    for i in order:
        key = plan[i][0]
        if key not in waited:
            copies[key].wait_recv()
            waited.add(key)
    local.wait()
    for c in list(copies.values()) + hidden_copies:
        c.wait_send()


def gather_all(head, hidden, gain, ny, nz, nv):
    rows, width = head.shape
    slots, breadth = hidden.shape
    split = max(128, min(width - 128, int(round(width * 0.384 / 128)) * 128))
    streams = 4 * (ny // 2 + nz // 2 + ny * (nz // 2) + nz * (ny // 2))
    out, normed = pl.pallas_call(
        functools.partial(head_gather_kernel, ny, nz, nv, split),
        out_shape=(
            jax.ShapeDtypeStruct((ny, nz, rows, width), head.dtype),
            jax.ShapeDtypeStruct((slots, nv * breadth), hidden.dtype),
        ),
        in_specs=[pl.BlockSpec(memory_space=pl.ANY)] * 2 + [pl.BlockSpec(memory_space=pltpu.VMEM)],
        out_specs=(pl.BlockSpec(memory_space=pl.ANY), pl.BlockSpec(memory_space=pltpu.VMEM)),
        scratch_shapes=[
            pltpu.SemaphoreType.DMA((streams,)),
            pltpu.SemaphoreType.DMA((streams,)),
            pltpu.SemaphoreType.DMA(()),
            pltpu.SemaphoreType.DMA((nv - 1,)),
            pltpu.SemaphoreType.DMA((nv - 1,)),
            pltpu.SemaphoreType.DMA(()),
            pltpu.VMEM((slots, nv * breadth), hidden.dtype),
        ],
        compiler_params=pltpu.CompilerParams(collective_id=0, has_side_effects=True),
        cost_estimate=pl.CostEstimate(
            flops=0, transcendentals=0, bytes_accessed=2 * ny * nz * rows * width * 2
        ),
    )(head, hidden, gain.astype(jnp.float32).reshape(1, nv * breadth))
    return out.reshape(ny * nz * rows, width), normed


def stats_kernel(n, stats_ref, out_ref, send_sem, recv_sem):
    dp = lax.axis_index("dp")
    v = lax.axis_index("vocab")
    barrier = pltpu.get_barrier_semaphore()
    for k in range(1, n):
        pl.semaphore_signal(barrier, inc=1, device_id=(dp, (v + k) % n), device_id_type=MESH)
    pl.semaphore_wait(barrier, n - 1)
    copies = []
    for k in range(1, n):
        c = pltpu.make_async_remote_copy(
            src_ref=stats_ref,
            dst_ref=out_ref.at[v],
            send_sem=send_sem.at[k - 1],
            recv_sem=recv_sem.at[k - 1],
            device_id=(dp, (v + k) % n),
            device_id_type=MESH,
        )
        c.start()
        copies.append(c)
    out_ref[v] = stats_ref[...]
    for c in copies:
        c.wait_recv()
    for c in copies:
        c.wait_send()


def exchange_stats(stats, n):
    return pl.pallas_call(
        functools.partial(stats_kernel, n),
        out_shape=jax.ShapeDtypeStruct((n,) + stats.shape, stats.dtype),
        in_specs=[pl.BlockSpec(memory_space=pltpu.VMEM)],
        out_specs=pl.BlockSpec(memory_space=pltpu.VMEM),
        scratch_shapes=[
            pltpu.SemaphoreType.DMA((n - 1,)),
            pltpu.SemaphoreType.DMA((n - 1,)),
        ],
        compiler_params=pltpu.CompilerParams(collective_id=1, has_side_effects=True),
    )(stats)


def local(ny, nz, hidden, gain, head, target_ids, seq_lens, seq_owner):
    groups = lax.axis_size("dp")
    slices = lax.axis_size("vocab")
    position = lax.axis_index("dp")
    slice_index = lax.axis_index("vocab")
    slots = hidden.shape[0]
    breadth = head.shape[1]
    owners = jnp.arange(groups, dtype=jnp.int32)
    loads = jnp.sum(jnp.where(seq_owner[:, None] == owners[None, :], seq_lens[:, None], 0), axis=0)
    own_live = jnp.arange(slots, dtype=jnp.int32) < loads[position]
    columns, normed = gather_all(head, hidden, gain, ny, nz, slices)
    logits = jnp.dot(normed, columns, preferred_element_type=jnp.float32)
    top_local = jnp.max(logits, axis=1)
    expo = jnp.exp(logits - top_local[:, None])
    total_local = jnp.sum(expo, axis=1)
    weighted_local = jnp.sum(expo * logits, axis=1)
    local_id = target_ids - slice_index * breadth
    ids = lax.broadcasted_iota(jnp.int32, logits.shape, 1)
    picked_local = jnp.sum(jnp.where(ids == local_id[:, None], logits, 0.0), axis=1)
    stats = jnp.stack([top_local, total_local, weighted_local, picked_local])
    every = exchange_stats(stats, slices)
    tops = every[:, 0]
    top = jnp.max(tops, axis=0)
    factor = jnp.exp(tops - top[None, :])
    total = jnp.sum(every[:, 1] * factor, axis=0)
    weighted = jnp.sum(every[:, 2] * factor, axis=0)
    picked = jnp.sum(every[:, 3], axis=0)
    lse = top + jnp.log(total)
    logprob = picked - lse
    entropy = lse - weighted / total
    return (jnp.where(own_live, logprob, 0.0), jnp.where(own_live, entropy, 0.0))


def solution(mesh):
    ny, nz = dp_grid(mesh)
    return jax.shard_map(
        functools.partial(local, ny, nz),
        mesh=mesh,
        in_specs=(P("dp", "vocab"), P(), P("dp", "vocab"), P("dp"), P(), P()),
        out_specs=(P("dp"), P("dp")),
        check_vma=False,
    )
```

```python
import functools

import jax
import jax.numpy as jnp
from jax import lax
from jax.experimental import pallas as pl
from jax.experimental.pallas import tpu as pltpu
from jax.sharding import PartitionSpec as P

EPS = 1e-05
MESH = pl.DeviceIdType.MESH


def dp_grid(mesh):
    size = mesh.shape["dp"]
    try:
        zs = {tuple(mesh.devices[i, 0].coords)[2] for i in range(size)}
        nz = len(zs)
    except Exception:
        nz = size // 4
    return size // nz, nz


def head_gather_kernel(ny, nz, nv, split, head_ref, hidden_ref, gain_ref, out_ref, normed_ref,
                       send_sem, recv_sem, local_sem, hsend_sem, hrecv_sem, hlocal_sem, feat_ref):
    dp = lax.axis_index("dp")
    v = lax.axis_index("vocab")
    y = dp // nz
    z = dp % nz
    yr = (y + 1) % ny
    yl = (y + ny - 1) % ny

    def zs(k):
        return (z + k + 8 * nz) % nz

    def ys(k):
        return (y + k + 8 * ny) % ny

    def dev(yy, zz):
        return (yy * nz + zz, v)

    width = head_ref.shape[1]
    parts = 2
    prow = head_ref.shape[0] // parts
    rows, hr = prow, prow // 2
    cols = (pl.ds(0, split), pl.ds(split, width - split))

    barrier = pltpu.get_barrier_semaphore()
    peers = [dev(yr, z), dev(yl, z), dev(y, zs(1)), dev(y, zs(-1))]
    peers += [(dp, (v + k) % nv) for k in range(1, nv)]
    for peer in peers:
        pl.semaphore_signal(barrier, inc=1, device_id=peer, device_id_type=MESH)
    pl.semaphore_wait(barrier, len(peers))

    copies = {}

    def send(key, src, dst, peer):
        c = pltpu.make_async_remote_copy(
            src_ref=src,
            dst_ref=dst,
            send_sem=send_sem.at[len(copies)],
            recv_sem=recv_sem.at[len(copies)],
            device_id=peer,
            device_id_type=MESH,
        )
        copies[key] = c
        c.start()

    def arrived(key):
        copies[key].wait_recv()

    local = pltpu.make_async_copy(head_ref, out_ref.at[y, z], local_sem)
    local.start()

    breadth = hidden_ref.shape[1]
    own_cols = feat_ref.at[:, pl.ds(pl.multiple_of(v * breadth, breadth), breadth)]
    hidden_copies = []
    for k in range(1, nv):
        c = pltpu.make_async_remote_copy(
            src_ref=hidden_ref,
            dst_ref=own_cols,
            send_sem=hsend_sem.at[k - 1],
            recv_sem=hrecv_sem.at[k - 1],
            device_id=(dp, (v + k) % nv),
            device_id_type=MESH,
        )
        c.start()
        hidden_copies.append(c)
    hidden_local = pltpu.make_async_copy(hidden_ref, own_cols, hlocal_sem)
    hidden_local.start()

    plan = []

    def ring_plan(name, n, block, right, left, first_src, needs0):
        steps = n // 2
        for step in range(1, steps + 1):
            for side, peer, sign in (("r", right, -1), ("l", left, 1)):
                key = f"{name}{side}{step}"
                view = block(sign * (step - 1))
                if 2 * step == n and opp != "split":
                    if side != opp:
                        continue
                    src = first_src if (step == 1 and first_src is not None) else view
                elif 2 * step == n:
                    view = view.at[pl.ds(0, hr)] if side == "r" else view.at[pl.ds(hr, rows - hr)]
                    src = view
                elif step == 1 and first_src is not None:
                    src = first_src
                else:
                    src = view
                if step == 1 and 2 * step == n and first_src is not None:
                    src = first_src.at[pl.ds(0, hr)] if side == "r" else first_src.at[pl.ds(hr, rows - hr)]
                needs = list(needs0) if step == 1 else [f"{name}{side}{step - 1}"]
                plan.append((key, src, view, peer, needs))

    right_y, left_y = dev(yr, z), dev(yl, z)
    right_z, left_z = dev(y, zs(1)), dev(y, zs(-1))

    def arrival_keys(name, n, offset):
        steps = n // 2
        if offset == 0:
            return []
        k = abs(offset) if abs(offset) <= steps else n - abs(offset)
        if 2 * k == n:
            return [f"{name}r{k}", f"{name}l{k}"] if opp == "split" else [f"{name}{opp}{k}"]
        return [f"{name}r{k}"] if offset < 0 else [f"{name}l{k}"]

    y_offsets = [0] + [s * k for k in range(1, ny // 2 + 1) for s in (-1, 1) if not (s == 1 and 2 * k == ny)]
    z_offsets = [0] + [s * k for k in range(1, nz // 2 + 1) for s in (-1, 1) if not (s == 1 and 2 * k == nz)]
    for q in range(parts):
        rq = pl.ds(q * prow, prow)
        opp = "r" if q % 2 == 0 else "l"
        ring_plan(f"ay{q}", ny, lambda k: out_ref.at[ys(k), z, rq, cols[0]], right_y, left_y,
                  head_ref.at[rq, cols[0]], [])
        ring_plan(f"bz{q}", nz, lambda k: out_ref.at[y, zs(k), rq, cols[1]], right_z, left_z,
                  head_ref.at[rq, cols[1]], [])
        for dy in y_offsets:
            ring_plan(f"az{q}.{dy + ny}_", nz,
                      lambda k, dy=dy: out_ref.at[ys(dy), zs(k), rq, cols[0]],
                      right_z, left_z, head_ref.at[rq, cols[0]] if dy == 0 else None,
                      arrival_keys(f"ay{q}", ny, dy))
        for dz in z_offsets:
            ring_plan(f"by{q}.{dz + nz}_", ny,
                      lambda k, dz=dz: out_ref.at[ys(k), zs(dz), rq, cols[1]],
                      right_y, left_y, head_ref.at[rq, cols[1]] if dz == 0 else None,
                      arrival_keys(f"bz{q}", nz, dz))

    level = {}
    for key, _, _, _, needs in plan:
        level[key] = 1 + max([level[n] for n in needs], default=-1)
    order = sorted(range(len(plan)), key=lambda i: (level[plan[i][0]], i))
    index = {plan[i][0]: i for i in range(len(plan))}
    waited = set()
    copies = {}
    for i in order:
        key, src, dst, peer, needs = plan[i]
        for n in needs:
            if n not in waited:
                copies[n].wait_recv()
                waited.add(n)
        c = pltpu.make_async_remote_copy(
            src_ref=src,
            dst_ref=dst,
            send_sem=send_sem.at[index[key]],
            recv_sem=recv_sem.at[index[key]],
            device_id=peer,
            device_id_type=MESH,
        )
        c.start()
        copies[key] = c
    hidden_local.wait()
    for c in hidden_copies:
        c.wait_recv()
    tile = 64

    def norm_rows(i, carry):
        r = pl.ds(pl.multiple_of(i * tile, tile), tile)
        wide = feat_ref[r, :].astype(jnp.float32)
        scale = lax.rsqrt(jnp.mean(wide * wide, axis=1, keepdims=True) + EPS)
        normed_ref[r, :] = (wide * scale * gain_ref[...]).astype(normed_ref.dtype)
        return carry

    lax.fori_loop(0, feat_ref.shape[0] // tile, norm_rows, 0)
    for i in order:
        key = plan[i][0]
        if key not in waited:
            copies[key].wait_recv()
            waited.add(key)
    local.wait()
    for c in list(copies.values()) + hidden_copies:
        c.wait_send()


def gather_all(head, hidden, gain, ny, nz, nv):
    rows, width = head.shape
    slots, breadth = hidden.shape
    split = max(128, min(width - 128, int(round(width * 0.384 / 128)) * 128))
    streams = 4 * (ny // 2 + nz // 2 + ny * (nz // 2) + nz * (ny // 2))
    out, normed = pl.pallas_call(
        functools.partial(head_gather_kernel, ny, nz, nv, split),
        out_shape=(
            jax.ShapeDtypeStruct((ny, nz, rows, width), head.dtype),
            jax.ShapeDtypeStruct((slots, nv * breadth), hidden.dtype),
        ),
        in_specs=[pl.BlockSpec(memory_space=pl.ANY)] * 2 + [pl.BlockSpec(memory_space=pltpu.VMEM)],
        out_specs=(pl.BlockSpec(memory_space=pl.ANY), pl.BlockSpec(memory_space=pltpu.VMEM)),
        scratch_shapes=[
            pltpu.SemaphoreType.DMA((streams,)),
            pltpu.SemaphoreType.DMA((streams,)),
            pltpu.SemaphoreType.DMA(()),
            pltpu.SemaphoreType.DMA((nv - 1,)),
            pltpu.SemaphoreType.DMA((nv - 1,)),
            pltpu.SemaphoreType.DMA(()),
            pltpu.VMEM((slots, nv * breadth), hidden.dtype),
        ],
        compiler_params=pltpu.CompilerParams(collective_id=0, has_side_effects=True),
        cost_estimate=pl.CostEstimate(
            flops=0, transcendentals=0, bytes_accessed=2 * ny * nz * rows * width * 2
        ),
    )(head, hidden, gain.astype(jnp.float32).reshape(1, nv * breadth))
    return out.reshape(ny * nz * rows, width), normed


def stats_kernel(n, stats_ref, out_ref, send_sem, recv_sem):
    dp = lax.axis_index("dp")
    v = lax.axis_index("vocab")
    barrier = pltpu.get_barrier_semaphore()
    for k in range(1, n):
        pl.semaphore_signal(barrier, inc=1, device_id=(dp, (v + k) % n), device_id_type=MESH)
    pl.semaphore_wait(barrier, n - 1)
    copies = []
    for k in range(1, n):
        c = pltpu.make_async_remote_copy(
            src_ref=stats_ref,
            dst_ref=out_ref.at[v],
            send_sem=send_sem.at[k - 1],
            recv_sem=recv_sem.at[k - 1],
            device_id=(dp, (v + k) % n),
            device_id_type=MESH,
        )
        c.start()
        copies.append(c)
    out_ref[v] = stats_ref[...]
    for c in copies:
        c.wait_recv()
    for c in copies:
        c.wait_send()


def exchange_stats(stats, n):
    return pl.pallas_call(
        functools.partial(stats_kernel, n),
        out_shape=jax.ShapeDtypeStruct((n,) + stats.shape, stats.dtype),
        in_specs=[pl.BlockSpec(memory_space=pltpu.VMEM)],
        out_specs=pl.BlockSpec(memory_space=pltpu.VMEM),
        scratch_shapes=[
            pltpu.SemaphoreType.DMA((n - 1,)),
            pltpu.SemaphoreType.DMA((n - 1,)),
        ],
        compiler_params=pltpu.CompilerParams(collective_id=1, has_side_effects=True),
    )(stats)


def local(ny, nz, hidden, gain, head, target_ids, seq_lens, seq_owner):
    groups = lax.axis_size("dp")
    slices = lax.axis_size("vocab")
    position = lax.axis_index("dp")
    slice_index = lax.axis_index("vocab")
    slots = hidden.shape[0]
    breadth = head.shape[1]
    owners = jnp.arange(groups, dtype=jnp.int32)
    loads = jnp.sum(jnp.where(seq_owner[:, None] == owners[None, :], seq_lens[:, None], 0), axis=0)
    own_live = jnp.arange(slots, dtype=jnp.int32) < loads[position]
    columns, normed = gather_all(head, hidden, gain, ny, nz, slices)
    logits = jnp.dot(normed, columns, preferred_element_type=jnp.float32)
    top_local = jnp.max(logits, axis=1)
    expo = jnp.exp(logits - top_local[:, None])
    total_local = jnp.sum(expo, axis=1)
    weighted_local = jnp.sum(expo * logits, axis=1)
    local_id = target_ids - slice_index * breadth
    ids = lax.broadcasted_iota(jnp.int32, logits.shape, 1)
    picked_local = jnp.sum(jnp.where(ids == local_id[:, None], logits, 0.0), axis=1)
    stats = jnp.stack([top_local, total_local, weighted_local, picked_local])
    every = exchange_stats(stats, slices)
    tops = every[:, 0]
    top = jnp.max(tops, axis=0)
    factor = jnp.exp(tops - top[None, :])
    total = jnp.sum(every[:, 1] * factor, axis=0)
    weighted = jnp.sum(every[:, 2] * factor, axis=0)
    picked = jnp.sum(every[:, 3], axis=0)
    lse = top + jnp.log(total)
    logprob = picked - lse
    entropy = lse - weighted / total
    return (jnp.where(own_live, logprob, 0.0), jnp.where(own_live, entropy, 0.0))


def solution(mesh):
    ny, nz = dp_grid(mesh)
    return jax.shard_map(
        functools.partial(local, ny, nz),
        mesh=mesh,
        in_specs=(P("dp", "vocab"), P(), P("dp", "vocab"), P("dp"), P(), P()),
        out_specs=(P("dp"), P("dp")),
        check_vma=False,
    )
```

```python
import functools

import jax
import jax.numpy as jnp
from jax import lax
from jax.experimental import pallas as pl
from jax.experimental.pallas import tpu as pltpu
from jax.sharding import PartitionSpec as P

EPS = 1e-05
MESH = pl.DeviceIdType.MESH


def dp_grid(mesh):
    size = mesh.shape["dp"]
    try:
        zs = {tuple(mesh.devices[i, 0].coords)[2] for i in range(size)}
        nz = len(zs)
    except Exception:
        nz = size // 4
    return size // nz, nz


def head_gather_kernel(ny, nz, nv, split, head_ref, hidden_ref, gain_ref, out_ref, normed_ref,
                       send_sem, recv_sem, local_sem, hsend_sem, hrecv_sem, hlocal_sem, feat_ref):
    dp = lax.axis_index("dp")
    v = lax.axis_index("vocab")
    y = dp // nz
    z = dp % nz
    yr = (y + 1) % ny
    yl = (y + ny - 1) % ny

    def zs(k):
        return (z + k + 8 * nz) % nz

    def ys(k):
        return (y + k + 8 * ny) % ny

    def dev(yy, zz):
        return (yy * nz + zz, v)

    width = head_ref.shape[1]
    parts = 2
    prow = head_ref.shape[0] // parts
    rows, hr = prow, prow // 2
    cols = (pl.ds(0, split), pl.ds(split, width - split))

    barrier = pltpu.get_barrier_semaphore()
    peers = [dev(yr, z), dev(yl, z), dev(y, zs(1)), dev(y, zs(-1))]
    peers += [(dp, (v + k) % nv) for k in range(1, nv)]
    for peer in peers:
        pl.semaphore_signal(barrier, inc=1, device_id=peer, device_id_type=MESH)
    pl.semaphore_wait(barrier, len(peers))

    copies = {}

    def send(key, src, dst, peer):
        c = pltpu.make_async_remote_copy(
            src_ref=src,
            dst_ref=dst,
            send_sem=send_sem.at[len(copies)],
            recv_sem=recv_sem.at[len(copies)],
            device_id=peer,
            device_id_type=MESH,
        )
        copies[key] = c
        c.start()

    def arrived(key):
        copies[key].wait_recv()

    local = pltpu.make_async_copy(head_ref, out_ref.at[y, z], local_sem)
    local.start()

    breadth = hidden_ref.shape[1]
    own_cols = feat_ref.at[:, pl.ds(pl.multiple_of(v * breadth, breadth), breadth)]
    hidden_copies = []
    for k in range(1, nv):
        c = pltpu.make_async_remote_copy(
            src_ref=hidden_ref,
            dst_ref=own_cols,
            send_sem=hsend_sem.at[k - 1],
            recv_sem=hrecv_sem.at[k - 1],
            device_id=(dp, (v + k) % nv),
            device_id_type=MESH,
        )
        c.start()
        hidden_copies.append(c)
    hidden_local = pltpu.make_async_copy(hidden_ref, own_cols, hlocal_sem)
    hidden_local.start()

    plan = []

    def ring_plan(name, n, block, right, left, first_src, needs0):
        steps = n // 2
        for step in range(1, steps + 1):
            for side, peer, sign in (("r", right, -1), ("l", left, 1)):
                key = f"{name}{side}{step}"
                view = block(sign * (step - 1))
                if 2 * step == n:
                    view = view.at[pl.ds(0, hr)] if side == "r" else view.at[pl.ds(hr, rows - hr)]
                    src = view
                elif step == 1 and first_src is not None:
                    src = first_src
                else:
                    src = view
                if step == 1 and 2 * step == n and first_src is not None:
                    src = first_src.at[pl.ds(0, hr)] if side == "r" else first_src.at[pl.ds(hr, rows - hr)]
                needs = list(needs0) if step == 1 else [f"{name}{side}{step - 1}"]
                plan.append((key, src, view, peer, needs))

    right_y, left_y = dev(yr, z), dev(yl, z)
    right_z, left_z = dev(y, zs(1)), dev(y, zs(-1))

    def arrival_keys(name, n, offset):
        steps = n // 2
        if offset == 0:
            return []
        k = abs(offset) if abs(offset) <= steps else n - abs(offset)
        if 2 * k == n:
            return [f"{name}r{k}", f"{name}l{k}"]
        return [f"{name}r{k}"] if offset < 0 else [f"{name}l{k}"]

    y_offsets = [0] + [s * k for k in range(1, ny // 2 + 1) for s in (-1, 1) if not (s == 1 and 2 * k == ny)]
    z_offsets = [0] + [s * k for k in range(1, nz // 2 + 1) for s in (-1, 1) if not (s == 1 and 2 * k == nz)]
    for q in range(parts):
        rq = pl.ds(q * prow, prow)
        ring_plan(f"ay{q}", ny, lambda k: out_ref.at[ys(k), z, rq, cols[0]], right_y, left_y,
                  head_ref.at[rq, cols[0]], [])
        ring_plan(f"bz{q}", nz, lambda k: out_ref.at[y, zs(k), rq, cols[1]], right_z, left_z,
                  head_ref.at[rq, cols[1]], [])
        for dy in y_offsets:
            ring_plan(f"az{q}.{dy + ny}_", nz,
                      lambda k, dy=dy: out_ref.at[ys(dy), zs(k), rq, cols[0]],
                      right_z, left_z, head_ref.at[rq, cols[0]] if dy == 0 else None,
                      arrival_keys(f"ay{q}", ny, dy))
        for dz in z_offsets:
            ring_plan(f"by{q}.{dz + nz}_", ny,
                      lambda k, dz=dz: out_ref.at[ys(k), zs(dz), rq, cols[1]],
                      right_y, left_y, head_ref.at[rq, cols[1]] if dz == 0 else None,
                      arrival_keys(f"bz{q}", nz, dz))

    level = {}
    for key, _, _, _, needs in plan:
        level[key] = 1 + max([level[n] for n in needs], default=-1)
    order = sorted(range(len(plan)), key=lambda i: (level[plan[i][0]], i))
    index = {plan[i][0]: i for i in range(len(plan))}
    waited = set()
    copies = {}
    for i in order:
        key, src, dst, peer, needs = plan[i]
        for n in needs:
            if n not in waited:
                copies[n].wait_recv()
                waited.add(n)
        c = pltpu.make_async_remote_copy(
            src_ref=src,
            dst_ref=dst,
            send_sem=send_sem.at[index[key]],
            recv_sem=recv_sem.at[index[key]],
            device_id=peer,
            device_id_type=MESH,
        )
        c.start()
        copies[key] = c
    hidden_local.wait()
    for c in hidden_copies:
        c.wait_recv()
    tile = 64

    def norm_rows(i, carry):
        r = pl.ds(pl.multiple_of(i * tile, tile), tile)
        wide = feat_ref[r, :].astype(jnp.float32)
        scale = lax.rsqrt(jnp.mean(wide * wide, axis=1, keepdims=True) + EPS)
        normed_ref[r, :] = (wide * scale * gain_ref[...]).astype(normed_ref.dtype)
        return carry

    lax.fori_loop(0, feat_ref.shape[0] // tile, norm_rows, 0)
    for i in order:
        key = plan[i][0]
        if key not in waited:
            copies[key].wait_recv()
            waited.add(key)
    local.wait()
    for c in list(copies.values()) + hidden_copies:
        c.wait_send()


def gather_all(head, hidden, gain, ny, nz, nv):
    rows, width = head.shape
    slots, breadth = hidden.shape
    split = max(128, min(width - 128, int(round(width * 0.384 / 128)) * 128))
    streams = 4 * (ny // 2 + nz // 2 + ny * (nz // 2) + nz * (ny // 2))
    out, normed = pl.pallas_call(
        functools.partial(head_gather_kernel, ny, nz, nv, split),
        out_shape=(
            jax.ShapeDtypeStruct((ny, nz, rows, width), head.dtype),
            jax.ShapeDtypeStruct((slots, nv * breadth), hidden.dtype),
        ),
        in_specs=[pl.BlockSpec(memory_space=pl.ANY)] * 2 + [pl.BlockSpec(memory_space=pltpu.VMEM)],
        out_specs=(pl.BlockSpec(memory_space=pl.ANY), pl.BlockSpec(memory_space=pltpu.VMEM)),
        scratch_shapes=[
            pltpu.SemaphoreType.DMA((streams,)),
            pltpu.SemaphoreType.DMA((streams,)),
            pltpu.SemaphoreType.DMA(()),
            pltpu.SemaphoreType.DMA((nv - 1,)),
            pltpu.SemaphoreType.DMA((nv - 1,)),
            pltpu.SemaphoreType.DMA(()),
            pltpu.VMEM((slots, nv * breadth), hidden.dtype),
        ],
        compiler_params=pltpu.CompilerParams(collective_id=0, has_side_effects=True),
        cost_estimate=pl.CostEstimate(
            flops=0, transcendentals=0, bytes_accessed=2 * ny * nz * rows * width * 2
        ),
    )(head, hidden, gain.astype(jnp.float32).reshape(1, nv * breadth))
    return out.reshape(ny * nz * rows, width), normed


def stats_kernel(n, stats_ref, out_ref, send_sem, recv_sem):
    dp = lax.axis_index("dp")
    v = lax.axis_index("vocab")
    barrier = pltpu.get_barrier_semaphore()
    for k in range(1, n):
        pl.semaphore_signal(barrier, inc=1, device_id=(dp, (v + k) % n), device_id_type=MESH)
    pl.semaphore_wait(barrier, n - 1)
    copies = []
    for k in range(1, n):
        c = pltpu.make_async_remote_copy(
            src_ref=stats_ref,
            dst_ref=out_ref.at[v],
            send_sem=send_sem.at[k - 1],
            recv_sem=recv_sem.at[k - 1],
            device_id=(dp, (v + k) % n),
            device_id_type=MESH,
        )
        c.start()
        copies.append(c)
    out_ref[v] = stats_ref[...]
    for c in copies:
        c.wait_recv()
    for c in copies:
        c.wait_send()


def exchange_stats(stats, n):
    return pl.pallas_call(
        functools.partial(stats_kernel, n),
        out_shape=jax.ShapeDtypeStruct((n,) + stats.shape, stats.dtype),
        in_specs=[pl.BlockSpec(memory_space=pltpu.VMEM)],
        out_specs=pl.BlockSpec(memory_space=pltpu.VMEM),
        scratch_shapes=[
            pltpu.SemaphoreType.DMA((n - 1,)),
            pltpu.SemaphoreType.DMA((n - 1,)),
        ],
        compiler_params=pltpu.CompilerParams(collective_id=1, has_side_effects=True),
    )(stats)


def local(ny, nz, hidden, gain, head, target_ids, seq_lens, seq_owner):
    groups = lax.axis_size("dp")
    slices = lax.axis_size("vocab")
    position = lax.axis_index("dp")
    slice_index = lax.axis_index("vocab")
    slots = hidden.shape[0]
    breadth = head.shape[1]
    owners = jnp.arange(groups, dtype=jnp.int32)
    loads = jnp.sum(jnp.where(seq_owner[:, None] == owners[None, :], seq_lens[:, None], 0), axis=0)
    own_live = jnp.arange(slots, dtype=jnp.int32) < loads[position]
    columns, normed = gather_all(head, hidden, gain, ny, nz, slices)
    logits = jnp.dot(normed, columns, preferred_element_type=jnp.float32)
    top_local = jnp.max(logits, axis=1)
    expo = jnp.exp(logits - top_local[:, None])
    total_local = jnp.sum(expo, axis=1)
    weighted_local = jnp.sum(expo * logits, axis=1)
    local_id = target_ids - slice_index * breadth
    inside = (local_id >= 0) & (local_id < breadth)
    chosen = jnp.take_along_axis(logits, jnp.clip(local_id, 0, breadth - 1)[:, None], axis=1)[:, 0]
    picked_local = jnp.where(inside, chosen, 0.0)
    stats = jnp.stack([top_local, total_local, weighted_local, picked_local])
    every = exchange_stats(stats, slices)
    tops = every[:, 0]
    top = jnp.max(tops, axis=0)
    factor = jnp.exp(tops - top[None, :])
    total = jnp.sum(every[:, 1] * factor, axis=0)
    weighted = jnp.sum(every[:, 2] * factor, axis=0)
    picked = jnp.sum(every[:, 3], axis=0)
    lse = top + jnp.log(total)
    logprob = picked - lse
    entropy = lse - weighted / total
    return (jnp.where(own_live, logprob, 0.0), jnp.where(own_live, entropy, 0.0))


def solution(mesh):
    ny, nz = dp_grid(mesh)
    return jax.shard_map(
        functools.partial(local, ny, nz),
        mesh=mesh,
        in_specs=(P("dp", "vocab"), P(), P("dp", "vocab"), P("dp"), P(), P()),
        out_specs=(P("dp"), P("dp")),
        check_vma=False,
    )
```

```python
import functools

import jax
import jax.numpy as jnp
from jax import lax
from jax.experimental import pallas as pl
from jax.experimental.pallas import tpu as pltpu
from jax.sharding import PartitionSpec as P

EPS = 1e-05
MESH = pl.DeviceIdType.MESH


def dp_grid(mesh):
    size = mesh.shape["dp"]
    try:
        zs = {tuple(mesh.devices[i, 0].coords)[2] for i in range(size)}
        nz = len(zs)
    except Exception:
        nz = size // 4
    return size // nz, nz


def head_gather_kernel(ny, nz, nv, split, head_ref, hidden_ref, gain_ref, out_ref, normed_ref,
                       send_sem, recv_sem, local_sem, hsend_sem, hrecv_sem, hlocal_sem, feat_ref):
    dp = lax.axis_index("dp")
    v = lax.axis_index("vocab")
    y = dp // nz
    z = dp % nz
    yr = (y + 1) % ny
    yl = (y + ny - 1) % ny

    def zs(k):
        return (z + k + 8 * nz) % nz

    def ys(k):
        return (y + k + 8 * ny) % ny

    def dev(yy, zz):
        return (yy * nz + zz, v)

    width = head_ref.shape[1]
    parts = 2
    prow = head_ref.shape[0] // parts
    rows, hr = prow, prow // 2
    cols = (pl.ds(0, split), pl.ds(split, width - split))

    barrier = pltpu.get_barrier_semaphore()
    peers = [dev(yr, z), dev(yl, z), dev(y, zs(1)), dev(y, zs(-1))]
    peers += [(dp, (v + k) % nv) for k in range(1, nv)]
    for peer in peers:
        pl.semaphore_signal(barrier, inc=1, device_id=peer, device_id_type=MESH)
    pl.semaphore_wait(barrier, len(peers))

    copies = {}

    def send(key, src, dst, peer):
        c = pltpu.make_async_remote_copy(
            src_ref=src,
            dst_ref=dst,
            send_sem=send_sem.at[len(copies)],
            recv_sem=recv_sem.at[len(copies)],
            device_id=peer,
            device_id_type=MESH,
        )
        copies[key] = c
        c.start()

    def arrived(key):
        copies[key].wait_recv()

    local = pltpu.make_async_copy(head_ref, out_ref.at[y, z], local_sem)
    local.start()

    breadth = hidden_ref.shape[1]
    own_cols = feat_ref.at[:, pl.ds(pl.multiple_of(v * breadth, breadth), breadth)]

    plan = []

    def ring_plan(name, n, block, right, left, first_src, needs0):
        steps = n // 2
        for step in range(1, steps + 1):
            for side, peer, sign in (("r", right, -1), ("l", left, 1)):
                key = f"{name}{side}{step}"
                view = block(sign * (step - 1))
                if 2 * step == n:
                    view = view.at[pl.ds(0, hr)] if side == "r" else view.at[pl.ds(hr, rows - hr)]
                    src = view
                elif step == 1 and first_src is not None:
                    src = first_src
                else:
                    src = view
                if step == 1 and 2 * step == n and first_src is not None:
                    src = first_src.at[pl.ds(0, hr)] if side == "r" else first_src.at[pl.ds(hr, rows - hr)]
                needs = list(needs0) if step == 1 else [f"{name}{side}{step - 1}"]
                plan.append((key, src, view, peer, needs))

    right_y, left_y = dev(yr, z), dev(yl, z)
    right_z, left_z = dev(y, zs(1)), dev(y, zs(-1))

    def arrival_keys(name, n, offset):
        steps = n // 2
        if offset == 0:
            return []
        k = abs(offset) if abs(offset) <= steps else n - abs(offset)
        if 2 * k == n:
            return [f"{name}r{k}", f"{name}l{k}"]
        return [f"{name}r{k}"] if offset < 0 else [f"{name}l{k}"]

    y_offsets = [0] + [s * k for k in range(1, ny // 2 + 1) for s in (-1, 1) if not (s == 1 and 2 * k == ny)]
    z_offsets = [0] + [s * k for k in range(1, nz // 2 + 1) for s in (-1, 1) if not (s == 1 and 2 * k == nz)]
    for q in range(parts):
        rq = pl.ds(q * prow, prow)
        ring_plan(f"ay{q}", ny, lambda k: out_ref.at[ys(k), z, rq, cols[0]], right_y, left_y,
                  head_ref.at[rq, cols[0]], [])
        ring_plan(f"bz{q}", nz, lambda k: out_ref.at[y, zs(k), rq, cols[1]], right_z, left_z,
                  head_ref.at[rq, cols[1]], [])
        for dy in y_offsets:
            ring_plan(f"az{q}.{dy + ny}_", nz,
                      lambda k, dy=dy: out_ref.at[ys(dy), zs(k), rq, cols[0]],
                      right_z, left_z, head_ref.at[rq, cols[0]] if dy == 0 else None,
                      arrival_keys(f"ay{q}", ny, dy))
        for dz in z_offsets:
            ring_plan(f"by{q}.{dz + nz}_", ny,
                      lambda k, dz=dz: out_ref.at[ys(k), zs(dz), rq, cols[1]],
                      right_y, left_y, head_ref.at[rq, cols[1]] if dz == 0 else None,
                      arrival_keys(f"bz{q}", nz, dz))

    level = {}
    for key, _, _, _, needs in plan:
        level[key] = 1 + max([level[n] for n in needs], default=-1)
    order = sorted(range(len(plan)), key=lambda i: (level[plan[i][0]], i))
    index = {plan[i][0]: i for i in range(len(plan))}
    waited = set()
    copies = {}
    hidden_copies = []
    hidden_local = None
    for i in order:
        key, src, dst, peer, needs = plan[i]
        if hidden_local is None and level[key] >= 1:
            for k in range(1, nv):
                c = pltpu.make_async_remote_copy(
                    src_ref=hidden_ref,
                    dst_ref=own_cols,
                    send_sem=hsend_sem.at[k - 1],
                    recv_sem=hrecv_sem.at[k - 1],
                    device_id=(dp, (v + k) % nv),
                    device_id_type=MESH,
                )
                c.start()
                hidden_copies.append(c)
            hidden_local = pltpu.make_async_copy(hidden_ref, own_cols, hlocal_sem)
            hidden_local.start()
        for n in needs:
            if n not in waited:
                copies[n].wait_recv()
                waited.add(n)
        c = pltpu.make_async_remote_copy(
            src_ref=src,
            dst_ref=dst,
            send_sem=send_sem.at[index[key]],
            recv_sem=recv_sem.at[index[key]],
            device_id=peer,
            device_id_type=MESH,
        )
        c.start()
        copies[key] = c
    hidden_local.wait()
    for c in hidden_copies:
        c.wait_recv()
    tile = 64

    def norm_rows(i, carry):
        r = pl.ds(pl.multiple_of(i * tile, tile), tile)
        wide = feat_ref[r, :].astype(jnp.float32)
        scale = lax.rsqrt(jnp.mean(wide * wide, axis=1, keepdims=True) + EPS)
        normed_ref[r, :] = (wide * scale * gain_ref[...]).astype(normed_ref.dtype)
        return carry

    lax.fori_loop(0, feat_ref.shape[0] // tile, norm_rows, 0)
    for i in order:
        key = plan[i][0]
        if key not in waited:
            copies[key].wait_recv()
            waited.add(key)
    local.wait()
    for c in list(copies.values()) + hidden_copies:
        c.wait_send()


def gather_all(head, hidden, gain, ny, nz, nv):
    rows, width = head.shape
    slots, breadth = hidden.shape
    split = max(128, min(width - 128, int(round(width * 0.384 / 128)) * 128))
    streams = 4 * (ny // 2 + nz // 2 + ny * (nz // 2) + nz * (ny // 2))
    out, normed = pl.pallas_call(
        functools.partial(head_gather_kernel, ny, nz, nv, split),
        out_shape=(
            jax.ShapeDtypeStruct((ny, nz, rows, width), head.dtype),
            jax.ShapeDtypeStruct((slots, nv * breadth), hidden.dtype),
        ),
        in_specs=[pl.BlockSpec(memory_space=pl.ANY)] * 2 + [pl.BlockSpec(memory_space=pltpu.VMEM)],
        out_specs=(pl.BlockSpec(memory_space=pl.ANY), pl.BlockSpec(memory_space=pltpu.VMEM)),
        scratch_shapes=[
            pltpu.SemaphoreType.DMA((streams,)),
            pltpu.SemaphoreType.DMA((streams,)),
            pltpu.SemaphoreType.DMA(()),
            pltpu.SemaphoreType.DMA((nv - 1,)),
            pltpu.SemaphoreType.DMA((nv - 1,)),
            pltpu.SemaphoreType.DMA(()),
            pltpu.VMEM((slots, nv * breadth), hidden.dtype),
        ],
        compiler_params=pltpu.CompilerParams(collective_id=0, has_side_effects=True),
        cost_estimate=pl.CostEstimate(
            flops=0, transcendentals=0, bytes_accessed=2 * ny * nz * rows * width * 2
        ),
    )(head, hidden, gain.astype(jnp.float32).reshape(1, nv * breadth))
    return out.reshape(ny * nz * rows, width), normed


def stats_kernel(n, stats_ref, out_ref, send_sem, recv_sem):
    dp = lax.axis_index("dp")
    v = lax.axis_index("vocab")
    barrier = pltpu.get_barrier_semaphore()
    for k in range(1, n):
        pl.semaphore_signal(barrier, inc=1, device_id=(dp, (v + k) % n), device_id_type=MESH)
    pl.semaphore_wait(barrier, n - 1)
    copies = []
    for k in range(1, n):
        c = pltpu.make_async_remote_copy(
            src_ref=stats_ref,
            dst_ref=out_ref.at[v],
            send_sem=send_sem.at[k - 1],
            recv_sem=recv_sem.at[k - 1],
            device_id=(dp, (v + k) % n),
            device_id_type=MESH,
        )
        c.start()
        copies.append(c)
    out_ref[v] = stats_ref[...]
    for c in copies:
        c.wait_recv()
    for c in copies:
        c.wait_send()


def exchange_stats(stats, n):
    return pl.pallas_call(
        functools.partial(stats_kernel, n),
        out_shape=jax.ShapeDtypeStruct((n,) + stats.shape, stats.dtype),
        in_specs=[pl.BlockSpec(memory_space=pltpu.VMEM)],
        out_specs=pl.BlockSpec(memory_space=pltpu.VMEM),
        scratch_shapes=[
            pltpu.SemaphoreType.DMA((n - 1,)),
            pltpu.SemaphoreType.DMA((n - 1,)),
        ],
        compiler_params=pltpu.CompilerParams(collective_id=1, has_side_effects=True),
    )(stats)


def local(ny, nz, hidden, gain, head, target_ids, seq_lens, seq_owner):
    groups = lax.axis_size("dp")
    slices = lax.axis_size("vocab")
    position = lax.axis_index("dp")
    slice_index = lax.axis_index("vocab")
    slots = hidden.shape[0]
    breadth = head.shape[1]
    owners = jnp.arange(groups, dtype=jnp.int32)
    loads = jnp.sum(jnp.where(seq_owner[:, None] == owners[None, :], seq_lens[:, None], 0), axis=0)
    own_live = jnp.arange(slots, dtype=jnp.int32) < loads[position]
    columns, normed = gather_all(head, hidden, gain, ny, nz, slices)
    logits = jnp.dot(normed, columns, preferred_element_type=jnp.float32)
    top_local = jnp.max(logits, axis=1)
    expo = jnp.exp(logits - top_local[:, None])
    total_local = jnp.sum(expo, axis=1)
    weighted_local = jnp.sum(expo * logits, axis=1)
    local_id = target_ids - slice_index * breadth
    ids = lax.broadcasted_iota(jnp.int32, logits.shape, 1)
    picked_local = jnp.sum(jnp.where(ids == local_id[:, None], logits, 0.0), axis=1)
    stats = jnp.stack([top_local, total_local, weighted_local, picked_local])
    every = exchange_stats(stats, slices)
    tops = every[:, 0]
    top = jnp.max(tops, axis=0)
    factor = jnp.exp(tops - top[None, :])
    total = jnp.sum(every[:, 1] * factor, axis=0)
    weighted = jnp.sum(every[:, 2] * factor, axis=0)
    picked = jnp.sum(every[:, 3], axis=0)
    lse = top + jnp.log(total)
    logprob = picked - lse
    entropy = lse - weighted / total
    return (jnp.where(own_live, logprob, 0.0), jnp.where(own_live, entropy, 0.0))


def solution(mesh):
    ny, nz = dp_grid(mesh)
    return jax.shard_map(
        functools.partial(local, ny, nz),
        mesh=mesh,
        in_specs=(P("dp", "vocab"), P(), P("dp", "vocab"), P("dp"), P(), P()),
        out_specs=(P("dp"), P("dp")),
        check_vma=False,
    )
```

```python
import functools

import jax
import jax.numpy as jnp
from jax import lax
from jax.experimental import pallas as pl
from jax.experimental.pallas import tpu as pltpu
from jax.sharding import PartitionSpec as P

EPS = 1e-05
MESH = pl.DeviceIdType.MESH


def dp_grid(mesh):
    size = mesh.shape["dp"]
    try:
        zs = {tuple(mesh.devices[i, 0].coords)[2] for i in range(size)}
        nz = len(zs)
    except Exception:
        nz = size // 4
    return size // nz, nz


def head_gather_kernel(ny, nz, nv, split, head_ref, hidden_ref, gain_ref, out_ref, normed_ref,
                       send_sem, recv_sem, local_sem, hsend_sem, hrecv_sem, hlocal_sem, feat_ref):
    dp = lax.axis_index("dp")
    v = lax.axis_index("vocab")
    y = dp // nz
    z = dp % nz
    yr = (y + 1) % ny
    yl = (y + ny - 1) % ny

    def zs(k):
        return (z + k + 8 * nz) % nz

    def ys(k):
        return (y + k + 8 * ny) % ny

    def dev(yy, zz):
        return (yy * nz + zz, v)

    width = head_ref.shape[1]
    parts = 2
    prow = head_ref.shape[0] // parts
    rows, hr = prow, prow // 2
    cols = (pl.ds(0, split), pl.ds(split, width - split))

    barrier = pltpu.get_barrier_semaphore()
    peers = [dev(yr, z), dev(yl, z), dev(y, zs(1)), dev(y, zs(-1))]
    peers += [(dp, (v + k) % nv) for k in range(1, nv)]
    for peer in peers:
        pl.semaphore_signal(barrier, inc=1, device_id=peer, device_id_type=MESH)
    pl.semaphore_wait(barrier, len(peers))

    copies = {}

    def send(key, src, dst, peer):
        c = pltpu.make_async_remote_copy(
            src_ref=src,
            dst_ref=dst,
            send_sem=send_sem.at[len(copies)],
            recv_sem=recv_sem.at[len(copies)],
            device_id=peer,
            device_id_type=MESH,
        )
        copies[key] = c
        c.start()

    def arrived(key):
        copies[key].wait_recv()

    local = pltpu.make_async_copy(head_ref, out_ref.at[y, z], local_sem)
    local.start()

    breadth = hidden_ref.shape[1]
    own_cols = feat_ref.at[:, pl.ds(pl.multiple_of(v * breadth, breadth), breadth)]
    hidden_copies = []
    for k in range(1, nv):
        c = pltpu.make_async_remote_copy(
            src_ref=hidden_ref,
            dst_ref=own_cols,
            send_sem=hsend_sem.at[k - 1],
            recv_sem=hrecv_sem.at[k - 1],
            device_id=(dp, (v + k) % nv),
            device_id_type=MESH,
        )
        c.start()
        hidden_copies.append(c)
    hidden_local = pltpu.make_async_copy(hidden_ref, own_cols, hlocal_sem)
    hidden_local.start()

    plan = []

    def ring_plan(name, n, block, right, left, first_src, needs0):
        steps = n // 2
        for step in range(1, steps + 1):
            for side, peer, sign in (("r", right, -1), ("l", left, 1)):
                key = f"{name}{side}{step}"
                view = block(sign * (step - 1))
                if 2 * step == n:
                    view = view.at[pl.ds(0, hr)] if side == "r" else view.at[pl.ds(hr, rows - hr)]
                    src = view
                elif step == 1 and first_src is not None:
                    src = first_src
                else:
                    src = view
                if step == 1 and 2 * step == n and first_src is not None:
                    src = first_src.at[pl.ds(0, hr)] if side == "r" else first_src.at[pl.ds(hr, rows - hr)]
                needs = list(needs0) if step == 1 else [f"{name}{side}{step - 1}"]
                plan.append((key, src, view, peer, needs))

    right_y, left_y = dev(yr, z), dev(yl, z)
    right_z, left_z = dev(y, zs(1)), dev(y, zs(-1))

    def arrival_keys(name, n, offset):
        steps = n // 2
        if offset == 0:
            return []
        k = abs(offset) if abs(offset) <= steps else n - abs(offset)
        if 2 * k == n:
            return [f"{name}r{k}", f"{name}l{k}"]
        return [f"{name}r{k}"] if offset < 0 else [f"{name}l{k}"]

    y_offsets = [0] + [s * k for k in range(1, ny // 2 + 1) for s in (-1, 1) if not (s == 1 and 2 * k == ny)]
    z_offsets = [0] + [s * k for k in range(1, nz // 2 + 1) for s in (-1, 1) if not (s == 1 and 2 * k == nz)]
    for q in range(parts):
        rq = pl.ds(q * prow, prow)
        ring_plan(f"ay{q}", ny, lambda k: out_ref.at[ys(k), z, rq, cols[0]], right_y, left_y,
                  head_ref.at[rq, cols[0]], [])
        ring_plan(f"bz{q}", nz, lambda k: out_ref.at[y, zs(k), rq, cols[1]], right_z, left_z,
                  head_ref.at[rq, cols[1]], [])
        for dy in y_offsets:
            ring_plan(f"az{q}.{dy + ny}_", nz,
                      lambda k, dy=dy: out_ref.at[ys(dy), zs(k), rq, cols[0]],
                      right_z, left_z, head_ref.at[rq, cols[0]] if dy == 0 else None,
                      arrival_keys(f"ay{q}", ny, dy))
        for dz in z_offsets:
            ring_plan(f"by{q}.{dz + nz}_", ny,
                      lambda k, dz=dz: out_ref.at[ys(k), zs(dz), rq, cols[1]],
                      right_y, left_y, head_ref.at[rq, cols[1]] if dz == 0 else None,
                      arrival_keys(f"bz{q}", nz, dz))

    level = {}
    for key, _, _, _, needs in plan:
        level[key] = 1 + max([level[n] for n in needs], default=-1)
    order = sorted(range(len(plan)), key=lambda i: (level[plan[i][0]], i))
    index = {plan[i][0]: i for i in range(len(plan))}
    waited = set()
    copies = {}
    for i in order:
        key, src, dst, peer, needs = plan[i]
        for n in needs:
            if n not in waited:
                copies[n].wait_recv()
                waited.add(n)
        c = pltpu.make_async_remote_copy(
            src_ref=src,
            dst_ref=dst,
            send_sem=send_sem.at[index[key]],
            recv_sem=recv_sem.at[index[key]],
            device_id=peer,
            device_id_type=MESH,
        )
        c.start()
        copies[key] = c
    hidden_local.wait()
    for c in hidden_copies:
        c.wait_recv()
    tile = 64

    def norm_rows(i, carry):
        r = pl.ds(pl.multiple_of(i * tile, tile), tile)
        wide = feat_ref[r, :].astype(jnp.float32)
        scale = lax.rsqrt(jnp.mean(wide * wide, axis=1, keepdims=True) + EPS)
        normed_ref[r, :] = (wide * scale * gain_ref[...]).astype(normed_ref.dtype)
        return carry

    lax.fori_loop(0, feat_ref.shape[0] // tile, norm_rows, 0)
    for i in order:
        key = plan[i][0]
        if key not in waited:
            copies[key].wait_recv()
            waited.add(key)
    local.wait()
    for c in list(copies.values()) + hidden_copies:
        c.wait_send()


def gather_all(head, hidden, gain, ny, nz, nv):
    rows, width = head.shape
    slots, breadth = hidden.shape
    split = max(128, min(width - 128, int(round(width * 0.45 / 128)) * 128))
    streams = 4 * (ny // 2 + nz // 2 + ny * (nz // 2) + nz * (ny // 2))
    out, normed = pl.pallas_call(
        functools.partial(head_gather_kernel, ny, nz, nv, split),
        out_shape=(
            jax.ShapeDtypeStruct((ny, nz, rows, width), head.dtype),
            jax.ShapeDtypeStruct((slots, nv * breadth), hidden.dtype),
        ),
        in_specs=[pl.BlockSpec(memory_space=pl.ANY)] * 2 + [pl.BlockSpec(memory_space=pltpu.VMEM)],
        out_specs=(pl.BlockSpec(memory_space=pl.ANY), pl.BlockSpec(memory_space=pltpu.VMEM)),
        scratch_shapes=[
            pltpu.SemaphoreType.DMA((streams,)),
            pltpu.SemaphoreType.DMA((streams,)),
            pltpu.SemaphoreType.DMA(()),
            pltpu.SemaphoreType.DMA((nv - 1,)),
            pltpu.SemaphoreType.DMA((nv - 1,)),
            pltpu.SemaphoreType.DMA(()),
            pltpu.VMEM((slots, nv * breadth), hidden.dtype),
        ],
        compiler_params=pltpu.CompilerParams(collective_id=0, has_side_effects=True),
        cost_estimate=pl.CostEstimate(
            flops=0, transcendentals=0, bytes_accessed=2 * ny * nz * rows * width * 2
        ),
    )(head, hidden, gain.astype(jnp.float32).reshape(1, nv * breadth))
    return out.reshape(ny * nz * rows, width), normed


def stats_kernel(n, stats_ref, out_ref, send_sem, recv_sem):
    dp = lax.axis_index("dp")
    v = lax.axis_index("vocab")
    barrier = pltpu.get_barrier_semaphore()
    for k in range(1, n):
        pl.semaphore_signal(barrier, inc=1, device_id=(dp, (v + k) % n), device_id_type=MESH)
    pl.semaphore_wait(barrier, n - 1)
    copies = []
    for k in range(1, n):
        c = pltpu.make_async_remote_copy(
            src_ref=stats_ref,
            dst_ref=out_ref.at[v],
            send_sem=send_sem.at[k - 1],
            recv_sem=recv_sem.at[k - 1],
            device_id=(dp, (v + k) % n),
            device_id_type=MESH,
        )
        c.start()
        copies.append(c)
    out_ref[v] = stats_ref[...]
    for c in copies:
        c.wait_recv()
    for c in copies:
        c.wait_send()


def exchange_stats(stats, n):
    return pl.pallas_call(
        functools.partial(stats_kernel, n),
        out_shape=jax.ShapeDtypeStruct((n,) + stats.shape, stats.dtype),
        in_specs=[pl.BlockSpec(memory_space=pltpu.VMEM)],
        out_specs=pl.BlockSpec(memory_space=pltpu.VMEM),
        scratch_shapes=[
            pltpu.SemaphoreType.DMA((n - 1,)),
            pltpu.SemaphoreType.DMA((n - 1,)),
        ],
        compiler_params=pltpu.CompilerParams(collective_id=1, has_side_effects=True),
    )(stats)


def local(ny, nz, hidden, gain, head, target_ids, seq_lens, seq_owner):
    groups = lax.axis_size("dp")
    slices = lax.axis_size("vocab")
    position = lax.axis_index("dp")
    slice_index = lax.axis_index("vocab")
    slots = hidden.shape[0]
    breadth = head.shape[1]
    owners = jnp.arange(groups, dtype=jnp.int32)
    loads = jnp.sum(jnp.where(seq_owner[:, None] == owners[None, :], seq_lens[:, None], 0), axis=0)
    own_live = jnp.arange(slots, dtype=jnp.int32) < loads[position]
    columns, normed = gather_all(head, hidden, gain, ny, nz, slices)
    logits = jnp.dot(normed, columns, preferred_element_type=jnp.float32)
    top_local = jnp.max(logits, axis=1)
    expo = jnp.exp(logits - top_local[:, None])
    total_local = jnp.sum(expo, axis=1)
    weighted_local = jnp.sum(expo * logits, axis=1)
    local_id = target_ids - slice_index * breadth
    ids = lax.broadcasted_iota(jnp.int32, logits.shape, 1)
    picked_local = jnp.sum(jnp.where(ids == local_id[:, None], logits, 0.0), axis=1)
    stats = jnp.stack([top_local, total_local, weighted_local, picked_local])
    every = exchange_stats(stats, slices)
    tops = every[:, 0]
    top = jnp.max(tops, axis=0)
    factor = jnp.exp(tops - top[None, :])
    total = jnp.sum(every[:, 1] * factor, axis=0)
    weighted = jnp.sum(every[:, 2] * factor, axis=0)
    picked = jnp.sum(every[:, 3], axis=0)
    lse = top + jnp.log(total)
    logprob = picked - lse
    entropy = lse - weighted / total
    return (jnp.where(own_live, logprob, 0.0), jnp.where(own_live, entropy, 0.0))


def solution(mesh):
    ny, nz = dp_grid(mesh)
    return jax.shard_map(
        functools.partial(local, ny, nz),
        mesh=mesh,
        in_specs=(P("dp", "vocab"), P(), P("dp", "vocab"), P("dp"), P(), P()),
        out_specs=(P("dp"), P("dp")),
        check_vma=False,
    )
```

```python
import functools

import jax
import jax.numpy as jnp
from jax import lax
from jax.experimental import pallas as pl
from jax.experimental.pallas import tpu as pltpu
from jax.sharding import PartitionSpec as P

EPS = 1e-05
MESH = pl.DeviceIdType.MESH


def dp_grid(mesh):
    size = mesh.shape["dp"]
    try:
        zs = {tuple(mesh.devices[i, 0].coords)[2] for i in range(size)}
        nz = len(zs)
    except Exception:
        nz = size // 4
    return size // nz, nz


def head_gather_kernel(ny, nz, nv, split, head_ref, hidden_ref, gain_ref, out_ref, normed_ref,
                       send_sem, recv_sem, local_sem, hsend_sem, hrecv_sem, hlocal_sem, feat_ref):
    dp = lax.axis_index("dp")
    v = lax.axis_index("vocab")
    y = dp // nz
    z = dp % nz
    yr = (y + 1) % ny
    yl = (y + ny - 1) % ny

    def zs(k):
        return (z + k + 8 * nz) % nz

    def ys(k):
        return (y + k + 8 * ny) % ny

    def dev(yy, zz):
        return (yy * nz + zz, v)

    width = head_ref.shape[1]
    parts = 2
    prow = head_ref.shape[0] // parts
    rows, hr = prow, prow // 2
    cols = (pl.ds(0, split), pl.ds(split, width - split))

    barrier = pltpu.get_barrier_semaphore()
    peers = [dev(yr, z), dev(yl, z), dev(y, zs(1)), dev(y, zs(-1))]
    peers += [(dp, (v + k) % nv) for k in range(1, nv)]
    for peer in peers:
        pl.semaphore_signal(barrier, inc=1, device_id=peer, device_id_type=MESH)
    pl.semaphore_wait(barrier, len(peers))

    copies = {}

    def send(key, src, dst, peer):
        c = pltpu.make_async_remote_copy(
            src_ref=src,
            dst_ref=dst,
            send_sem=send_sem.at[len(copies)],
            recv_sem=recv_sem.at[len(copies)],
            device_id=peer,
            device_id_type=MESH,
        )
        copies[key] = c
        c.start()

    def arrived(key):
        copies[key].wait_recv()

    local = pltpu.make_async_copy(head_ref, out_ref.at[y, z], local_sem)
    local.start()

    breadth = hidden_ref.shape[1]
    own_cols = feat_ref.at[:, pl.ds(pl.multiple_of(v * breadth, breadth), breadth)]
    hidden_copies = []
    for k in range(1, nv):
        c = pltpu.make_async_remote_copy(
            src_ref=hidden_ref,
            dst_ref=own_cols,
            send_sem=hsend_sem.at[k - 1],
            recv_sem=hrecv_sem.at[k - 1],
            device_id=(dp, (v + k) % nv),
            device_id_type=MESH,
        )
        c.start()
        hidden_copies.append(c)
    hidden_local = pltpu.make_async_copy(hidden_ref, own_cols, hlocal_sem)
    hidden_local.start()

    plan = []

    def ring_plan(name, n, block, right, left, first_src, needs0):
        steps = n // 2
        for step in range(1, steps + 1):
            for side, peer, sign in (("r", right, -1), ("l", left, 1)):
                key = f"{name}{side}{step}"
                view = block(sign * (step - 1))
                if 2 * step == n:
                    view = view.at[pl.ds(0, hr)] if side == "r" else view.at[pl.ds(hr, rows - hr)]
                    src = view
                elif step == 1 and first_src is not None:
                    src = first_src
                else:
                    src = view
                if step == 1 and 2 * step == n and first_src is not None:
                    src = first_src.at[pl.ds(0, hr)] if side == "r" else first_src.at[pl.ds(hr, rows - hr)]
                needs = list(needs0) if step == 1 else [f"{name}{side}{step - 1}"]
                plan.append((key, src, view, peer, needs))

    right_y, left_y = dev(yr, z), dev(yl, z)
    right_z, left_z = dev(y, zs(1)), dev(y, zs(-1))

    def arrival_keys(name, n, offset):
        steps = n // 2
        if offset == 0:
            return []
        k = abs(offset) if abs(offset) <= steps else n - abs(offset)
        if 2 * k == n:
            return [f"{name}r{k}", f"{name}l{k}"]
        return [f"{name}r{k}"] if offset < 0 else [f"{name}l{k}"]

    y_offsets = [0] + [s * k for k in range(1, ny // 2 + 1) for s in (-1, 1) if not (s == 1 and 2 * k == ny)]
    z_offsets = [0] + [s * k for k in range(1, nz // 2 + 1) for s in (-1, 1) if not (s == 1 and 2 * k == nz)]
    for q in range(parts):
        rq = pl.ds(q * prow, prow)
        ring_plan(f"ay{q}", ny, lambda k: out_ref.at[ys(k), z, rq, cols[0]], right_y, left_y,
                  head_ref.at[rq, cols[0]], [])
        ring_plan(f"bz{q}", nz, lambda k: out_ref.at[y, zs(k), rq, cols[1]], right_z, left_z,
                  head_ref.at[rq, cols[1]], [])
        for dy in y_offsets:
            ring_plan(f"az{q}.{dy + ny}_", nz,
                      lambda k, dy=dy: out_ref.at[ys(dy), zs(k), rq, cols[0]],
                      right_z, left_z, head_ref.at[rq, cols[0]] if dy == 0 else None,
                      arrival_keys(f"ay{q}", ny, dy))
        for dz in z_offsets:
            ring_plan(f"by{q}.{dz + nz}_", ny,
                      lambda k, dz=dz: out_ref.at[ys(k), zs(dz), rq, cols[1]],
                      right_y, left_y, head_ref.at[rq, cols[1]] if dz == 0 else None,
                      arrival_keys(f"bz{q}", nz, dz))

    level = {}
    for key, _, _, _, needs in plan:
        level[key] = 1 + max([level[n] for n in needs], default=-1)
    tail = {key: 0 for key, _, _, _, _ in plan}
    for key, _, _, _, needs in reversed(plan):
        for n in needs:
            tail[n] = max(tail[n], tail[key] + 1)
    order = sorted(range(len(plan)), key=lambda i: (level[plan[i][0]], -tail[plan[i][0]], i))
    index = {plan[i][0]: i for i in range(len(plan))}
    waited = set()
    copies = {}
    for i in order:
        key, src, dst, peer, needs = plan[i]
        for n in needs:
            if n not in waited:
                copies[n].wait_recv()
                waited.add(n)
        c = pltpu.make_async_remote_copy(
            src_ref=src,
            dst_ref=dst,
            send_sem=send_sem.at[index[key]],
            recv_sem=recv_sem.at[index[key]],
            device_id=peer,
            device_id_type=MESH,
        )
        c.start()
        copies[key] = c
    hidden_local.wait()
    for c in hidden_copies:
        c.wait_recv()
    tile = 64

    def norm_rows(i, carry):
        r = pl.ds(pl.multiple_of(i * tile, tile), tile)
        wide = feat_ref[r, :].astype(jnp.float32)
        scale = lax.rsqrt(jnp.mean(wide * wide, axis=1, keepdims=True) + EPS)
        normed_ref[r, :] = (wide * scale * gain_ref[...]).astype(normed_ref.dtype)
        return carry

    lax.fori_loop(0, feat_ref.shape[0] // tile, norm_rows, 0)
    for i in order:
        key = plan[i][0]
        if key not in waited:
            copies[key].wait_recv()
            waited.add(key)
    local.wait()
    for c in list(copies.values()) + hidden_copies:
        c.wait_send()


def gather_all(head, hidden, gain, ny, nz, nv):
    rows, width = head.shape
    slots, breadth = hidden.shape
    split = max(128, min(width - 128, int(round(width * 0.384 / 128)) * 128))
    streams = 4 * (ny // 2 + nz // 2 + ny * (nz // 2) + nz * (ny // 2))
    out, normed = pl.pallas_call(
        functools.partial(head_gather_kernel, ny, nz, nv, split),
        out_shape=(
            jax.ShapeDtypeStruct((ny, nz, rows, width), head.dtype),
            jax.ShapeDtypeStruct((slots, nv * breadth), hidden.dtype),
        ),
        in_specs=[pl.BlockSpec(memory_space=pl.ANY)] * 2 + [pl.BlockSpec(memory_space=pltpu.VMEM)],
        out_specs=(pl.BlockSpec(memory_space=pl.ANY), pl.BlockSpec(memory_space=pltpu.VMEM)),
        scratch_shapes=[
            pltpu.SemaphoreType.DMA((streams,)),
            pltpu.SemaphoreType.DMA((streams,)),
            pltpu.SemaphoreType.DMA(()),
            pltpu.SemaphoreType.DMA((nv - 1,)),
            pltpu.SemaphoreType.DMA((nv - 1,)),
            pltpu.SemaphoreType.DMA(()),
            pltpu.VMEM((slots, nv * breadth), hidden.dtype),
        ],
        compiler_params=pltpu.CompilerParams(collective_id=0, has_side_effects=True),
        cost_estimate=pl.CostEstimate(
            flops=0, transcendentals=0, bytes_accessed=2 * ny * nz * rows * width * 2
        ),
    )(head, hidden, gain.astype(jnp.float32).reshape(1, nv * breadth))
    return out.reshape(ny * nz * rows, width), normed


def stats_kernel(n, stats_ref, out_ref, send_sem, recv_sem):
    dp = lax.axis_index("dp")
    v = lax.axis_index("vocab")
    barrier = pltpu.get_barrier_semaphore()
    for k in range(1, n):
        pl.semaphore_signal(barrier, inc=1, device_id=(dp, (v + k) % n), device_id_type=MESH)
    pl.semaphore_wait(barrier, n - 1)
    copies = []
    for k in range(1, n):
        c = pltpu.make_async_remote_copy(
            src_ref=stats_ref,
            dst_ref=out_ref.at[v],
            send_sem=send_sem.at[k - 1],
            recv_sem=recv_sem.at[k - 1],
            device_id=(dp, (v + k) % n),
            device_id_type=MESH,
        )
        c.start()
        copies.append(c)
    out_ref[v] = stats_ref[...]
    for c in copies:
        c.wait_recv()
    for c in copies:
        c.wait_send()


def exchange_stats(stats, n):
    return pl.pallas_call(
        functools.partial(stats_kernel, n),
        out_shape=jax.ShapeDtypeStruct((n,) + stats.shape, stats.dtype),
        in_specs=[pl.BlockSpec(memory_space=pltpu.VMEM)],
        out_specs=pl.BlockSpec(memory_space=pltpu.VMEM),
        scratch_shapes=[
            pltpu.SemaphoreType.DMA((n - 1,)),
            pltpu.SemaphoreType.DMA((n - 1,)),
        ],
        compiler_params=pltpu.CompilerParams(collective_id=1, has_side_effects=True),
    )(stats)


def local(ny, nz, hidden, gain, head, target_ids, seq_lens, seq_owner):
    groups = lax.axis_size("dp")
    slices = lax.axis_size("vocab")
    position = lax.axis_index("dp")
    slice_index = lax.axis_index("vocab")
    slots = hidden.shape[0]
    breadth = head.shape[1]
    owners = jnp.arange(groups, dtype=jnp.int32)
    loads = jnp.sum(jnp.where(seq_owner[:, None] == owners[None, :], seq_lens[:, None], 0), axis=0)
    own_live = jnp.arange(slots, dtype=jnp.int32) < loads[position]
    columns, normed = gather_all(head, hidden, gain, ny, nz, slices)
    logits = jnp.dot(normed, columns, preferred_element_type=jnp.float32)
    top_local = jnp.max(logits, axis=1)
    expo = jnp.exp(logits - top_local[:, None])
    total_local = jnp.sum(expo, axis=1)
    weighted_local = jnp.sum(expo * logits, axis=1)
    local_id = target_ids - slice_index * breadth
    ids = lax.broadcasted_iota(jnp.int32, logits.shape, 1)
    picked_local = jnp.sum(jnp.where(ids == local_id[:, None], logits, 0.0), axis=1)
    stats = jnp.stack([top_local, total_local, weighted_local, picked_local])
    every = exchange_stats(stats, slices)
    tops = every[:, 0]
    top = jnp.max(tops, axis=0)
    factor = jnp.exp(tops - top[None, :])
    total = jnp.sum(every[:, 1] * factor, axis=0)
    weighted = jnp.sum(every[:, 2] * factor, axis=0)
    picked = jnp.sum(every[:, 3], axis=0)
    lse = top + jnp.log(total)
    logprob = picked - lse
    entropy = lse - weighted / total
    return (jnp.where(own_live, logprob, 0.0), jnp.where(own_live, entropy, 0.0))


def solution(mesh):
    ny, nz = dp_grid(mesh)
    return jax.shard_map(
        functools.partial(local, ny, nz),
        mesh=mesh,
        in_specs=(P("dp", "vocab"), P(), P("dp", "vocab"), P("dp"), P(), P()),
        out_specs=(P("dp"), P("dp")),
        check_vma=False,
    )
```

```python
import functools

import jax
import jax.numpy as jnp
from jax import lax
from jax.experimental import pallas as pl
from jax.experimental.pallas import tpu as pltpu
from jax.sharding import PartitionSpec as P

EPS = 1e-05
MESH = pl.DeviceIdType.MESH


def dp_grid(mesh):
    size = mesh.shape["dp"]
    try:
        zs = {tuple(mesh.devices[i, 0].coords)[2] for i in range(size)}
        nz = len(zs)
    except Exception:
        nz = size // 4
    return size // nz, nz


def head_gather_kernel(ny, nz, nv, split, head_ref, hidden_ref, gain_ref, out_ref, normed_ref,
                       send_sem, recv_sem, local_sem, hsend_sem, hrecv_sem, hlocal_sem, feat_ref):
    dp = lax.axis_index("dp")
    v = lax.axis_index("vocab")
    y = dp // nz
    z = dp % nz
    yr = (y + 1) % ny
    yl = (y + ny - 1) % ny

    def zs(k):
        return (z + k + 8 * nz) % nz

    def ys(k):
        return (y + k + 8 * ny) % ny

    def dev(yy, zz):
        return (yy * nz + zz, v)

    width = head_ref.shape[1]
    parts = 2
    prow = head_ref.shape[0] // parts
    rows, hr = prow, prow // 2
    cols = (pl.ds(0, split), pl.ds(split, width - split))

    barrier = pltpu.get_barrier_semaphore()
    peers = [dev(yr, z), dev(yl, z), dev(y, zs(1)), dev(y, zs(-1))]
    peers += [(dp, (v + k) % nv) for k in range(1, nv)]
    for peer in peers:
        pl.semaphore_signal(barrier, inc=1, device_id=peer, device_id_type=MESH)
    pl.semaphore_wait(barrier, len(peers))

    copies = {}

    def send(key, src, dst, peer):
        c = pltpu.make_async_remote_copy(
            src_ref=src,
            dst_ref=dst,
            send_sem=send_sem.at[len(copies)],
            recv_sem=recv_sem.at[len(copies)],
            device_id=peer,
            device_id_type=MESH,
        )
        copies[key] = c
        c.start()

    def arrived(key):
        copies[key].wait_recv()

    local = pltpu.make_async_copy(head_ref, out_ref.at[y, z], local_sem)
    local.start()

    breadth = hidden_ref.shape[1]
    own_cols = feat_ref.at[:, pl.ds(pl.multiple_of(v * breadth, breadth), breadth)]
    hidden_copies = []
    for k in range(1, nv):
        c = pltpu.make_async_remote_copy(
            src_ref=hidden_ref,
            dst_ref=own_cols,
            send_sem=hsend_sem.at[k - 1],
            recv_sem=hrecv_sem.at[k - 1],
            device_id=(dp, (v + k) % nv),
            device_id_type=MESH,
        )
        c.start()
        hidden_copies.append(c)
    hidden_local = pltpu.make_async_copy(hidden_ref, own_cols, hlocal_sem)
    hidden_local.start()

    plan = []

    def ring_plan(name, n, block, right, left, first_src, needs0):
        steps = n // 2
        for step in range(1, steps + 1):
            for side, peer, sign in (("r", right, -1), ("l", left, 1)):
                key = f"{name}{side}{step}"
                view = block(sign * (step - 1))
                if 2 * step == n:
                    view = view.at[pl.ds(0, hr)] if side == "r" else view.at[pl.ds(hr, rows - hr)]
                    src = view
                elif step == 1 and first_src is not None:
                    src = first_src
                else:
                    src = view
                if step == 1 and 2 * step == n and first_src is not None:
                    src = first_src.at[pl.ds(0, hr)] if side == "r" else first_src.at[pl.ds(hr, rows - hr)]
                needs = list(needs0) if step == 1 else [f"{name}{side}{step - 1}"]
                plan.append((key, src, view, peer, needs))

    right_y, left_y = dev(yr, z), dev(yl, z)
    right_z, left_z = dev(y, zs(1)), dev(y, zs(-1))

    def arrival_keys(name, n, offset):
        steps = n // 2
        if offset == 0:
            return []
        k = abs(offset) if abs(offset) <= steps else n - abs(offset)
        if 2 * k == n:
            return [f"{name}r{k}", f"{name}l{k}"]
        return [f"{name}r{k}"] if offset < 0 else [f"{name}l{k}"]

    y_offsets = [0] + [s * k for k in range(1, ny // 2 + 1) for s in (-1, 1) if not (s == 1 and 2 * k == ny)]
    z_offsets = [0] + [s * k for k in range(1, nz // 2 + 1) for s in (-1, 1) if not (s == 1 and 2 * k == nz)]
    for q in range(parts):
        rq = pl.ds(q * prow, prow)
        ring_plan(f"ay{q}", ny, lambda k: out_ref.at[ys(k), z, rq, cols[0]], right_y, left_y,
                  head_ref.at[rq, cols[0]], [])
        ring_plan(f"bz{q}", nz, lambda k: out_ref.at[y, zs(k), rq, cols[1]], right_z, left_z,
                  head_ref.at[rq, cols[1]], [])
        for dy in y_offsets:
            ring_plan(f"az{q}.{dy + ny}_", nz,
                      lambda k, dy=dy: out_ref.at[ys(dy), zs(k), rq, cols[0]],
                      right_z, left_z, head_ref.at[rq, cols[0]] if dy == 0 else None,
                      arrival_keys(f"ay{q}", ny, dy))
        for dz in z_offsets:
            ring_plan(f"by{q}.{dz + nz}_", ny,
                      lambda k, dz=dz: out_ref.at[ys(k), zs(dz), rq, cols[1]],
                      right_y, left_y, head_ref.at[rq, cols[1]] if dz == 0 else None,
                      arrival_keys(f"bz{q}", nz, dz))

    level = {}
    for key, _, _, _, needs in plan:
        level[key] = 1 + max([level[n] for n in needs], default=-1)
    order = sorted(range(len(plan)), key=lambda i: (level[plan[i][0]], i))
    index = {plan[i][0]: i for i in range(len(plan))}
    waited = set()
    copies = {}
    for i in order:
        key, src, dst, peer, needs = plan[i]
        for n in needs:
            if n not in waited:
                copies[n].wait_recv()
                waited.add(n)
        c = pltpu.make_async_remote_copy(
            src_ref=src,
            dst_ref=dst,
            send_sem=send_sem.at[index[key]],
            recv_sem=recv_sem.at[index[key]],
            device_id=peer,
            device_id_type=MESH,
        )
        c.start()
        copies[key] = c
    hidden_local.wait()
    for c in hidden_copies:
        c.wait_recv()
    tile = 256

    def norm_rows(i, carry):
        r = pl.ds(pl.multiple_of(i * tile, tile), tile)
        wide = feat_ref[r, :].astype(jnp.float32)
        scale = lax.rsqrt(jnp.mean(wide * wide, axis=1, keepdims=True) + EPS)
        normed_ref[r, :] = (wide * scale * gain_ref[...]).astype(normed_ref.dtype)
        return carry

    lax.fori_loop(0, feat_ref.shape[0] // tile, norm_rows, 0)
    for i in order:
        key = plan[i][0]
        if key not in waited:
            copies[key].wait_recv()
            waited.add(key)
    local.wait()
    for c in list(copies.values()) + hidden_copies:
        c.wait_send()


def gather_all(head, hidden, gain, ny, nz, nv):
    rows, width = head.shape
    slots, breadth = hidden.shape
    split = max(128, min(width - 128, int(round(width * 0.384 / 128)) * 128))
    streams = 4 * (ny // 2 + nz // 2 + ny * (nz // 2) + nz * (ny // 2))
    out, normed = pl.pallas_call(
        functools.partial(head_gather_kernel, ny, nz, nv, split),
        out_shape=(
            jax.ShapeDtypeStruct((ny, nz, rows, width), head.dtype),
            jax.ShapeDtypeStruct((slots, nv * breadth), hidden.dtype),
        ),
        in_specs=[pl.BlockSpec(memory_space=pl.ANY)] * 2 + [pl.BlockSpec(memory_space=pltpu.VMEM)],
        out_specs=(pl.BlockSpec(memory_space=pl.ANY), pl.BlockSpec(memory_space=pltpu.VMEM)),
        scratch_shapes=[
            pltpu.SemaphoreType.DMA((streams,)),
            pltpu.SemaphoreType.DMA((streams,)),
            pltpu.SemaphoreType.DMA(()),
            pltpu.SemaphoreType.DMA((nv - 1,)),
            pltpu.SemaphoreType.DMA((nv - 1,)),
            pltpu.SemaphoreType.DMA(()),
            pltpu.VMEM((slots, nv * breadth), hidden.dtype),
        ],
        compiler_params=pltpu.CompilerParams(collective_id=0, has_side_effects=True),
        cost_estimate=pl.CostEstimate(
            flops=0, transcendentals=0, bytes_accessed=2 * ny * nz * rows * width * 2
        ),
    )(head, hidden, gain.astype(jnp.float32).reshape(1, nv * breadth))
    return out.reshape(ny * nz * rows, width), normed


def stats_kernel(n, stats_ref, out_ref, send_sem, recv_sem):
    dp = lax.axis_index("dp")
    v = lax.axis_index("vocab")
    barrier = pltpu.get_barrier_semaphore()
    for k in range(1, n):
        pl.semaphore_signal(barrier, inc=1, device_id=(dp, (v + k) % n), device_id_type=MESH)
    pl.semaphore_wait(barrier, n - 1)
    copies = []
    for k in range(1, n):
        c = pltpu.make_async_remote_copy(
            src_ref=stats_ref,
            dst_ref=out_ref.at[v],
            send_sem=send_sem.at[k - 1],
            recv_sem=recv_sem.at[k - 1],
            device_id=(dp, (v + k) % n),
            device_id_type=MESH,
        )
        c.start()
        copies.append(c)
    out_ref[v] = stats_ref[...]
    for c in copies:
        c.wait_recv()
    for c in copies:
        c.wait_send()


def exchange_stats(stats, n):
    return pl.pallas_call(
        functools.partial(stats_kernel, n),
        out_shape=jax.ShapeDtypeStruct((n,) + stats.shape, stats.dtype),
        in_specs=[pl.BlockSpec(memory_space=pltpu.VMEM)],
        out_specs=pl.BlockSpec(memory_space=pltpu.VMEM),
        scratch_shapes=[
            pltpu.SemaphoreType.DMA((n - 1,)),
            pltpu.SemaphoreType.DMA((n - 1,)),
        ],
        compiler_params=pltpu.CompilerParams(collective_id=1, has_side_effects=True),
    )(stats)


def local(ny, nz, hidden, gain, head, target_ids, seq_lens, seq_owner):
    groups = lax.axis_size("dp")
    slices = lax.axis_size("vocab")
    position = lax.axis_index("dp")
    slice_index = lax.axis_index("vocab")
    slots = hidden.shape[0]
    breadth = head.shape[1]
    owners = jnp.arange(groups, dtype=jnp.int32)
    loads = jnp.sum(jnp.where(seq_owner[:, None] == owners[None, :], seq_lens[:, None], 0), axis=0)
    own_live = jnp.arange(slots, dtype=jnp.int32) < loads[position]
    columns, normed = gather_all(head, hidden, gain, ny, nz, slices)
    logits = jnp.dot(normed, columns, preferred_element_type=jnp.float32)
    top_local = jnp.max(logits, axis=1)
    expo = jnp.exp(logits - top_local[:, None])
    total_local = jnp.sum(expo, axis=1)
    weighted_local = jnp.sum(expo * logits, axis=1)
    local_id = target_ids - slice_index * breadth
    ids = lax.broadcasted_iota(jnp.int32, logits.shape, 1)
    picked_local = jnp.sum(jnp.where(ids == local_id[:, None], logits, 0.0), axis=1)
    stats = jnp.stack([top_local, total_local, weighted_local, picked_local])
    every = exchange_stats(stats, slices)
    tops = every[:, 0]
    top = jnp.max(tops, axis=0)
    factor = jnp.exp(tops - top[None, :])
    total = jnp.sum(every[:, 1] * factor, axis=0)
    weighted = jnp.sum(every[:, 2] * factor, axis=0)
    picked = jnp.sum(every[:, 3], axis=0)
    lse = top + jnp.log(total)
    logprob = picked - lse
    entropy = lse - weighted / total
    return (jnp.where(own_live, logprob, 0.0), jnp.where(own_live, entropy, 0.0))


def solution(mesh):
    ny, nz = dp_grid(mesh)
    return jax.shard_map(
        functools.partial(local, ny, nz),
        mesh=mesh,
        in_specs=(P("dp", "vocab"), P(), P("dp", "vocab"), P("dp"), P(), P()),
        out_specs=(P("dp"), P("dp")),
        check_vma=False,
    )
```
